32 devices in a mesh: section: 2 (over x), fsdp: 16 (over z, y, core).
Axes of the slice: x: 2, y: 2, z: 4, core: 2. Of those that a mesh axis runs over, the one named last changes fastest.
Arguments:
- hidden_in: bfloat16 [16, 128, 4096], P('fsdp', 'section'), may hold values from -40 to 40
- queries: bfloat16 [2, 16, 128, 4096], P('section', 'fsdp'), may hold values from -260 to 260
- key_weight: bfloat16 [2, 4096, 512], P('section', 'fsdp'), may hold values from -0.09375 to 0.09375
- value_weight: bfloat16 [2, 4096, 512], P('section', 'fsdp'), may hold values from -0.09375 to 0.09375
- norm_gain: float32 [2, 4096], P('section'), may hold values from 0.5 to 1.5
Outputs:
- section_outputs: bfloat16 [2, 16, 128, 4096], P('section', 'fsdp')
The draws below stay inside these ranges and needn't reach their ends.
All inputs are finite; a program needn't handle non-finite values.
Results may differ from the reference program's by a relative error of at most 0.013.
Values may be sent and summed in bfloat16 or wider, within the bound.
A program may use at most 64 MiB of HBM per device.

```python
import math
import jax
import jax.numpy as jnp
from jax import lax

D = 4096
QH = 32
KVH = 4
HD = 128
TOK_DEV = 128
SECTIONS = 2
SEQS = 16


def draw_hidden_in(key, part):
    keys = jax.random.split(jax.random.fold_in(key, 11), 3)
    row_scale = jnp.exp(jax.random.uniform(keys[1], (SEQS, TOK_DEV, 1), jnp.float32, -1.15, 1.15))
    col_scale = jnp.exp(jax.random.uniform(keys[2], (SEQS, 1, D), jnp.float32, -1.15, 1.15))
    base = jnp.clip(jax.random.normal(keys[0], (SEQS, TOK_DEV, D), jnp.float32), -4.0, 4.0)
    return (base * row_scale * col_scale).astype(jnp.bfloat16)


def draw_queries(key, part):
    keys = jax.random.split(jax.random.fold_in(key, 23), 1)
    return jnp.clip(jax.random.normal(keys[0], (SECTIONS, SEQS, TOK_DEV, D), jnp.float32), -4.5, 4.5).astype(jnp.bfloat16)


def block_levels(rng, dims, cuts, low, largest):
    def one(axis_at, shards_of):
        heights = jax.random.uniform(jax.random.fold_in(jax.random.fold_in(rng, 6), axis_at), (shards_of,), jnp.float32, low / len(cuts), largest / len(cuts))
        return jnp.repeat(jnp.exp(heights), dims[axis_at] // shards_of).reshape((-1,) + (1,) * (len(dims) - axis_at - 1))

    factor_of = one(*cuts[0])
    for cut in cuts[1:]:
        factor_of = factor_of * one(*cut)
    return factor_of


def centred(rng, extent, scale, reach, cuts=(), kind=jnp.bfloat16):
    factor_of = block_levels(rng, extent, cuts, -0.22, 0.18) if cuts else 1.0
    values = jax.random.normal(rng, extent, jnp.float32) * scale * factor_of
    return jnp.minimum(jnp.maximum(values, -reach), reach).astype(kind)


def setup_inputs(seed: int = 0) -> dict:
    splits = jax.random.split(jax.random.key(seed), 6)
    hidden_in = draw_hidden_in(jax.random.fold_in(splits[5], 71), 0)
    queries = draw_queries(jax.random.fold_in(splits[5], 71), 0)
    key_weight = centred(splits[2], (SECTIONS, D, KVH * HD), D ** -0.5, 0.09375, ((0, 2), (1, 16)))
    value_weight = centred(splits[3], (SECTIONS, D, KVH * HD), D ** -0.5, 0.09375, ((0, 2), (1, 16)))
    norm_gain = jnp.clip(1.0 + 0.1 * jax.random.normal(splits[4], (SECTIONS, D), jnp.float32), 0.5, 1.5)
    return dict(hidden_in=hidden_in, queries=queries, key_weight=key_weight, value_weight=value_weight, norm_gain=norm_gain)


epsilon = 1e-05

def rms_norm(hidden, section_gain):
    hidden_f32 = hidden.astype(jnp.float32)
    mean_square = lax.optimization_barrier(jnp.mean(hidden_f32 * hidden_f32, axis=-1, keepdims=True))
    return (hidden_f32 * lax.rsqrt(mean_square + epsilon) * section_gain.astype(jnp.float32)).astype(jnp.bfloat16)

def rotate(heads, positions):
    half_width = heads.shape[-1] // 2
    frequency = jnp.exp(jnp.arange(half_width, dtype=jnp.float32) * (-2.0 * math.log(10000.0) / heads.shape[-1]))
    angles = positions[:, None] * frequency[None, :]
    cosine = jnp.cos(angles)[:, None, :]
    sine_table = jnp.sin(angles)[:, None, :]
    first_half = heads[..., :half_width]
    second_half = heads[..., half_width:]
    return jnp.concatenate([first_half * cosine - second_half * sine_table, second_half * cosine + first_half * sine_table], axis=-1)

def attend(query_heads, key_heads, value_heads, query_pos, key_pos):
    scores = jnp.einsum('lkgd,rkd->kglr', query_heads.astype(jnp.float32), key_heads.astype(jnp.float32))
    scores = scores * (1.0 / math.sqrt(HD))
    allowed = key_pos[None, :] <= query_pos[:, None]
    scores = jnp.where(allowed, scores, -1e+30)
    row_max = lax.optimization_barrier(jnp.max(scores, axis=-1, keepdims=True))
    weights = jnp.exp(scores - row_max)
    softmax_probs = (weights / lax.optimization_barrier(jnp.sum(weights, axis=-1, keepdims=True))).astype(jnp.bfloat16)
    attn_mixed = jnp.einsum('kglr,rkd->lkgd', softmax_probs.astype(jnp.float32), value_heads.astype(jnp.float32))
    return attn_mixed.reshape(query_heads.shape[0], -1)

def apply_layer(hidden, query_rows, key_proj, value_proj, section_gain):
    row_count = hidden.shape[0]
    positions = jnp.arange(row_count, dtype=jnp.float32)
    normed = rms_norm(hidden, section_gain)
    key_heads = jnp.dot(normed, key_proj, preferred_element_type=jnp.float32).reshape(row_count, KVH, HD)
    key_heads = rotate(key_heads, positions).astype(jnp.bfloat16)
    value_heads = jnp.dot(normed, value_proj, preferred_element_type=jnp.float32).astype(jnp.bfloat16).reshape(row_count, KVH, HD)
    query_heads = rotate(query_rows.astype(jnp.float32).reshape(row_count, QH, HD), positions).astype(jnp.bfloat16)
    query_heads = query_heads.reshape(row_count, KVH, QH // KVH, HD)
    attn_mixed = attend(query_heads, key_heads, value_heads, positions, positions)
    return (hidden.astype(jnp.float32) + attn_mixed).astype(jnp.bfloat16)

def reference(hidden_in, queries, key_weight, value_weight, norm_gain):

    def one_sequence(operands):
        hidden, query_seq = operands
        section_list = []
        for section_index in range(SECTIONS):
            hidden = apply_layer(hidden, query_seq[section_index], key_weight[section_index], value_weight[section_index], norm_gain[section_index])
            section_list.append(hidden)
        return jnp.stack(section_list)
    result = lax.map(one_sequence, (hidden_in, jnp.swapaxes(queries, 0, 1)))
    return jnp.swapaxes(result, 0, 1)
```

```python
import functools
import math

import jax
import jax.numpy as jnp
import numpy as np
from jax import lax
from jax.experimental import pallas as pl
from jax.experimental.pallas import tpu as pltpu
from jax.sharding import PartitionSpec as P

HD = 128
EPS = 1e-05
MESH = pl.DeviceIdType.MESH


def rope_tables(rows):
    half = HD // 2
    frequency = np.exp(np.arange(half, dtype=np.float32) * np.float32(-2.0 * math.log(10000.0) / HD))
    angles = np.arange(rows, dtype=np.float32)[:, None] * frequency[None, :].astype(np.float32)
    cosine, sine = np.cos(angles), np.sin(angles)
    return (
        np.concatenate([cosine, cosine], 1).astype(np.float32),
        np.concatenate([-sine, sine], 1).astype(np.float32),
    )


def rope(u, cosine, sine):
    return u * cosine + pltpu.roll(u, HD // 2, 1) * sine


def kernel(
    n, sections, outer, inner,
    hid, q_in, kw, vw, gain_in, cos_in, sin_in,
    out,
    w, stage, xs, x1, xg, q0, q1, acc, kv0, kv1, gains, ssq, cos_ref, sin_ref,
    w_recv, w_send, stage_send, own_sem, load_sem, gain_sem, hid_recv, hid_send, hid_own,
    q_sem, x1_sem, kv_sem, pass_sem,
):
    s = lax.axis_index("section")
    f = lax.axis_index("fsdp")
    side = lax.rem(s, 2)
    pair = s // 2
    mate = {"section": s + 1 - 2 * side}
    core = lax.rem(f, 2)
    chip = f // 2
    i = lax.rem(chip, inner)
    o = chip // inner
    rows, width = xs.shape
    part = hid.shape[1]
    kvw = kw.shape[2]
    kv_heads = kvw // HD
    mine_heads = kv_heads // 2
    slots = 2 * mine_heads
    group = width // kvw
    gw = group * HD
    depth = kw.shape[1]
    chips = n // 2
    blk = width // chips
    half = width // 2
    pieces = half // blk

    def index(oo, ii, cc):
        return (oo * inner + ii) * 2 + cc

    local = []
    for hh in range(mine_heads):
        for to_mate in (False, True):
            head = (1 - side if to_mate else side) * mine_heads + hh
            cols = pl.ds(pl.multiple_of(head * HD, HD), HD)
            for kind, src in enumerate((kw, vw)):
                lanes = pl.ds(kind * HD, HD)
                dst = stage.at[hh, :, lanes] if to_mate else w.at[side * mine_heads + hh, f, :, lanes]
                local.append(pltpu.make_async_copy(src.at[0, :, cols], dst, own_sem.at[len(local)]))
    for copy in local:
        copy.start()
    loads = [
        pltpu.make_async_copy(src, dst, load_sem.at[at])
        for at, (src, dst) in enumerate(
            ((gain_in, gains.at[side]), (cos_in, cos_ref), (sin_in, sin_ref)))
    ]
    for load in loads:
        load.start()

    my_q = pl.ds(pl.multiple_of(side * half, half), half)

    def q_local(which):
        if which == 0:
            return pltpu.make_async_copy(q_in.at[0, 0, :, pl.ds(0, half)], q0, load_sem.at[3])
        return pltpu.make_async_copy(q_in.at[0, 0], q1, load_sem.at[3])

    pl.when(side == 0)(lambda: q_local(0).start())
    pl.when(side == 1)(lambda: q_local(1).start())

    targets = (
        (o > 0, index(o - 1, i, core)),
        (o < outer - 1, index(o + 1, i, core)),
        (i > 0, index(o, i - 1, core)),
        (i < inner - 1, index(o, i + 1, core)),
        (None, index(o, i, 1 - core)),
    )

    barrier = pltpu.get_barrier_semaphore()
    for cond, target in targets:
        def greet(target=target):
            pl.semaphore_signal(barrier, inc=1, device_id={"fsdp": target}, device_id_type=MESH)
        if cond is None:
            greet()
        else:
            pl.when(cond)(greet)
    for step in range(1, sections):
        pl.semaphore_signal(
            barrier, inc=1, device_id={"section": lax.rem(s + step, sections)}, device_id_type=MESH
        )
    expected = (
        jnp.where(o > 0, 1, 0) + jnp.where(o < outer - 1, 1, 0)
        + jnp.where(i > 0, 1, 0) + jnp.where(i < inner - 1, 1, 0) + sections
    )
    pl.semaphore_wait(barrier, expected)

    few = max(16, (depth * 3 // 16 + 8) // 16 * 16)
    cuts = (pl.ds(0, depth - few), pl.ds(depth - few, few))
    main, tail = 0, 1

    def w_copy(k, which, way, origin):
        piece = w.at[k, origin, cuts[which]]
        return pltpu.make_async_remote_copy(
            src_ref=piece, dst_ref=piece,
            send_sem=w_send.at[k, which, way, origin // 2], recv_sem=w_recv.at[k, which, origin],
            device_id={"fsdp": targets[way][1]}, device_id_type=MESH,
        )

    def on_way(way, act):
        cond = targets[way][0]
        if cond is None:
            act()
        else:
            pl.when(cond)(act)

    def w_start(k, which, way, origin):
        on_way(way, lambda: w_copy(k, which, way, origin).start())

    def stage_copy(layer, hh, which):
        k = layer * mine_heads + hh
        return pltpu.make_async_remote_copy(
            src_ref=stage.at[hh, cuts[which]], dst_ref=w.at[k, f, cuts[which]],
            send_sem=stage_send.at[hh, which], recv_sem=w_recv.at[k, which, f],
            device_id=mate, device_id_type=MESH,
        )

    def send_stage(hh):
        for which in (tail, main):
            stage_copy(side, hh, which).start()

    gain_copy = pltpu.make_async_remote_copy(
        src_ref=gain_in, dst_ref=gains.at[side], send_sem=gain_sem.at[0], recv_sem=gain_sem.at[1],
        device_id=mate, device_id_type=MESH,
    )
    gain_back = pltpu.make_async_remote_copy(
        src_ref=gain_in, dst_ref=gains.at[1 - side], send_sem=gain_sem.at[0], recv_sem=gain_sem.at[1],
        device_id=mate, device_id_type=MESH,
    )

    tokens = pl.ds(pl.multiple_of(s * part, part), part)

    def hid_copy(to):
        return pltpu.make_async_remote_copy(
            src_ref=hid.at[0], dst_ref=xs.at[tokens], send_sem=hid_send.at[to],
            recv_sem=hid_recv.at[s], device_id={"section": to}, device_id_type=MESH,
        )

    hid_local = pltpu.make_async_copy(hid.at[0], xs.at[tokens], hid_own)

    def send_hidden():
        for to in range(2):
            pl.when(s != to)(lambda to=to: hid_copy(to).start())
        pl.when(s < 2)(lambda: hid_local.start())

    def q_copy(g):
        return pltpu.make_async_remote_copy(
            src_ref=q_in.at[0, 0, :, pl.ds(half + g * gw, gw)], dst_ref=q0.at[:, pl.ds(g * gw, gw)],
            send_sem=q_sem.at[0, g], recv_sem=q_sem.at[1, g], device_id=mate, device_id_type=MESH,
        )

    def x1_cols(of, b):
        return pl.ds(pl.multiple_of(of * half + b * blk, blk), blk)

    def x1_copy(of, b):
        return pltpu.make_async_remote_copy(
            src_ref=x1.at[:, x1_cols(of, b)], dst_ref=x1.at[:, x1_cols(of, b)],
            send_sem=x1_sem.at[0, b], recv_sem=x1_sem.at[1, b], device_id=mate, device_id_type=MESH,
        )

    def kv_copy(hh):
        return pltpu.make_async_remote_copy(
            src_ref=kv1.at[hh], dst_ref=kv1.at[hh],
            send_sem=kv_sem.at[0, hh], recv_sem=kv_sem.at[1, hh], device_id=mate, device_id_type=MESH,
        )

    def pass_copy(to):
        return pltpu.make_async_remote_copy(
            src_ref=out.at[0, 0], dst_ref=xs, send_sem=pass_sem.at[to], recv_sem=pass_sem.at[2],
            device_id={"section": jnp.minimum(s + 1 + to, sections - 1)}, device_id_type=MESH,
        )

    for copy in local:
        copy.wait()

    send_stage(0)
    gain_copy.start()

    @pl.when(side == 0)
    def _():
        for hh in range(1, mine_heads):
            send_stage(hh)
    send_hidden()

    @pl.when(side == 1)
    def _():
        for hh in range(1, mine_heads):
            send_stage(hh)

    @pl.when(side == 0)
    def _():
        for g in range(mine_heads):
            q_copy(g).start()

    def own(k):
        away = k // mine_heads != side

        def got(which):
            pl.when(away)(lambda: w_copy(k, which, 4, f).wait_recv())

        got(tail)
        for way in (2, 3):
            w_start(k, tail, way, f)
        got(main)
        for way in range(5):
            w_start(k, main, way, f)
        for way in (0, 1, 4):
            w_start(k, tail, way, f)

    def rope_queries(ref, first, count):
        def one(h, _):
            cols = pl.ds(pl.multiple_of((first + h) * HD, HD), HD)
            u = ref[:, cols].astype(jnp.float32)
            ref[:, cols] = rope(u, cos_ref[...], sin_ref[...]).astype(jnp.bfloat16)
            return 0
        lax.fori_loop(0, count, one, 0)

    pl.when(side == 1)(lambda: own(mine_heads))
    pl.when(side == 0)(lambda: own(0))

    for load in loads:
        load.wait()

    @pl.when(side == 1)
    def _():
        q_local(1).wait()
        rope_queries(q1, 0, width // HD)

    @pl.when(side == 0)
    def _():
        q_local(0).wait()
        rope_queries(q0, 0, half // HD)

    pl.when(side == 1)(lambda: own(0))

    def relay(k, which, origin, ways):
        w_copy(k, which, 4, origin).wait_recv()
        for way in ways:
            w_start(k, which, way, origin)

    def drain(k, which, origin, ways):
        for way in ways:
            on_way(way, lambda way=way: w_copy(k, which, way, origin).wait_send())

    def sides(t, act):
        for sign, way in ((-1, 1), (1, 0)):
            far = o - t if sign < 0 else o + t
            there = (far >= 0) if sign < 0 else ((far < outer) & (t > 0))
            act(far, there, way)

    def around(there, act):
        for d in range(1, inner):
            pl.when(there & (i - d >= 0))(lambda d=d: act(i - d, 3))
            pl.when(there & (i + d < inner))(lambda d=d: act(i + d, 2))

    def along_outer(k, t, receive):
        def act(far, there, way):
            pl.when(there)(lambda: receive(k, main, index(far, i, core), (way, 2, 3, 4)))
        sides(t, act)

        def act_tail(far, there, way):
            pl.when(there)(lambda: receive(k, tail, index(far, i, core), (way, 4)))
            around(there, lambda ii, _: receive(k, tail, index(far, ii, core), (way, 4)))
        sides(t, act_tail)

    def along_inner(k, t, receive):
        def act(far, there, _):
            around(there, lambda ii, way: receive(k, main, index(far, ii, core), (way, 4)))
        sides(t, act)

    def first_inner(k, receive):
        around(o >= 0, lambda ii, way: receive(k, tail, index(o, ii, core), (way, 0, 1, 4)))

    def other_core(k):
        def one(c, _):
            for which in (main, tail):
                w_copy(k, which, 4, 2 * c + 1 - core).wait_recv()
            return 0
        lax.fori_loop(0, chips, one, 0)

    row = lax.broadcasted_iota(jnp.int32, (rows, rows), 0)
    col = lax.broadcasted_iota(jnp.int32, (rows, rows), 1)
    scale = math.log2(math.e) / math.sqrt(HD)

    def scaled(src, cols, layer):
        x = src[:, cols].astype(jnp.float32)
        xg[:, cols] = (x * gains[layer, :, cols]).astype(jnp.bfloat16)
        square = x * x
        total = square[:, :HD]
        for at in range(1, square.shape[1] // HD):
            total += square[:, at * HD:(at + 1) * HD]
        ssq[layer] += total

    def project(k, first, count, fresh):
        cols = pl.ds(pl.multiple_of(first * blk, blk), count * blk)
        b = w[k, pl.ds(first * 2, count * 2)].reshape(count * blk, 2 * HD)
        y = jnp.dot(xg[:, cols], b, preferred_element_type=jnp.float32)
        acc[k] = y if fresh else acc[k] + y

    def row_scale(layer):
        return lax.rsqrt(jnp.sum(ssq[layer], axis=-1, keepdims=True) / width + EPS)

    def finish(k, r, ref, at):
        y = acc[k] * r
        ref[at, 0] = rope(y[:, :HD], cos_ref[...], sin_ref[...]).astype(jnp.bfloat16)
        ref[at, 1] = y[:, HD:].astype(jnp.bfloat16)

    def attend(q_ref, q_first, k, v, x_ref, x_first, write):
        v = jnp.concatenate([v, jnp.ones((rows, HD), jnp.bfloat16)], axis=1)
        allowed = (col <= row)[None]
        q = jnp.concatenate(
            [q_ref[:, pl.ds(pl.multiple_of(q_first + h * HD, HD), HD)] for h in range(group)], axis=0)
        scores = lax.dot_general(q, k, (((1,), (1,)), ((), ())), preferred_element_type=jnp.float32)
        scores = jnp.where(allowed, scores.reshape(group, rows, rows), -1e30)
        top = jnp.max(scores, axis=-1, keepdims=True)
        p = jnp.exp2((scores - top) * scale).astype(jnp.bfloat16).reshape(group * rows, rows)
        mixed = jnp.dot(p, v, preferred_element_type=jnp.float32)
        mixed = mixed[:, :HD] / mixed[:, HD:]
        for h in range(group):
            cols = pl.ds(pl.multiple_of(x_first + h * HD, HD), HD)
            write(cols, (
                x_ref[:, cols].astype(jnp.float32) + mixed[h * rows:(h + 1) * rows]
            ).astype(jnp.bfloat16))

    def write_x1(cols, value):
        x1[:, cols] = value

    def write_out(cols, value):
        out[0, 0, :, cols] = value

    ssq[...] = jnp.zeros_like(ssq)

    def first_inputs():
        @pl.when(pair == 0)
        def _():
            hid_local.wait()
            for j in range(sections):
                @pl.when(s != j)
                def _(j=j):
                    pltpu.make_async_remote_copy(
                        src_ref=hid.at[0], dst_ref=xs.at[pl.ds(j * part, part)],
                        send_sem=hid_send.at[0], recv_sem=hid_recv.at[j],
                        device_id={"section": 0}, device_id_type=MESH,
                    ).wait_recv()
        if sections > 2:
            pl.when(pair > 0)(lambda: pass_copy(0).wait_recv())
        gain_back.wait_recv()

        def one(b, _):
            scaled(xs, pl.ds(pl.multiple_of(b * blk, blk), blk), 0)
            return 0
        lax.fori_loop(0, chips, one, 0)

    def first_layer(hh):
        other_core(hh)
        project(hh, 0, chips, True)
        finish(hh, row_scale(0), kv0, hh)

    def first_attention(g):
        @pl.when(side == 1)
        def _():
            pltpu.make_async_remote_copy(
                src_ref=q_in.at[0, 0, :, pl.ds(half, gw)], dst_ref=q0.at[:, pl.ds(pl.multiple_of(g * gw, gw), gw)],
                send_sem=q_sem.at[0, g], recv_sem=q_sem.at[1, g], device_id=mate, device_id_type=MESH,
            ).wait_recv()
            rope_queries(q0, g * group, group)
        attend(q0, g * gw, kv0[g, 0], kv0[g, 1], xs, side * half + g * gw, write_x1)
        for b in range(gw // blk):
            x1_copy(side, g * (gw // blk) + b).start()
        def one(b, _):
            scaled(x1, x1_cols(side, g * (gw // blk) + b), 1)
            return 0
        lax.fori_loop(0, gw // blk, one, 0)

    def at(k, t):
        return k * outer + min(t, outer - 1)

    steps = slots * outer
    later = jnp.where(pair > 0, steps, 0) if sections > 2 else 0

    def step(u, _):
        k = u // outer
        t = lax.rem(u, outer)

        @pl.when(u < steps)
        def _():
            @pl.when(t == 0)
            def _():
                pl.when((k + 1 < slots) & ((side == 0) | (k + 1 != mine_heads)))(lambda: own(k + 1))
                first_inner(k, relay)
            along_outer(k, t + 1, relay)
            along_inner(k, t, relay)

        v = u - later

        @pl.when(v == at(mine_heads - 1, 2))
        def _():
            first_inputs()

        for hh in range(mine_heads):
            pl.when(v == at(mine_heads - 1, 2 if hh < mine_heads - 1 else 3))(lambda hh=hh: first_layer(hh))

        spots = [at(mine_heads, 0), at(mine_heads, 2)] + [at(mine_heads, 3)] * (mine_heads - 2)
        for g, spot in enumerate(spots):
            pl.when(v == spot)(lambda g=g: first_attention(g))

        @pl.when(v == at(slots - 1, 2))
        def _():
            for k1 in range(mine_heads, slots - 1):
                other_core(k1)
                project(k1, side * pieces, pieces, True)
        return 0

    lax.fori_loop(0, steps + later, step, 0)

    other_core(slots - 1)
    project(slots - 1, side * pieces, pieces, True)

    def arrive(b, _):
        x1_copy(1 - side, b).wait_recv()
        cols = x1_cols(1 - side, b)
        scaled(x1, cols, 1)
        return 0
    lax.fori_loop(0, pieces, arrive, 0)

    r1 = row_scale(1)
    for hh in range(mine_heads):
        k1 = mine_heads + hh
        project(k1, (1 - side) * pieces, pieces, False)
        finish(k1, r1, kv1, side * mine_heads + hh)
        pl.when(side == 0)(lambda hh=hh: kv_copy(hh).start())

    @pl.when(side == 0)
    def _():
        out[0, 0] = x1[...]

    @pl.when(side == 1)
    def _():
        def one(g, _):
            head = jnp.where(g < mine_heads, mine_heads + g, g - mine_heads)
            pl.when(g >= mine_heads)(lambda: kv_copy(g - mine_heads).wait_recv())
            attend(q1, head * gw, kv1[head, 0], kv1[head, 1], x1, head * gw, write_out)
            return 0
        lax.fori_loop(0, kv_heads, one, 0)
        if sections > 2:
            @pl.when(s < sections - 1)
            def _():
                for to in range(2):
                    pass_copy(to).start()

    for hh in range(mine_heads):
        for which in (tail, main):
            stage_copy(side, hh, which).wait_send()
    gain_copy.wait_send()
    for to in range(2):
        pl.when(s != to)(lambda to=to: hid_copy(to).wait_send())
    if sections > 2:
        @pl.when(pair > 0)
        def _():
            pass
    for b in range(pieces):
        x1_copy(side, b).wait_send()

    @pl.when(side == 0)
    def _():
        for g in range(mine_heads):
            q_copy(g).wait_send()
        for hh in range(mine_heads):
            kv_copy(hh).wait_send()

    if sections > 2:
        @pl.when((side == 1) & (s < sections - 1))
        def _():
            for to in range(2):
                pass_copy(to).wait_send()

    def drain_step(u, _):
        k = u // outer
        t = lax.rem(u, outer)

        @pl.when(t == 0)
        def _():
            for which in (main, tail):
                drain(k, which, f, range(5))
            first_inner(k, drain)
        along_outer(k, t + 1, drain)
        along_inner(k, t, drain)
        return 0

    lax.fori_loop(0, steps, drain_step, 0)


def solution(mesh):
    sections, n = mesh.shape["section"], mesh.shape["fsdp"]
    chips = n // 2
    outer = 4 if chips % 4 == 0 else 1
    inner = chips // outer

    def body(hidden_in, queries, key_weight, value_weight, norm_gain):
        rows, width = queries.shape[2:]
        depth, kvw = key_weight.shape[1:]
        cosine, sine = rope_tables(rows)
        hbm = pl.BlockSpec(memory_space=pltpu.HBM)
        vmem = pl.BlockSpec(memory_space=pltpu.VMEM)
        dma = pltpu.SemaphoreType.DMA
        bf16, f32 = jnp.bfloat16, jnp.float32
        heads = kvw // HD // 2
        return pl.pallas_call(
            functools.partial(kernel, n, sections, outer, inner),
            out_shape=jax.ShapeDtypeStruct(queries.shape, bf16),
            in_specs=[hbm] * 7,
            out_specs=vmem,
            scratch_shapes=[
                pltpu.VMEM((2 * heads, n, depth, 2 * HD), bf16),
                pltpu.VMEM((heads, depth, 2 * HD), bf16),
                pltpu.VMEM((rows, width), bf16),
                pltpu.VMEM((rows, width), bf16),
                pltpu.VMEM((rows, width), bf16),
                pltpu.VMEM((rows, width // 2), bf16),
                pltpu.VMEM((rows, width), bf16),
                pltpu.VMEM((2 * heads, rows, 2 * HD), f32),
                pltpu.VMEM((heads, 2, rows, HD), bf16),
                pltpu.VMEM((2 * heads, 2, rows, HD), bf16),
                pltpu.VMEM((2, 1, width), f32),
                pltpu.VMEM((2, rows, HD), f32),
                pltpu.VMEM((rows, HD), f32),
                pltpu.VMEM((rows, HD), f32),
                dma((2 * heads, 2, n)), dma((2 * heads, 2, 5, chips)), dma((heads, 2)), dma((4 * heads,)),
                dma((4,)), dma((2,)), dma((sections,)), dma((2,)), dma,
                dma((2, heads)), dma((2, chips // 2)), dma((2, heads)), dma((3,)),
            ],
            compiler_params=pltpu.CompilerParams(
                collective_id=0, has_side_effects=True, vmem_limit_bytes=28 * 2**20
            ),
        )(*(
            pltpu.with_memory_space_constraint(x, pltpu.HBM)
            for x in (hidden_in, queries, key_weight, value_weight, norm_gain, jnp.asarray(cosine), jnp.asarray(sine))
        ))

    placed = (
        P("fsdp", "section", None),
        P("section", "fsdp", None, None),
        P("section", "fsdp", None),
        P("section", "fsdp", None),
        P("section", None),
    )
    return jax.shard_map(
        body, mesh=mesh, in_specs=placed, out_specs=P("section", "fsdp", None, None), check_vma=False
    )
```

```python
import functools
import math

import jax
import jax.numpy as jnp
import numpy as np
from jax import lax
from jax.experimental import pallas as pl
from jax.experimental.pallas import tpu as pltpu
from jax.sharding import PartitionSpec as P

HD = 128
EPS = 1e-05
MESH = pl.DeviceIdType.MESH


def rope_tables(rows):
    half = HD // 2
    frequency = np.exp(np.arange(half, dtype=np.float32) * np.float32(-2.0 * math.log(10000.0) / HD))
    angles = np.arange(rows, dtype=np.float32)[:, None] * frequency[None, :].astype(np.float32)
    cosine, sine = np.cos(angles), np.sin(angles)
    return (
        np.concatenate([cosine, cosine], 1).astype(np.float32),
        np.concatenate([-sine, sine], 1).astype(np.float32),
    )


def rope(u, cosine, sine):
    return u * cosine + pltpu.roll(u, HD // 2, 1) * sine


def chain_kernel(
    n, sections, outer, inner,
    hid, q_in, kw, vw, gain_in, cos_in, sin_in,
    out,
    w, xin, xs, qs, qp, normed, acc, kv, kvp, gain, cos_ref, sin_ref,
    w_recv, w_send, own_sem, hid_recv, hid_send, hid_own, q_sem, kv_sem, x_sem, load_sem,
):
    s = lax.axis_index("section")
    f = lax.axis_index("fsdp")
    core = lax.rem(f, 2)
    chip = f // 2
    i = lax.rem(chip, inner)
    o = chip // inner
    rows, width = xs.shape
    part = hid.shape[1]
    kvw = kw.shape[2]
    kv_heads = kvw // HD
    group = width // kvw
    depth = kw.shape[1]

    def index(oo, ii, cc):
        return (oo * inner + ii) * 2 + cc

    own_k = pltpu.make_async_copy(kw.at[0], w.at[f, 0], own_sem.at[0])
    own_v = pltpu.make_async_copy(vw.at[0], w.at[f, 1], own_sem.at[1])
    own_k.start()
    own_v.start()
    loads = [
        pltpu.make_async_copy(src, dst, load_sem.at[at])
        for at, (src, dst) in enumerate(
            ((q_in.at[0, 0], qs), (gain_in, gain), (cos_in, cos_ref), (sin_in, sin_ref)))
    ]
    for load in loads:
        load.start()

    targets = (
        (o > 0, index(o - 1, i, core)),
        (o < outer - 1, index(o + 1, i, core)),
        (i > 0, index(o, i - 1, core)),
        (i < inner - 1, index(o, i + 1, core)),
        (None, index(o, i, 1 - core)),
    )

    barrier = pltpu.get_barrier_semaphore()
    for cond, target in targets:
        def greet(target=target):
            pl.semaphore_signal(barrier, inc=1, device_id={"fsdp": target}, device_id_type=MESH)
        if cond is None:
            greet()
        else:
            pl.when(cond)(greet)
    for step in range(1, sections):
        pl.semaphore_signal(
            barrier, inc=1, device_id={"section": lax.rem(s + step, sections)}, device_id_type=MESH
        )
    expected = (
        jnp.where(o > 0, 1, 0) + jnp.where(o < outer - 1, 1, 0)
        + jnp.where(i > 0, 1, 0) + jnp.where(i < inner - 1, 1, 0) + sections
    )
    pl.semaphore_wait(barrier, expected)

    few = max(16, depth // 8)
    first = (depth - few + 16) // 32 * 16
    cuts = (pl.ds(0, first), pl.ds(first, depth - few - first), pl.ds(depth - few, few))
    mains, tail = (0, 1), 2

    def w_copy(which, way, origin):
        piece = w.at[origin, :, cuts[which]]
        return pltpu.make_async_remote_copy(
            src_ref=piece, dst_ref=piece,
            send_sem=w_send.at[which, way, origin], recv_sem=w_recv.at[which, origin],
            device_id={"fsdp": targets[way][1]}, device_id_type=MESH,
        )

    def w_start(which, way, origin):
        cond = targets[way][0]
        if cond is None:
            w_copy(which, way, origin).start()
        else:
            pl.when(cond)(lambda: w_copy(which, way, origin).start())

    own_k.wait()
    own_v.wait()
    for way in (2, 3):
        w_start(tail, way, f)
    for which in mains:
        for way in range(5):
            w_start(which, way, f)
    for way in (0, 1, 4):
        w_start(tail, way, f)

    mine = pl.ds(pl.multiple_of(s * part, part), part)

    def hid_copy(to):
        dst = xs if to == 0 else xin
        return pltpu.make_async_remote_copy(
            src_ref=hid.at[0], dst_ref=dst.at[mine], send_sem=hid_send.at[to],
            recv_sem=hid_recv.at[s], device_id={"section": to}, device_id_type=MESH,
        )

    def hid_local(to):
        dst = xs if to == 0 else xin
        return pltpu.make_async_copy(hid.at[0], dst.at[mine], hid_own)

    for to in range(min(2, sections)):
        pl.when(s != to)(lambda to=to: hid_copy(to).start())
        pl.when(s == to)(lambda to=to: hid_local(to).start())

    q_copy = pltpu.make_async_remote_copy(
        src_ref=q_in.at[0, 0], dst_ref=qp, send_sem=q_sem.at[0], recv_sem=q_sem.at[1],
        device_id={"section": jnp.minimum(s + 1, sections - 1)}, device_id_type=MESH,
    )
    def kv_copy(g):
        return pltpu.make_async_remote_copy(
            src_ref=kv.at[g], dst_ref=kvp.at[g], send_sem=kv_sem.at[0, g], recv_sem=kv_sem.at[1, g],
            device_id={"section": jnp.minimum(s + 1, sections - 1)}, device_id_type=MESH,
        )

    x_copy = pltpu.make_async_remote_copy(
        src_ref=xs, dst_ref=xin, send_sem=x_sem.at[0], recv_sem=x_sem.at[1],
        device_id={"section": jnp.minimum(s + 1, sections - 1)}, device_id_type=MESH,
    )
    last = s == sections - 1
    pl.when(jnp.logical_not(last))(lambda: q_copy.start())

    for load in loads:
        load.wait()

    def rope_queries(ref):
        def one(h, _):
            cols = pl.ds(pl.multiple_of(h * HD, HD), HD)
            u = ref[:, cols].astype(jnp.float32)
            ref[:, cols] = rope(u, cos_ref[...], sin_ref[...]).astype(jnp.bfloat16)
            return 0
        lax.fori_loop(0, width // HD, one, 0)

    rope_queries(qs)

    def hid_arrive(to):
        hid_local(to).wait()
        dst = xs if to == 0 else xin
        for step in range(1, sections):
            j = lax.rem(to + step, sections)
            pltpu.make_async_remote_copy(
                src_ref=hid.at[0], dst_ref=dst.at[pl.ds(j * part, part)],
                send_sem=hid_send.at[to], recv_sem=hid_recv.at[j],
                device_id={"section": to}, device_id_type=MESH,
            ).wait_recv()

    block = 16

    def norm():
        def one(r, _):
            at = pl.ds(pl.multiple_of(r * block, block), block)
            x = xs[at, :].astype(jnp.float32)
            mean_square = jnp.mean(x * x, axis=-1, keepdims=True)
            y = (x * lax.rsqrt(mean_square + EPS) * gain[...]).astype(jnp.bfloat16)
            for pair in range(n // 2):
                normed[pair, at, :] = y[:, pair * 2 * depth:(pair + 1) * 2 * depth]
            return 0
        lax.fori_loop(0, rows // block, one, 0)

    def project(pair):
        a = normed[pair]
        for half in range(2):
            b = w[pl.ds(pair * 2, 2), half].reshape(2 * depth, kvw)
            acc[half] += jnp.dot(a, b, preferred_element_type=jnp.float32)

    acc[...] = jnp.zeros_like(acc)

    def arrive(which, origin, ways):
        w_copy(which, 4, origin).wait_recv()
        for way in ways:
            w_start(which, way, origin)

    def relay(which, origin, ways):
        arrive(which, origin, ways)

    def from_other(which, origin, ways):
        arrive(which, origin, ())

    def project_pair(which, origin, ways):
        if which == tail - 1:
            project(origin // 2)

    def sides(t, act):
        for sign, way in ((-1, 1), (1, 0)):
            far = o - t if sign < 0 else o + t
            there = (far >= 0) if sign < 0 else ((far < outer) & (t > 0))
            act(far, there, way)

    def around(there, act):
        for d in range(1, inner):
            pl.when(there & (i - d >= 0))(lambda d=d: act(i - d, 3))
            pl.when(there & (i + d < inner))(lambda d=d: act(i + d, 2))

    def along_outer(t, c, receive):
        for which in mains:
            def act(far, there, way, which=which):
                pl.when(there)(lambda: receive(which, index(far, i, c), (way, 2, 3, 4)))
            sides(t, act)

        def act_tail(far, there, way):
            pl.when(there)(lambda: receive(tail, index(far, i, c), (way, 4)))
            around(there, lambda ii, _: receive(tail, index(far, ii, c), (way, 4)))
        sides(t, act_tail)

    def along_inner(t, c, receive):
        for which in mains:
            def act(far, there, _, which=which):
                around(there, lambda ii, way: receive(which, index(far, ii, c), (way, 4)))
            sides(t, act)

    def first_inner(c, receive):
        around(o >= 0, lambda ii, way: receive(tail, index(o, ii, c), (way, 0, 1, 4)))

    first_inner(core, relay)

    def step(t, _):
        along_outer(t + 1, core, relay)

        @pl.when((t == 0) & (s == 0))
        def _():
            hid_arrive(0)
            norm()

        @pl.when(t == 0)
        def _():
            for which in (*mains, tail):
                arrive(which, index(o, i, 1 - core), ())
            first_inner(1 - core, from_other)

        along_inner(t, core, relay)
        along_outer(t + 1, 1 - core, from_other)
        along_inner(t, 1 - core, from_other)

        @pl.when(s == 0)
        def _():
            pl.when(t == 0)(lambda: project(chip))
            along_outer(t + 1, core, project_pair)
            along_inner(t, core, project_pair)

        return 0

    lax.fori_loop(0, outer, step, 0)

    row = lax.broadcasted_iota(jnp.int32, (rows, rows), 0)
    col = lax.broadcasted_iota(jnp.int32, (rows, rows), 1)
    scale = math.log2(math.e) / math.sqrt(HD)

    def attend(q_ref, kv_ref, x_ref, o_write, ready):
        ones = jnp.ones((rows, HD), jnp.bfloat16)
        allowed = (col <= row)[None]

        def one(g, _):
            ready(g)
            k = kv_ref[g, 0]
            v = jnp.concatenate([kv_ref[g, 1], ones], axis=1)
            base = g * group * HD
            cols = [pl.ds(pl.multiple_of(base + h * HD, HD), HD) for h in range(group)]
            q = jnp.concatenate([q_ref[:, c] for c in cols], axis=0)
            scores = lax.dot_general(q, k, (((1,), (1,)), ((), ())), preferred_element_type=jnp.float32)
            scores = jnp.where(allowed, scores.reshape(group, rows, rows), -1e30)
            top = jnp.max(scores, axis=-1, keepdims=True)
            p = jnp.exp2((scores - top) * scale).astype(jnp.bfloat16).reshape(group * rows, rows)
            mixed = jnp.dot(p, v, preferred_element_type=jnp.float32)
            mixed = mixed[:, :HD] / mixed[:, HD:]
            for h in range(group):
                o_write(cols[h], (
                    x_ref[:, cols[h]].astype(jnp.float32) + mixed[h * rows:(h + 1) * rows]
                ).astype(jnp.bfloat16))
            return 0

        lax.fori_loop(0, kv_heads, one, 0)

    def write_xs(c, value):
        xs[:, c] = value

    def write_out(c, value):
        out[0, 0, :, c] = value

    @pl.when(s > 0)
    def _():
        q_copy.wait_recv()
        rope_queries(qp)
        pl.when(s == 1)(lambda: hid_arrive(1))
        if sections > 2:
            pl.when(s > 1)(lambda: x_copy.wait_recv())
        attend(qp, kvp, xin, write_xs, lambda g: kv_copy(g).wait_recv())
        if sections > 2:
            pl.when(jnp.logical_not(last))(lambda: x_copy.start())
        norm()
        def one(j, _):
            project(j)
            return 0
        lax.fori_loop(0, n // 2, one, 0)

    for h in range(kv_heads):
        at = slice(h * HD, (h + 1) * HD)
        kv[h, 0] = rope(acc[0, :, at], cos_ref[...], sin_ref[...]).astype(jnp.bfloat16)
        kv[h, 1] = acc[1, :, at].astype(jnp.bfloat16)
        pl.when(jnp.logical_not(last))(lambda h=h: kv_copy(h).start())
    attend(qs, kv, xs, write_out, lambda g: None)

    def drain(which, origin, ways):
        for way in ways:
            cond = targets[way][0]
            if cond is None:
                w_copy(which, way, origin).wait_send()
            else:
                pl.when(cond)(lambda way=way: w_copy(which, way, origin).wait_send())

    for which in (*mains, tail):
        drain(which, f, range(5))
    first_inner(core, drain)

    def drain_step(t, _):
        along_outer(t + 1, core, drain)
        along_inner(t, core, drain)
        return 0

    lax.fori_loop(0, outer, drain_step, 0)
    for to in range(min(2, sections)):
        pl.when(s != to)(lambda to=to: hid_copy(to).wait_send())

    @pl.when(jnp.logical_not(last))
    def _():
        q_copy.wait_send()
        for h in range(kv_heads):
            kv_copy(h).wait_send()
        if sections > 2:
            pl.when(s > 0)(lambda: x_copy.wait_send())


ORDER = (
    "OU00", "OT00", "OM000", "OM110", "OM001", "*Q", "OM010", "OM011", "ZM000", "OT01", "ZM001", "OU01",
    "Y001", "F00", "ZM010", "Y000", "OT10", "ZM011", "ZM020", "Y010", "ZT00", "ZM021", "Y030", "ZT01", "Y011",
    "OT11", "OM100", "*X", "Y021", "Y020", "ZM100", "Y031", "ZT02", "*P", "OU10", "*A0", "ZM110", "OU11",
    "F10", "*A1", "ZM120", "ZT10", "Y110", "ZT11", "*D", "Y100", "*M", "Y120", "Y130", "ZT12", "*H",
)


def pair_kernel(
    n, outer, inner,
    hid, q_in, kw, vw, gain_in, cos_in, sin_in,
    out,
    w, stage, xs, x1, xb, xr, q0, q1, acc, give, take, kv0, kv1, gains, ssq, cos_ref, sin_ref,
    w_recv, w_send, stage_send, own_sem, load_sem, gain_sem, hid_sem, hid_own,
    q_sem, x1_sem, kv_sem, swap0_sem, swap_sem, part_sem,
):
    side = lax.axis_index("section")
    f = lax.axis_index("fsdp")
    mate = {"section": 1 - side}
    core = lax.rem(f, 2)
    chip = f // 2
    i = lax.rem(chip, inner)
    o = chip // inner
    twin = {"fsdp": 2 * chip + 1 - core}
    rows, width = xs.shape
    part = hid.shape[1]
    kvw = kw.shape[2]
    kv_heads = kvw // HD
    heads = kv_heads // 2
    group = width // kvw
    gw = group * HD
    depth = kw.shape[1]
    chips = n // 2
    blk = width // chips
    half = width // 2
    pieces = half // blk
    per_group = gw // blk

    local = []
    for hh in range(heads):
        for to_mate in (False, True):
            head = (1 - side if to_mate else side) * heads + hh
            cols = pl.ds(pl.multiple_of(head * HD, HD), HD)
            at = pl.ds(hh * depth, depth)
            for kind, src in enumerate((kw, vw)):
                lanes = pl.ds(kind * HD, HD)
                dst = stage.at[at, lanes] if to_mate else w.at[side, chip, at, lanes]
                local.append(pltpu.make_async_copy(src.at[0, :, cols], dst, own_sem.at[len(local)]))
    for copy in local:
        copy.start()
    loads = [
        pltpu.make_async_copy(src, dst, load_sem.at[at])
        for at, (src, dst) in enumerate(
            ((gain_in, gains.at[side]), (cos_in, cos_ref), (sin_in, sin_ref)))
    ]
    for load in loads:
        load.start()

    def q_local(which):
        if which == 0:
            return pltpu.make_async_copy(q_in.at[0, 0, :, pl.ds(0, half)], q0, load_sem.at[3])
        return pltpu.make_async_copy(q_in.at[0, 0], q1, load_sem.at[3])

    for which in range(2):
        pl.when(side == which)(lambda which=which: q_local(which).start())

    def index(oo, ii):
        return (oo * inner + ii) * 2 + core

    targets = (
        (o > 0, index(o - 1, i)),
        (o < outer - 1, index(o + 1, i)),
        (i > 0, index(o, i - 1)),
        (i < inner - 1, index(o, i + 1)),
    )

    barrier = pltpu.get_barrier_semaphore()
    for cond, target in targets:
        pl.when(cond)(lambda target=target: pl.semaphore_signal(
            barrier, inc=1, device_id={"fsdp": target}, device_id_type=MESH))
    for device in (twin, mate):
        pl.semaphore_signal(barrier, inc=1, device_id=device, device_id_type=MESH)
    expected = (
        jnp.where(o > 0, 1, 0) + jnp.where(o < outer - 1, 1, 0)
        + jnp.where(i > 0, 1, 0) + jnp.where(i < inner - 1, 1, 0) + 2
    )
    pl.semaphore_wait(barrier, expected)

    deep = heads * depth
    few = max(16, (deep * 96 // 512 + 8) // 16 * 16)
    splits = (2, 1)
    cuts = []
    for layer in range(2):
        edges = [(deep - few) * at // splits[layer] // 16 * 16 for at in range(splits[layer])] + [deep - few, deep]
        cuts.append([pl.ds(a, b - a) for a, b in zip(edges, edges[1:])])

    def w_copy(layer, which, way, origin):
        piece = w.at[layer, origin, cuts[layer][which]]
        return pltpu.make_async_remote_copy(
            src_ref=piece, dst_ref=piece,
            send_sem=w_send.at[layer, which, way, origin], recv_sem=w_recv.at[layer, which, origin],
            device_id={"fsdp": targets[way][1]}, device_id_type=MESH,
        )

    def w_start(layer, which, way, origin):
        pl.when(targets[way][0])(lambda: w_copy(layer, which, way, origin).start())

    def stage_copy(layer, which):
        return pltpu.make_async_remote_copy(
            src_ref=stage.at[cuts[layer][which]], dst_ref=w.at[layer, chip, cuts[layer][which]],
            send_sem=stage_send.at[which], recv_sem=w_recv.at[layer, which, chip],
            device_id=mate, device_id_type=MESH,
        )

    def gain_copy(layer):
        return pltpu.make_async_remote_copy(
            src_ref=gain_in, dst_ref=gains.at[layer], send_sem=gain_sem.at[0], recv_sem=gain_sem.at[1],
            device_id=mate, device_id_type=MESH,
        )

    def hid_copy(of):
        return pltpu.make_async_remote_copy(
            src_ref=hid.at[0], dst_ref=xs.at[pl.ds(pl.multiple_of(of * part, part), part)],
            send_sem=hid_sem.at[0], recv_sem=hid_sem.at[1], device_id=mate, device_id_type=MESH,
        )

    hid_local = pltpu.make_async_copy(
        hid.at[0], xs.at[pl.ds(pl.multiple_of(side * part, part), part)], hid_own)

    def q_copy(g):
        return pltpu.make_async_remote_copy(
            src_ref=q_in.at[0, 0, :, pl.ds(half + g * gw, gw)], dst_ref=q0.at[:, pl.ds(g * gw, gw)],
            send_sem=q_sem.at[0, g], recv_sem=q_sem.at[1, g], device_id=mate, device_id_type=MESH,
        )

    def x1_copy(of, b):
        cols = pl.ds(pl.multiple_of(of * half + b * blk, blk), blk)
        return pltpu.make_async_remote_copy(
            src_ref=x1.at[:, cols], dst_ref=x1.at[:, cols],
            send_sem=x1_sem.at[0, b], recv_sem=x1_sem.at[1, b], device_id=mate, device_id_type=MESH,
        )

    def kv_copy(hh):
        return pltpu.make_async_remote_copy(
            src_ref=kv1.at[hh], dst_ref=kv1.at[hh],
            send_sem=kv_sem.at[0, hh], recv_sem=kv_sem.at[1, hh], device_id=mate, device_id_type=MESH,
        )

    swap0 = pltpu.make_async_remote_copy(
        src_ref=xb.at[0, 1 - core], dst_ref=xr.at[0], send_sem=swap0_sem.at[0], recv_sem=swap0_sem.at[1],
        device_id=twin, device_id_type=MESH,
    )

    def swap_copy(c):
        cols = pl.ds(pl.multiple_of(c * depth, depth), depth)
        return pltpu.make_async_remote_copy(
            src_ref=xb.at[1, 1 - core, :, cols], dst_ref=xr.at[1, :, cols],
            send_sem=swap_sem.at[0, c], recv_sem=swap_sem.at[1, c], device_id=twin, device_id_type=MESH,
        )

    def part_copy(layer, hh):
        return pltpu.make_async_remote_copy(
            src_ref=give.at[layer, hh], dst_ref=take.at[layer, hh],
            send_sem=part_sem.at[0, layer, hh], recv_sem=part_sem.at[1, layer, hh],
            device_id=twin, device_id_type=MESH,
        )

    for copy in local:
        copy.wait()

    for layer in range(2):
        @pl.when(side == layer)
        def _(layer=layer):
            for which in range(splits[layer] + 1):
                stage_copy(layer, which).start()
    gain_copy(side).start()
    hid_copy(side).start()
    hid_local.start()

    @pl.when(side == 0)
    def _():
        for g in range(heads):
            q_copy(g).start()

    def rope_queries(ref, first, count):
        def one(h, _):
            cols = pl.ds(pl.multiple_of((first + h) * HD, HD), HD)
            u = ref[:, cols].astype(jnp.float32)
            ref[:, cols] = rope(u, cos_ref[...], sin_ref[...]).astype(jnp.bfloat16)
            return 0
        lax.fori_loop(0, count, one, 0)

    def relay(layer, which, origin, ways):
        w_copy(layer, which, 0, origin).wait_recv()
        for way in ways:
            w_start(layer, which, way, origin)

    def drain(layer, which, origin, ways):
        for way in ways:
            pl.when(targets[way][0])(lambda way=way: w_copy(layer, which, way, origin).wait_send())

    def sides(t, act):
        if t == 0:
            act(o, None, 0)
        else:
            act(o - t, o - t >= 0, 1)
            act(o + t, o + t < outer, 0)

    def around(there, act):
        for d in range(1, inner):
            for cond, ii, way in ((i - d >= 0, i - d, 3), (i + d < inner, i + d, 2)):
                pl.when(cond if there is None else there & cond)(lambda ii=ii, way=way: act(ii, way))

    def own(kind, layer, on, which, receive):
        ways = {"OM": (0, 1, 2, 3), "OT": (2, 3), "OU": (0, 1)}[kind]

        @pl.when(side == on)
        def _():
            if receive is relay:
                if on != layer and kind != "OU":
                    w_copy(layer, which, 0, chip).wait_recv()
                for way in ways:
                    w_start(layer, which, way, chip)
            else:
                drain(layer, which, chip, ways)

    def far(t, act):
        sides(t, lambda oo, there, way: pl.when(there)(lambda: act(oo, way)))

    def move(kind, layer, t, which, receive):
        tail = splits[layer]
        if kind[0] == "O":
            own(kind, layer, t, tail if which is None else which, receive)
        elif kind == "F":
            around(None, lambda ii, way: receive(layer, tail, o * inner + ii, (way, 0, 1)))
        elif kind == "ZM":
            far(t + 1, lambda oo, way: receive(layer, which, oo * inner + i, (way, 2, 3)))
        elif kind == "ZT":
            def both(oo, there, way):
                pl.when(there)(lambda: receive(layer, tail, oo * inner + i, (way,)))
                around(there, lambda ii, _: receive(layer, tail, oo * inner + ii, (way,)))
            sides(t + 1, both)
        elif kind == "Y":
            sides(t, lambda oo, there, _: around(
                there, lambda ii, way: receive(layer, which, oo * inner + ii, (way,))))

    row = lax.broadcasted_iota(jnp.int32, (rows, rows), 0)
    col = lax.broadcasted_iota(jnp.int32, (rows, rows), 1)
    scale = math.log2(math.e) / math.sqrt(HD)

    def scaled(src, c, layer):
        cols = pl.ds(pl.multiple_of(c * blk, blk), blk)
        x = src[:, cols].astype(jnp.float32)
        y = (x * gains[layer, :, cols]).astype(jnp.bfloat16)
        for kind in range(2):
            xb[layer, kind, :, pl.ds(pl.multiple_of(c * depth, depth), depth)] = y[:, kind * depth:(kind + 1) * depth]
        square = x * x
        total = square[:, :HD]
        for at in range(1, blk // HD):
            total += square[:, at * HD:(at + 1) * HD]
        ssq[layer] += total

    def project(layer, hh, first, count, fresh):
        cols = pl.ds(pl.multiple_of(first * depth, depth), count * depth)
        a = jnp.concatenate([xb[layer, core, :, cols], xr[layer, :, cols]], axis=0)
        b = w[layer, pl.ds(first, count), hh * depth:(hh + 1) * depth].reshape(count * depth, 2 * HD)
        y = jnp.dot(a, b, preferred_element_type=jnp.float32)
        if fresh:
            acc[layer, hh] = y[:rows]
            give[layer, hh] = y[rows:]
        else:
            acc[layer, hh] += y[:rows]
            give[layer, hh] += y[rows:]

    def finish(layer, hh, ref, at):
        part_copy(layer, hh).wait_recv()
        r = lax.rsqrt(jnp.sum(ssq[layer], axis=-1, keepdims=True) / width + EPS)
        y = (acc[layer, hh] + take[layer, hh]) * r
        ref[at, 0] = rope(y[:, :HD], cos_ref[...], sin_ref[...]).astype(jnp.bfloat16)
        ref[at, 1] = y[:, HD:].astype(jnp.bfloat16)

    def attend(q_ref, q_first, k, v, x_ref, x_first, write):
        v = jnp.concatenate([v, jnp.ones((rows, HD), jnp.bfloat16)], axis=1)
        allowed = (col <= row)[None]
        q = jnp.concatenate(
            [q_ref[:, pl.ds(pl.multiple_of(q_first + h * HD, HD), HD)] for h in range(group)], axis=0)
        scores = lax.dot_general(q, k, (((1,), (1,)), ((), ())), preferred_element_type=jnp.float32)
        scores = jnp.where(allowed, scores.reshape(group, rows, rows), -1e30)
        top = jnp.max(scores, axis=-1, keepdims=True)
        p = jnp.exp2((scores - top) * scale).astype(jnp.bfloat16).reshape(group * rows, rows)
        mixed = jnp.dot(p, v, preferred_element_type=jnp.float32)
        mixed = mixed[:, :HD] / mixed[:, HD:]
        for h in range(group):
            cols = pl.ds(pl.multiple_of(x_first + h * HD, HD), HD)
            write(cols, (
                x_ref[:, cols].astype(jnp.float32) + mixed[h * rows:(h + 1) * rows]
            ).astype(jnp.bfloat16))

    def write_x1(cols, value):
        x1[:, cols] = value

    def write_out(cols, value):
        out[0, 0, :, cols] = value

    def queries_in():
        for load in loads:
            load.wait()

        @pl.when(side == 1)
        def _():
            q_local(1).wait()
            rope_queries(q1, 0, width // HD)

        @pl.when(side == 0)
        def _():
            q_local(0).wait()
            rope_queries(q0, 0, half // HD)
        ssq[...] = jnp.zeros_like(ssq)

    def inputs_in():
        hid_local.wait()
        hid_copy(1 - side).wait_recv()
        gain_copy(1 - side).wait_recv()

        def one(c, _):
            scaled(xs, c, 0)
            return 0
        lax.fori_loop(0, chips, one, 0)
        swap0.start()

    def first_layer():
        swap0.wait_recv()
        for hh in range(heads):
            project(0, hh, 0, chips, True)
            part_copy(0, hh).start()
        for hh in range(heads):
            finish(0, hh, kv0, hh)

    def first_attention(g):
        @pl.when(side == 1)
        def _():
            q_copy(g).wait_recv()
            rope_queries(q0, g * group, group)
        attend(q0, g * gw, kv0[g, 0], kv0[g, 1], xs, side * half + g * gw, write_x1)

        def one(b, _):
            x1_copy(side, b).start()
            scaled(x1, side * pieces + b, 1)
            swap_copy(side * pieces + b).start()
            return 0
        lax.fori_loop(g * per_group, (g + 1) * per_group, one, 0)

    def own_half():
        def one(b, _):
            swap_copy(side * pieces + b).wait_recv()
            return 0
        lax.fori_loop(0, pieces, one, 0)
        for hh in range(heads):
            project(1, hh, side * pieces, pieces, True)

    def mate_in(b, _):
        c = (1 - side) * pieces + b
        x1_copy(1 - side, b).wait_recv()
        scaled(x1, c, 1)
        swap_copy(c).start()
        return 0

    def drain_layer(layer):
        for kind, at, t, which in moves:
            if at == layer:
                move(kind, at, t, which, drain)

    moves = []
    for word in ORDER:
        if word[0] == "*":
            if word == "*Q":
                queries_in()
            elif word == "*X":
                inputs_in()
            elif word == "*P":
                first_layer()
            elif word[1] == "A":
                first_attention(int(word[2]))
            elif word == "*D":
                drain_layer(0)
            elif word == "*H":
                own_half()
            elif word == "*M":
                lax.fori_loop(0, pieces // 2, mate_in, 0)
        else:
            kind = word.rstrip("0123456789")
            digits = [int(d) for d in word[len(kind):]]
            step = (kind, digits[0], digits[1], digits[2] if len(digits) > 2 else None)
            moves.append(step)
            move(*step, relay)

    lax.fori_loop(pieces // 2, pieces, mate_in, 0)

    def wait_swap(b, _):
        swap_copy((1 - side) * pieces + b).wait_recv()
        return 0
    lax.fori_loop(0, pieces, wait_swap, 0)
    for hh in range(heads):
        project(1, hh, (1 - side) * pieces, pieces, False)
        part_copy(1, hh).start()
    for hh in range(heads):
        finish(1, hh, kv1, side * heads + hh)
        pl.when(side == 0)(lambda hh=hh: kv_copy(hh).start())

    @pl.when(side == 0)
    def _():
        out[0, 0] = x1[...]

    @pl.when(side == 1)
    def _():
        def one(g, _):
            head = jnp.where(g < heads, heads + g, g - heads)
            pl.when(g >= heads)(lambda: kv_copy(g - heads).wait_recv())
            attend(q1, head * gw, kv1[head, 0], kv1[head, 1], x1, head * gw, write_out)
            return 0
        lax.fori_loop(0, kv_heads, one, 0)

    drain_layer(1)
    for layer in range(2):
        @pl.when(side == layer)
        def _(layer=layer):
            for which in range(splits[layer] + 1):
                stage_copy(layer, which).wait_send()
    gain_copy(side).wait_send()
    hid_copy(side).wait_send()
    swap0.wait_send()
    for c in range(chips):
        swap_copy(c).wait_send()
    for layer in range(2):
        for hh in range(heads):
            part_copy(layer, hh).wait_send()
    for b in range(pieces):
        x1_copy(side, b).wait_send()

    @pl.when(side == 0)
    def _():
        for g in range(heads):
            q_copy(g).wait_send()
        for hh in range(heads):
            kv_copy(hh).wait_send()


def solution(mesh):
    sections, n = mesh.shape["section"], mesh.shape["fsdp"]
    chips = n // 2
    outer = 4 if chips % 4 == 0 else 1
    inner = chips // outer

    def body(hidden_in, queries, key_weight, value_weight, norm_gain):
        rows, width = queries.shape[2:]
        depth, kvw = key_weight.shape[1:]
        cosine, sine = rope_tables(rows)
        hbm = pl.BlockSpec(memory_space=pltpu.HBM)
        vmem = pl.BlockSpec(memory_space=pltpu.VMEM)
        dma = pltpu.SemaphoreType.DMA
        bf16, f32 = jnp.bfloat16, jnp.float32
        if sections == 2 and outer == 4 and depth % HD == 0:
            heads = kvw // HD // 2
            pieces = chips // 2
            run = functools.partial(pair_kernel, n, outer, inner)
            scratch = [
                pltpu.VMEM((2, chips, heads * depth, 2 * HD), bf16),
                pltpu.VMEM((heads * depth, 2 * HD), bf16),
                pltpu.VMEM((rows, width), bf16),
                pltpu.VMEM((rows, width), bf16),
                pltpu.VMEM((2, 2, rows, width // 2), bf16),
                pltpu.VMEM((2, rows, width // 2), bf16),
                pltpu.VMEM((rows, width // 2), bf16),
                pltpu.VMEM((rows, width), bf16),
                pltpu.VMEM((2, heads, rows, 2 * HD), f32),
                pltpu.VMEM((2, heads, rows, 2 * HD), f32),
                pltpu.VMEM((2, heads, rows, 2 * HD), f32),
                pltpu.VMEM((heads, 2, rows, HD), bf16),
                pltpu.VMEM((2 * heads, 2, rows, HD), bf16),
                pltpu.VMEM((2, 1, width), f32),
                pltpu.VMEM((2, rows, HD), f32),
                pltpu.VMEM((rows, HD), f32),
                pltpu.VMEM((rows, HD), f32),
                dma((2, 3, chips)), dma((2, 3, 4, chips)), dma((3,)), dma((4 * heads,)),
                dma((4,)), dma((2,)), dma((2,)), dma,
                dma((2, heads)), dma((2, pieces)), dma((2, heads)), dma((2,)), dma((2, chips)), dma((2, 2, heads)),
            ]
        else:
            run = functools.partial(chain_kernel, n, sections, outer, inner)
            scratch = [
                pltpu.VMEM((n, 2, depth, kvw), bf16),
                pltpu.VMEM((rows, width), bf16),
                pltpu.VMEM((rows, width), bf16),
                pltpu.VMEM((rows, width), bf16),
                pltpu.VMEM((rows, width), bf16),
                pltpu.VMEM((n // 2, rows, 2 * depth), bf16),
                pltpu.VMEM((2, rows, kvw), f32),
                pltpu.VMEM((kvw // HD, 2, rows, HD), bf16),
                pltpu.VMEM((kvw // HD, 2, rows, HD), bf16),
                pltpu.VMEM((1, width), f32),
                pltpu.VMEM((rows, HD), f32),
                pltpu.VMEM((rows, HD), f32),
                dma((3, n)), dma((3, 5, n)), dma((2,)), dma((sections,)), dma((2,)), dma,
                dma((2,)), dma((2, kvw // HD)), dma((2,)), dma((4,)),
            ]
        return pl.pallas_call(
            run,
            out_shape=jax.ShapeDtypeStruct(queries.shape, bf16),
            in_specs=[hbm] * 7,
            out_specs=vmem,
            scratch_shapes=scratch,
            compiler_params=pltpu.CompilerParams(
                collective_id=0, has_side_effects=True, vmem_limit_bytes=28 * 2**20
            ),
        )(*(
            pltpu.with_memory_space_constraint(x, pltpu.HBM)
            for x in (hidden_in, queries, key_weight, value_weight, norm_gain, jnp.asarray(cosine), jnp.asarray(sine))
        ))

    placed = (
        P("fsdp", "section", None),
        P("section", "fsdp", None, None),
        P("section", "fsdp", None),
        P("section", "fsdp", None),
        P("section", None),
    )
    return jax.shard_map(
        body, mesh=mesh, in_specs=placed, out_specs=P("section", "fsdp", None, None), check_vma=False
    )
```

```python
import functools
import math

import jax
import jax.numpy as jnp
import numpy as np
from jax import lax
from jax.experimental import pallas as pl
from jax.experimental.pallas import tpu as pltpu
from jax.sharding import PartitionSpec as P

HD = 128
EPS = 1e-05
MESH = pl.DeviceIdType.MESH


def rope_tables(rows):
    half = HD // 2
    frequency = np.exp(np.arange(half, dtype=np.float32) * np.float32(-2.0 * math.log(10000.0) / HD))
    angles = np.arange(rows, dtype=np.float32)[:, None] * frequency[None, :].astype(np.float32)
    cosine, sine = np.cos(angles), np.sin(angles)
    return (
        np.concatenate([cosine, cosine], 1).astype(np.float32),
        np.concatenate([-sine, sine], 1).astype(np.float32),
    )


def rope(u, cosine, sine):
    return u * cosine + pltpu.roll(u, HD // 2, 1) * sine


def chain_kernel(
    n, sections, outer, inner,
    hid, q_in, kw, vw, gain_in, cos_in, sin_in,
    out,
    w, xin, xs, qs, qp, normed, acc, kv, kvp, gain, cos_ref, sin_ref,
    w_recv, w_send, own_sem, hid_recv, hid_send, hid_own, q_sem, kv_sem, x_sem, load_sem,
):
    s = lax.axis_index("section")
    f = lax.axis_index("fsdp")
    core = lax.rem(f, 2)
    chip = f // 2
    i = lax.rem(chip, inner)
    o = chip // inner
    rows, width = xs.shape
    part = hid.shape[1]
    kvw = kw.shape[2]
    kv_heads = kvw // HD
    group = width // kvw
    depth = kw.shape[1]

    def index(oo, ii, cc):
        return (oo * inner + ii) * 2 + cc

    own_k = pltpu.make_async_copy(kw.at[0], w.at[f, 0], own_sem.at[0])
    own_v = pltpu.make_async_copy(vw.at[0], w.at[f, 1], own_sem.at[1])
    own_k.start()
    own_v.start()
    loads = [
        pltpu.make_async_copy(src, dst, load_sem.at[at])
        for at, (src, dst) in enumerate(
            ((q_in.at[0, 0], qs), (gain_in, gain), (cos_in, cos_ref), (sin_in, sin_ref)))
    ]
    for load in loads:
        load.start()

    targets = (
        (o > 0, index(o - 1, i, core)),
        (o < outer - 1, index(o + 1, i, core)),
        (i > 0, index(o, i - 1, core)),
        (i < inner - 1, index(o, i + 1, core)),
        (None, index(o, i, 1 - core)),
    )

    barrier = pltpu.get_barrier_semaphore()
    for cond, target in targets:
        def greet(target=target):
            pl.semaphore_signal(barrier, inc=1, device_id={"fsdp": target}, device_id_type=MESH)
        if cond is None:
            greet()
        else:
            pl.when(cond)(greet)
    for step in range(1, sections):
        pl.semaphore_signal(
            barrier, inc=1, device_id={"section": lax.rem(s + step, sections)}, device_id_type=MESH
        )
    expected = (
        jnp.where(o > 0, 1, 0) + jnp.where(o < outer - 1, 1, 0)
        + jnp.where(i > 0, 1, 0) + jnp.where(i < inner - 1, 1, 0) + sections
    )
    pl.semaphore_wait(barrier, expected)

    few = max(16, depth // 8)
    first = (depth - few + 16) // 32 * 16
    cuts = (pl.ds(0, first), pl.ds(first, depth - few - first), pl.ds(depth - few, few))
    mains, tail = (0, 1), 2

    def w_copy(which, way, origin):
        piece = w.at[origin, :, cuts[which]]
        return pltpu.make_async_remote_copy(
            src_ref=piece, dst_ref=piece,
            send_sem=w_send.at[which, way, origin], recv_sem=w_recv.at[which, origin],
            device_id={"fsdp": targets[way][1]}, device_id_type=MESH,
        )

    def w_start(which, way, origin):
        cond = targets[way][0]
        if cond is None:
            w_copy(which, way, origin).start()
        else:
            pl.when(cond)(lambda: w_copy(which, way, origin).start())

    own_k.wait()
    own_v.wait()
    for way in (2, 3):
        w_start(tail, way, f)
    for which in mains:
        for way in range(5):
            w_start(which, way, f)
    for way in (0, 1, 4):
        w_start(tail, way, f)

    mine = pl.ds(pl.multiple_of(s * part, part), part)

    def hid_copy(to):
        dst = xs if to == 0 else xin
        return pltpu.make_async_remote_copy(
            src_ref=hid.at[0], dst_ref=dst.at[mine], send_sem=hid_send.at[to],
            recv_sem=hid_recv.at[s], device_id={"section": to}, device_id_type=MESH,
        )

    def hid_local(to):
        dst = xs if to == 0 else xin
        return pltpu.make_async_copy(hid.at[0], dst.at[mine], hid_own)

    for to in range(min(2, sections)):
        pl.when(s != to)(lambda to=to: hid_copy(to).start())
        pl.when(s == to)(lambda to=to: hid_local(to).start())

    q_copy = pltpu.make_async_remote_copy(
        src_ref=q_in.at[0, 0], dst_ref=qp, send_sem=q_sem.at[0], recv_sem=q_sem.at[1],
        device_id={"section": jnp.minimum(s + 1, sections - 1)}, device_id_type=MESH,
    )
    def kv_copy(g):
        return pltpu.make_async_remote_copy(
            src_ref=kv.at[g], dst_ref=kvp.at[g], send_sem=kv_sem.at[0, g], recv_sem=kv_sem.at[1, g],
            device_id={"section": jnp.minimum(s + 1, sections - 1)}, device_id_type=MESH,
        )

    x_copy = pltpu.make_async_remote_copy(
        src_ref=xs, dst_ref=xin, send_sem=x_sem.at[0], recv_sem=x_sem.at[1],
        device_id={"section": jnp.minimum(s + 1, sections - 1)}, device_id_type=MESH,
    )
    last = s == sections - 1
    pl.when(jnp.logical_not(last))(lambda: q_copy.start())

    for load in loads:
        load.wait()

    def rope_queries(ref):
        def one(h, _):
            cols = pl.ds(pl.multiple_of(h * HD, HD), HD)
            u = ref[:, cols].astype(jnp.float32)
            ref[:, cols] = rope(u, cos_ref[...], sin_ref[...]).astype(jnp.bfloat16)
            return 0
        lax.fori_loop(0, width // HD, one, 0)

    rope_queries(qs)

    def hid_arrive(to):
        hid_local(to).wait()
        dst = xs if to == 0 else xin
        for step in range(1, sections):
            j = lax.rem(to + step, sections)
            pltpu.make_async_remote_copy(
                src_ref=hid.at[0], dst_ref=dst.at[pl.ds(j * part, part)],
                send_sem=hid_send.at[to], recv_sem=hid_recv.at[j],
                device_id={"section": to}, device_id_type=MESH,
            ).wait_recv()

    block = 16

    def norm():
        def one(r, _):
            at = pl.ds(pl.multiple_of(r * block, block), block)
            x = xs[at, :].astype(jnp.float32)
            mean_square = jnp.mean(x * x, axis=-1, keepdims=True)
            y = (x * lax.rsqrt(mean_square + EPS) * gain[...]).astype(jnp.bfloat16)
            for pair in range(n // 2):
                normed[pair, at, :] = y[:, pair * 2 * depth:(pair + 1) * 2 * depth]
            return 0
        lax.fori_loop(0, rows // block, one, 0)

    def project(pair):
        a = normed[pair]
        for half in range(2):
            b = w[pl.ds(pair * 2, 2), half].reshape(2 * depth, kvw)
            acc[half] += jnp.dot(a, b, preferred_element_type=jnp.float32)

    acc[...] = jnp.zeros_like(acc)

    def arrive(which, origin, ways):
        w_copy(which, 4, origin).wait_recv()
        for way in ways:
            w_start(which, way, origin)

    def relay(which, origin, ways):
        arrive(which, origin, ways)

    def from_other(which, origin, ways):
        arrive(which, origin, ())

    def project_pair(which, origin, ways):
        if which == tail - 1:
            project(origin // 2)

    def sides(t, act):
        for sign, way in ((-1, 1), (1, 0)):
            far = o - t if sign < 0 else o + t
            there = (far >= 0) if sign < 0 else ((far < outer) & (t > 0))
            act(far, there, way)

    def around(there, act):
        for d in range(1, inner):
            pl.when(there & (i - d >= 0))(lambda d=d: act(i - d, 3))
            pl.when(there & (i + d < inner))(lambda d=d: act(i + d, 2))

    def along_outer(t, c, receive):
        for which in mains:
            def act(far, there, way, which=which):
                pl.when(there)(lambda: receive(which, index(far, i, c), (way, 2, 3, 4)))
            sides(t, act)

        def act_tail(far, there, way):
            pl.when(there)(lambda: receive(tail, index(far, i, c), (way, 4)))
            around(there, lambda ii, _: receive(tail, index(far, ii, c), (way, 4)))
        sides(t, act_tail)

    def along_inner(t, c, receive):
        for which in mains:
            def act(far, there, _, which=which):
                around(there, lambda ii, way: receive(which, index(far, ii, c), (way, 4)))
            sides(t, act)

    def first_inner(c, receive):
        around(o >= 0, lambda ii, way: receive(tail, index(o, ii, c), (way, 0, 1, 4)))

    first_inner(core, relay)

    def step(t, _):
        along_outer(t + 1, core, relay)

        @pl.when((t == 0) & (s == 0))
        def _():
            hid_arrive(0)
            norm()

        @pl.when(t == 0)
        def _():
            for which in (*mains, tail):
                arrive(which, index(o, i, 1 - core), ())
            first_inner(1 - core, from_other)

        along_inner(t, core, relay)
        along_outer(t + 1, 1 - core, from_other)
        along_inner(t, 1 - core, from_other)

        @pl.when(s == 0)
        def _():
            pl.when(t == 0)(lambda: project(chip))
            along_outer(t + 1, core, project_pair)
            along_inner(t, core, project_pair)

        return 0

    lax.fori_loop(0, outer, step, 0)

    row = lax.broadcasted_iota(jnp.int32, (rows, rows), 0)
    col = lax.broadcasted_iota(jnp.int32, (rows, rows), 1)
    scale = math.log2(math.e) / math.sqrt(HD)

    def attend(q_ref, kv_ref, x_ref, o_write, ready):
        ones = jnp.ones((rows, HD), jnp.bfloat16)
        allowed = (col <= row)[None]

        def one(g, _):
            ready(g)
            k = kv_ref[g, 0]
            v = jnp.concatenate([kv_ref[g, 1], ones], axis=1)
            base = g * group * HD
            cols = [pl.ds(pl.multiple_of(base + h * HD, HD), HD) for h in range(group)]
            q = jnp.concatenate([q_ref[:, c] for c in cols], axis=0)
            scores = lax.dot_general(q, k, (((1,), (1,)), ((), ())), preferred_element_type=jnp.float32)
            scores = jnp.where(allowed, scores.reshape(group, rows, rows), -1e30)
            top = jnp.max(scores, axis=-1, keepdims=True)
            p = jnp.exp2((scores - top) * scale).astype(jnp.bfloat16).reshape(group * rows, rows)
            mixed = jnp.dot(p, v, preferred_element_type=jnp.float32)
            mixed = mixed[:, :HD] / mixed[:, HD:]
            for h in range(group):
                o_write(cols[h], (
                    x_ref[:, cols[h]].astype(jnp.float32) + mixed[h * rows:(h + 1) * rows]
                ).astype(jnp.bfloat16))
            return 0

        lax.fori_loop(0, kv_heads, one, 0)

    def write_xs(c, value):
        xs[:, c] = value

    def write_out(c, value):
        out[0, 0, :, c] = value

    @pl.when(s > 0)
    def _():
        q_copy.wait_recv()
        rope_queries(qp)
        pl.when(s == 1)(lambda: hid_arrive(1))
        if sections > 2:
            pl.when(s > 1)(lambda: x_copy.wait_recv())
        attend(qp, kvp, xin, write_xs, lambda g: kv_copy(g).wait_recv())
        if sections > 2:
            pl.when(jnp.logical_not(last))(lambda: x_copy.start())
        norm()
        def one(j, _):
            project(j)
            return 0
        lax.fori_loop(0, n // 2, one, 0)

    for h in range(kv_heads):
        at = slice(h * HD, (h + 1) * HD)
        kv[h, 0] = rope(acc[0, :, at], cos_ref[...], sin_ref[...]).astype(jnp.bfloat16)
        kv[h, 1] = acc[1, :, at].astype(jnp.bfloat16)
        pl.when(jnp.logical_not(last))(lambda h=h: kv_copy(h).start())
    attend(qs, kv, xs, write_out, lambda g: None)

    def drain(which, origin, ways):
        for way in ways:
            cond = targets[way][0]
            if cond is None:
                w_copy(which, way, origin).wait_send()
            else:
                pl.when(cond)(lambda way=way: w_copy(which, way, origin).wait_send())

    for which in (*mains, tail):
        drain(which, f, range(5))
    first_inner(core, drain)

    def drain_step(t, _):
        along_outer(t + 1, core, drain)
        along_inner(t, core, drain)
        return 0

    lax.fori_loop(0, outer, drain_step, 0)
    for to in range(min(2, sections)):
        pl.when(s != to)(lambda to=to: hid_copy(to).wait_send())

    @pl.when(jnp.logical_not(last))
    def _():
        q_copy.wait_send()
        for h in range(kv_heads):
            kv_copy(h).wait_send()
        if sections > 2:
            pl.when(s > 0)(lambda: x_copy.wait_send())


ORDER = (
    "OT11", "OM000", "OM110", "OT00", "OM001", "OM111", "*Q", "OM010", "OM011", "OT01", "OU01", "ZM000",
    "ZM001", "F00", "OM101", "OU00", "ZM011", "ZM010", "ZM021", "ZM020", "ZT00", "*X", "Y010", "Y011", "ZT01",
    "OM100", "Y001", "Y020", "Y031", "OT10", "Y000", "Y021", "*R0", "ZT02", "Y030", "*P", "ZM101", "ZM100",
    "*A0", "OU11", "ZM110", "ZM111", "OU10", "F10", "*R1", "*A1", "*C", "*D", "ZM120", "Y101", "Y100",
    "ZM121", "ZT10", "ZT11", "*M", "Y110", "Y120", "Y130", "*S", "Y111", "Y121", "Y131", "*T", "ZT12",
)


def pair_kernel(
    n, outer, inner,
    hid, q_in, kw, vw, gain_in, cos_in, sin_in,
    out,
    w, stage, xs, x1, xb, xr, q0, q1, acc, give, take, kv0, kv1, gains, ssq, cos_ref, sin_ref,
    w_recv, w_send, stage_send, own_sem, load_sem, gain_sem, hid_sem, hid_own,
    q_sem, x1_sem, kv_sem, swap0_sem, swap_sem, part_sem,
):
    side = lax.axis_index("section")
    f = lax.axis_index("fsdp")
    mate = {"section": 1 - side}
    core = lax.rem(f, 2)
    chip = f // 2
    i = lax.rem(chip, inner)
    o = chip // inner
    twin = {"fsdp": 2 * chip + 1 - core}
    rows, width = xs.shape
    part = hid.shape[1]
    kvw = kw.shape[2]
    kv_heads = kvw // HD
    heads = kv_heads // 2
    group = width // kvw
    gw = group * HD
    depth = kw.shape[1]
    chips = n // 2
    blk = width // chips
    half = width // 2
    pieces = half // blk
    per_group = gw // blk

    local = []
    for hh in range(heads):
        for to_mate in (False, True):
            head = (1 - side if to_mate else side) * heads + hh
            cols = pl.ds(pl.multiple_of(head * HD, HD), HD)
            at = pl.ds(hh * depth, depth)
            for kind, src in enumerate((kw, vw)):
                lanes = pl.ds(kind * HD, HD)
                dst = stage.at[at, lanes] if to_mate else w.at[side, chip, at, lanes]
                local.append(pltpu.make_async_copy(src.at[0, :, cols], dst, own_sem.at[len(local)]))
    for copy in local:
        copy.start()
    loads = [
        pltpu.make_async_copy(src, dst, load_sem.at[at])
        for at, (src, dst) in enumerate(
            ((gain_in, gains.at[side]), (cos_in, cos_ref), (sin_in, sin_ref)))
    ]
    for load in loads:
        load.start()

    def q_local(which):
        if which == 0:
            return pltpu.make_async_copy(q_in.at[0, 0, :, pl.ds(0, half)], q0, load_sem.at[3])
        return pltpu.make_async_copy(q_in.at[0, 0], q1, load_sem.at[3])

    for which in range(2):
        pl.when(side == which)(lambda which=which: q_local(which).start())

    def index(oo, ii):
        return (oo * inner + ii) * 2 + core

    targets = (
        (o > 0, index(o - 1, i)),
        (o < outer - 1, index(o + 1, i)),
        (i > 0, index(o, i - 1)),
        (i < inner - 1, index(o, i + 1)),
    )

    barrier = pltpu.get_barrier_semaphore()
    for cond, target in targets:
        pl.when(cond)(lambda target=target: pl.semaphore_signal(
            barrier, inc=1, device_id={"fsdp": target}, device_id_type=MESH))
    for device in (twin, mate):
        pl.semaphore_signal(barrier, inc=1, device_id=device, device_id_type=MESH)
    expected = (
        jnp.where(o > 0, 1, 0) + jnp.where(o < outer - 1, 1, 0)
        + jnp.where(i > 0, 1, 0) + jnp.where(i < inner - 1, 1, 0) + 2
    )
    pl.semaphore_wait(barrier, expected)

    deep = heads * depth
    few = max(16, (deep * 96 // 512 + 8) // 16 * 16)
    early = (heads - 1) * depth
    cuts = (pl.ds(0, early), pl.ds(early, deep - few - early), pl.ds(deep - few, few))
    tail = 2

    def w_copy(layer, which, way, origin):
        piece = w.at[layer, origin, cuts[which]]
        return pltpu.make_async_remote_copy(
            src_ref=piece, dst_ref=piece,
            send_sem=w_send.at[layer, which, way, origin], recv_sem=w_recv.at[layer, which, origin],
            device_id={"fsdp": targets[way][1]}, device_id_type=MESH,
        )

    def w_start(layer, which, way, origin):
        pl.when(targets[way][0])(lambda: w_copy(layer, which, way, origin).start())

    def stage_copy(layer, which):
        return pltpu.make_async_remote_copy(
            src_ref=stage.at[cuts[which]], dst_ref=w.at[layer, chip, cuts[which]],
            send_sem=stage_send.at[which], recv_sem=w_recv.at[layer, which, chip],
            device_id=mate, device_id_type=MESH,
        )

    def gain_copy(layer):
        return pltpu.make_async_remote_copy(
            src_ref=gain_in, dst_ref=gains.at[layer], send_sem=gain_sem.at[0], recv_sem=gain_sem.at[1],
            device_id=mate, device_id_type=MESH,
        )

    def hid_copy(of):
        return pltpu.make_async_remote_copy(
            src_ref=hid.at[0], dst_ref=xs.at[pl.ds(pl.multiple_of(of * part, part), part)],
            send_sem=hid_sem.at[0], recv_sem=hid_sem.at[1], device_id=mate, device_id_type=MESH,
        )

    hid_local = pltpu.make_async_copy(
        hid.at[0], xs.at[pl.ds(pl.multiple_of(side * part, part), part)], hid_own)

    def q_copy(g):
        return pltpu.make_async_remote_copy(
            src_ref=q_in.at[0, 0, :, pl.ds(half + g * gw, gw)], dst_ref=q0.at[:, pl.ds(g * gw, gw)],
            send_sem=q_sem.at[0, g], recv_sem=q_sem.at[1, g], device_id=mate, device_id_type=MESH,
        )

    def x1_copy(of, b):
        cols = pl.ds(pl.multiple_of(of * half + b * blk, blk), blk)
        return pltpu.make_async_remote_copy(
            src_ref=x1.at[:, cols], dst_ref=x1.at[:, cols],
            send_sem=x1_sem.at[0, b], recv_sem=x1_sem.at[1, b], device_id=mate, device_id_type=MESH,
        )

    def kv_copy(hh):
        return pltpu.make_async_remote_copy(
            src_ref=kv1.at[hh], dst_ref=kv1.at[hh],
            send_sem=kv_sem.at[0, hh], recv_sem=kv_sem.at[1, hh], device_id=mate, device_id_type=MESH,
        )

    swap0 = pltpu.make_async_remote_copy(
        src_ref=xb.at[0, 1 - core], dst_ref=xr.at[0], send_sem=swap0_sem.at[0], recv_sem=swap0_sem.at[1],
        device_id=twin, device_id_type=MESH,
    )

    def swap_copy(c):
        cols = pl.ds(pl.multiple_of(c * depth, depth), depth)
        return pltpu.make_async_remote_copy(
            src_ref=xb.at[1, 1 - core, :, cols], dst_ref=xr.at[1, :, cols],
            send_sem=swap_sem.at[0, c], recv_sem=swap_sem.at[1, c], device_id=twin, device_id_type=MESH,
        )

    def part_copy(layer, hh):
        return pltpu.make_async_remote_copy(
            src_ref=give.at[layer, hh], dst_ref=take.at[layer, hh],
            send_sem=part_sem.at[0, layer, hh], recv_sem=part_sem.at[1, layer, hh],
            device_id=twin, device_id_type=MESH,
        )

    for copy in local:
        copy.wait()

    for layer in range(2):
        @pl.when(side == layer)
        def _(layer=layer):
            for which in range(3):
                stage_copy(layer, which).start()
    gain_copy(side).start()
    hid_copy(side).start()
    hid_local.start()

    @pl.when(side == 0)
    def _():
        for g in range(heads):
            q_copy(g).start()

    def rope_queries(ref, first, count):
        together = math.gcd(count, 4)

        def one(at, _):
            cosine, sine = cos_ref[...], sin_ref[...]
            for h in range(together):
                cols = pl.ds(pl.multiple_of((first + at * together + h) * HD, HD), HD)
                u = ref[:, cols].astype(jnp.float32)
                ref[:, cols] = rope(u, cosine, sine).astype(jnp.bfloat16)
            return 0
        lax.fori_loop(0, count // together, one, 0)

    def relay(layer, which, origin, ways):
        w_copy(layer, which, 0, origin).wait_recv()
        for way in ways:
            w_start(layer, which, way, origin)

    def drain(layer, which, origin, ways):
        for way in ways:
            pl.when(targets[way][0])(lambda way=way: w_copy(layer, which, way, origin).wait_send())

    def sides(t, act):
        if t == 0:
            act(o, None, 0)
        else:
            act(o - t, o - t >= 0, 1)
            act(o + t, o + t < outer, 0)

    def around(there, act):
        for d in range(1, inner):
            for cond, ii, way in ((i - d >= 0, i - d, 3), (i + d < inner, i + d, 2)):
                pl.when(cond if there is None else there & cond)(lambda ii=ii, way=way: act(ii, way))

    def own(kind, layer, on, which, receive):
        ways = {"OM": (0, 1, 2, 3), "OT": (2, 3), "OU": (0, 1)}[kind]

        @pl.when(side == on)
        def _():
            if receive is relay:
                if on != layer and kind != "OU":
                    w_copy(layer, which, 0, chip).wait_recv()
                for way in ways:
                    w_start(layer, which, way, chip)
            else:
                drain(layer, which, chip, ways)

    def far(t, act):
        sides(t, lambda oo, there, way: pl.when(there)(lambda: act(oo, way)))

    def move(kind, layer, t, which, receive):
        if kind[0] == "O":
            own(kind, layer, t, tail if which is None else which, receive)
        elif kind == "F":
            around(None, lambda ii, way: receive(layer, tail, o * inner + ii, (way, 0, 1)))
        elif kind == "ZM":
            far(t + 1, lambda oo, way: receive(layer, which, oo * inner + i, (way, 2, 3)))
        elif kind == "ZT":
            def both(oo, there, way):
                pl.when(there)(lambda: receive(layer, tail, oo * inner + i, (way,)))
                around(there, lambda ii, _: receive(layer, tail, oo * inner + ii, (way,)))
            sides(t + 1, both)
        elif kind == "Y":
            sides(t, lambda oo, there, _: around(
                there, lambda ii, way: receive(layer, which, oo * inner + ii, (way,))))

    row = lax.broadcasted_iota(jnp.int32, (rows, rows), 0)
    col = lax.broadcasted_iota(jnp.int32, (rows, rows), 1)
    scale = math.log2(math.e) / math.sqrt(HD)

    def scaled(src, c, layer):
        cols = pl.ds(pl.multiple_of(c * blk, blk), blk)
        x = src[:, cols].astype(jnp.float32)
        y = (x * gains[layer, :, cols]).astype(jnp.bfloat16)
        for kind in range(2):
            xb[layer, kind, :, pl.ds(pl.multiple_of(c * depth, depth), depth)] = y[:, kind * depth:(kind + 1) * depth]
        square = x * x
        total = square[:, :HD]
        for at in range(1, blk // HD):
            total += square[:, at * HD:(at + 1) * HD]
        ssq[layer] += total

    def project(layer, hh, first, count, fresh):
        cols = pl.ds(pl.multiple_of(first * depth, depth), count * depth)
        a = jnp.concatenate([xb[layer, core, :, cols], xr[layer, :, cols]], axis=0)
        b = w[layer, pl.ds(first, count), hh * depth:(hh + 1) * depth].reshape(count * depth, 2 * HD)
        y = jnp.dot(a, b, preferred_element_type=jnp.float32)
        if fresh:
            acc[layer, hh] = y[:rows]
            give[layer, hh] = y[rows:]
        else:
            acc[layer, hh] += y[:rows]
            give[layer, hh] += y[rows:]

    def finish(layer, hh, ref, at):
        part_copy(layer, hh).wait_recv()
        r = lax.rsqrt(jnp.sum(ssq[layer], axis=-1, keepdims=True) / width + EPS)
        y = (acc[layer, hh] + take[layer, hh]) * r
        ref[at, 0] = rope(y[:, :HD], cos_ref[...], sin_ref[...]).astype(jnp.bfloat16)
        ref[at, 1] = y[:, HD:].astype(jnp.bfloat16)

    def attend(q_ref, q_first, k, v, x_ref, x_first, write):
        v = jnp.concatenate([v, jnp.ones((rows, HD), jnp.bfloat16)], axis=1)
        allowed = (col <= row)[None]
        q = jnp.concatenate(
            [q_ref[:, pl.ds(pl.multiple_of(q_first + h * HD, HD), HD)] for h in range(group)], axis=0)
        scores = lax.dot_general(q, k, (((1,), (1,)), ((), ())), preferred_element_type=jnp.float32)
        scores = jnp.where(allowed, scores.reshape(group, rows, rows), -1e30)
        top = jnp.max(scores, axis=-1, keepdims=True)
        p = jnp.exp2((scores - top) * scale).astype(jnp.bfloat16).reshape(group * rows, rows)
        mixed = jnp.dot(p, v, preferred_element_type=jnp.float32)
        mixed = mixed[:, :HD] / mixed[:, HD:]
        for h in range(group):
            cols = pl.ds(pl.multiple_of(x_first + h * HD, HD), HD)
            write(cols, (
                x_ref[:, cols].astype(jnp.float32) + mixed[h * rows:(h + 1) * rows]
            ).astype(jnp.bfloat16))

    def write_x1(cols, value):
        x1[:, cols] = value

    def write_out(cols, value):
        out[0, 0, :, cols] = value

    def queries_in():
        for load in loads:
            load.wait()

        @pl.when(side == 1)
        def _():
            q_local(1).wait()
            rope_queries(q1, 0, width // HD)

        @pl.when(side == 0)
        def _():
            q_local(0).wait()
            rope_queries(q0, 0, half // HD)
        ssq[...] = jnp.zeros_like(ssq)

    def inputs_in():
        hid_local.wait()
        hid_copy(1 - side).wait_recv()
        gain_copy(1 - side).wait_recv()

        def one(c, _):
            scaled(xs, c, 0)
            return 0
        lax.fori_loop(0, chips, one, 0)
        swap0.start()

    def first_layer():
        swap0.wait_recv()
        for hh in range(heads):
            project(0, hh, 0, chips, True)
            part_copy(0, hh).start()

    def queries_arrive(g):
        @pl.when(side == 1)
        def _():
            q_copy(g).wait_recv()
            rope_queries(q0, g * group, group)

    def first_attention(g):
        finish(0, g, kv0, g)
        attend(q0, g * gw, kv0[g, 0], kv0[g, 1], xs, side * half + g * gw, write_x1)

        def one(b, _):
            x1_copy(side, b).start()
            scaled(x1, side * pieces + b, 1)
            swap_copy(side * pieces + b).start()
            return 0
        lax.fori_loop(g * per_group, (g + 1) * per_group, one, 0)

    def mate_in():
        def one(b, _):
            c = (1 - side) * pieces + b
            x1_copy(1 - side, b).wait_recv()
            scaled(x1, c, 1)
            swap_copy(c).start()
            return 0
        lax.fori_loop(0, pieces, one, 0)

    def swapped(of):
        def one(b, _):
            swap_copy(of * pieces + b).wait_recv()
            return 0
        lax.fori_loop(0, pieces, one, 0)

    def second_layer(hh, first, count, fresh, send=True):
        project(1, hh, first, count, fresh)
        if send:
            part_copy(1, hh).start()

    def second_done(hh):
        finish(1, hh, kv1, side * heads + hh)

    def send_done(hh):
        @pl.when(side == 0)
        def _():
            second_done(hh)
            kv_copy(hh).start()

    def first_side_in():
        @pl.when(side == 0)
        def _():
            mate_in()
            out[0, 0] = x1[...]
            swapped(1)
        swapped(side)

    def early_heads():
        for hh in range(heads - 1):
            pl.when(side == 0)(lambda hh=hh: second_layer(hh, 0, chips, True))
            pl.when(side == 1)(lambda hh=hh: second_layer(hh, side * pieces, pieces, True, send=False))

    def settle_first():
        for layer in range(2):
            @pl.when(side == layer)
            def _(layer=layer):
                for which in range(3):
                    stage_copy(layer, which).wait_send()
        gain_copy(side).wait_send()
        hid_copy(side).wait_send()
        swap0.wait_send()
        for hh in range(heads):
            part_copy(0, hh).wait_send()

    def drain_moves(layers):
        for step in [step for step in moves if step[1] in layers]:
            moves.remove(step)
            move(*step, drain)

    moves = []
    for word in ORDER:
        if word[0] == "*":
            if word == "*Q":
                queries_in()
            elif word == "*X":
                inputs_in()
            elif word == "*P":
                first_layer()
            elif word[1] == "A":
                first_attention(int(word[2]))
            elif word == "*C":
                settle_first()
            elif word == "*D":
                drain_moves((0,))
            elif word[1] == "R":
                queries_arrive(int(word[2]))
            elif word == "*M":
                first_side_in()
            elif word == "*S":
                early_heads()
            elif word == "*T":
                for hh in range(heads - 1):
                    send_done(hh)
        else:
            kind = word.rstrip("0123456789")
            digits = [int(d) for d in word[len(kind):]]
            step = (kind, digits[0], digits[1], digits[2] if len(digits) > 2 else None)
            moves.append(step)
            move(*step, relay)

    @pl.when(side == 1)
    def _():
        mate_in()
        swapped(0)
        for hh in range(heads - 1):
            second_layer(hh, (1 - side) * pieces, pieces, False)
    second_layer(heads - 1, 0, chips, True)
    send_done(heads - 1)

    @pl.when(side == 1)
    def _():
        for hh in range(heads - 1):
            second_done(hh)

        def one(g, _):
            pl.when(g == heads - 1)(lambda: second_done(heads - 1))
            attend(q1, (heads + g) * gw, kv1[heads + g, 0], kv1[heads + g, 1], x1, (heads + g) * gw, write_out)
            return 0
        lax.fori_loop(0, heads, one, 0)

    drain_moves((0, 1))
    for c in range(chips):
        swap_copy(c).wait_send()
    for hh in range(heads):
        part_copy(1, hh).wait_send()
    for b in range(pieces):
        x1_copy(side, b).wait_send()

    @pl.when(side == 0)
    def _():
        for g in range(heads):
            q_copy(g).wait_send()
        for hh in range(heads):
            kv_copy(hh).wait_send()

    @pl.when(side == 1)
    def _():
        def one(g, _):
            kv_copy(g).wait_recv()
            attend(q1, g * gw, kv1[g, 0], kv1[g, 1], x1, g * gw, write_out)
            return 0
        lax.fori_loop(0, heads, one, 0)


def solution(mesh):
    sections, n = mesh.shape["section"], mesh.shape["fsdp"]
    chips = n // 2
    outer = 4 if chips % 4 == 0 else 1
    inner = chips // outer

    def body(hidden_in, queries, key_weight, value_weight, norm_gain):
        rows, width = queries.shape[2:]
        depth, kvw = key_weight.shape[1:]
        cosine, sine = rope_tables(rows)
        hbm = pl.BlockSpec(memory_space=pltpu.HBM)
        vmem = pl.BlockSpec(memory_space=pltpu.VMEM)
        dma = pltpu.SemaphoreType.DMA
        bf16, f32 = jnp.bfloat16, jnp.float32
        if sections == 2 and outer == 4 and depth % HD == 0:
            heads = kvw // HD // 2
            pieces = chips // 2
            run = functools.partial(pair_kernel, n, outer, inner)
            scratch = [
                pltpu.VMEM((2, chips, heads * depth, 2 * HD), bf16),
                pltpu.VMEM((heads * depth, 2 * HD), bf16),
                pltpu.VMEM((rows, width), bf16),
                pltpu.VMEM((rows, width), bf16),
                pltpu.VMEM((2, 2, rows, width // 2), bf16),
                pltpu.VMEM((2, rows, width // 2), bf16),
                pltpu.VMEM((rows, width // 2), bf16),
                pltpu.VMEM((rows, width), bf16),
                pltpu.VMEM((2, heads, rows, 2 * HD), f32),
                pltpu.VMEM((2, heads, rows, 2 * HD), f32),
                pltpu.VMEM((2, heads, rows, 2 * HD), f32),
                pltpu.VMEM((heads, 2, rows, HD), bf16),
                pltpu.VMEM((2 * heads, 2, rows, HD), bf16),
                pltpu.VMEM((2, 1, width), f32),
                pltpu.VMEM((2, rows, HD), f32),
                pltpu.VMEM((rows, HD), f32),
                pltpu.VMEM((rows, HD), f32),
                dma((2, 3, chips)), dma((2, 3, 4, chips)), dma((3,)), dma((4 * heads,)),
                dma((4,)), dma((2,)), dma((2,)), dma,
                dma((2, heads)), dma((2, pieces)), dma((2, heads)), dma((2,)), dma((2, chips)), dma((2, 2, heads)),
            ]
        else:
            run = functools.partial(chain_kernel, n, sections, outer, inner)
            scratch = [
                pltpu.VMEM((n, 2, depth, kvw), bf16),
                pltpu.VMEM((rows, width), bf16),
                pltpu.VMEM((rows, width), bf16),
                pltpu.VMEM((rows, width), bf16),
                pltpu.VMEM((rows, width), bf16),
                pltpu.VMEM((n // 2, rows, 2 * depth), bf16),
                pltpu.VMEM((2, rows, kvw), f32),
                pltpu.VMEM((kvw // HD, 2, rows, HD), bf16),
                pltpu.VMEM((kvw // HD, 2, rows, HD), bf16),
                pltpu.VMEM((1, width), f32),
                pltpu.VMEM((rows, HD), f32),
                pltpu.VMEM((rows, HD), f32),
                dma((3, n)), dma((3, 5, n)), dma((2,)), dma((sections,)), dma((2,)), dma,
                dma((2,)), dma((2, kvw // HD)), dma((2,)), dma((4,)),
            ]
        return pl.pallas_call(
            run,
            out_shape=jax.ShapeDtypeStruct(queries.shape, bf16),
            in_specs=[hbm] * 7,
            out_specs=vmem,
            scratch_shapes=scratch,
            compiler_params=pltpu.CompilerParams(
                collective_id=0, has_side_effects=True, vmem_limit_bytes=28 * 2**20
            ),
        )(*(
            pltpu.with_memory_space_constraint(x, pltpu.HBM)
            for x in (hidden_in, queries, key_weight, value_weight, norm_gain, jnp.asarray(cosine), jnp.asarray(sine))
        ))

    placed = (
        P("fsdp", "section", None),
        P("section", "fsdp", None, None),
        P("section", "fsdp", None),
        P("section", "fsdp", None),
        P("section", None),
    )
    return jax.shard_map(
        body, mesh=mesh, in_specs=placed, out_specs=P("section", "fsdp", None, None), check_vma=False
    )
```

```python
import functools
import math

import jax
import jax.numpy as jnp
import numpy as np
from jax import lax
from jax.experimental import pallas as pl
from jax.experimental.pallas import tpu as pltpu
from jax.sharding import PartitionSpec as P

HD = 128
EPS = 1e-05
MESH = pl.DeviceIdType.MESH


def rope_tables(rows):
    half = HD // 2
    frequency = np.exp(np.arange(half, dtype=np.float32) * np.float32(-2.0 * math.log(10000.0) / HD))
    angles = np.arange(rows, dtype=np.float32)[:, None] * frequency[None, :].astype(np.float32)
    cosine, sine = np.cos(angles), np.sin(angles)
    return (
        np.concatenate([cosine, cosine], 1).astype(np.float32),
        np.concatenate([-sine, sine], 1).astype(np.float32),
    )


def rope(u, cosine, sine):
    return u * cosine + pltpu.roll(u, HD // 2, 1) * sine


def chain_kernel(
    n, sections, outer, inner,
    hid, q_in, kw, vw, gain_in, cos_in, sin_in,
    out,
    w, xin, xs, qs, qp, normed, acc, kv, kvp, gain, cos_ref, sin_ref,
    w_recv, w_send, own_sem, hid_recv, hid_send, hid_own, q_sem, kv_sem, x_sem, load_sem,
):
    s = lax.axis_index("section")
    f = lax.axis_index("fsdp")
    core = lax.rem(f, 2)
    chip = f // 2
    i = lax.rem(chip, inner)
    o = chip // inner
    rows, width = xs.shape
    part = hid.shape[1]
    kvw = kw.shape[2]
    kv_heads = kvw // HD
    group = width // kvw
    depth = kw.shape[1]

    def index(oo, ii, cc):
        return (oo * inner + ii) * 2 + cc

    own_k = pltpu.make_async_copy(kw.at[0], w.at[f, 0], own_sem.at[0])
    own_v = pltpu.make_async_copy(vw.at[0], w.at[f, 1], own_sem.at[1])
    own_k.start()
    own_v.start()
    loads = [
        pltpu.make_async_copy(src, dst, load_sem.at[at])
        for at, (src, dst) in enumerate(
            ((q_in.at[0, 0], qs), (gain_in, gain), (cos_in, cos_ref), (sin_in, sin_ref)))
    ]
    for load in loads:
        load.start()

    targets = (
        (o > 0, index(o - 1, i, core)),
        (o < outer - 1, index(o + 1, i, core)),
        (i > 0, index(o, i - 1, core)),
        (i < inner - 1, index(o, i + 1, core)),
        (None, index(o, i, 1 - core)),
    )

    barrier = pltpu.get_barrier_semaphore()
    for cond, target in targets:
        def greet(target=target):
            pl.semaphore_signal(barrier, inc=1, device_id={"fsdp": target}, device_id_type=MESH)
        if cond is None:
            greet()
        else:
            pl.when(cond)(greet)
    for step in range(1, sections):
        pl.semaphore_signal(
            barrier, inc=1, device_id={"section": lax.rem(s + step, sections)}, device_id_type=MESH
        )
    expected = (
        jnp.where(o > 0, 1, 0) + jnp.where(o < outer - 1, 1, 0)
        + jnp.where(i > 0, 1, 0) + jnp.where(i < inner - 1, 1, 0) + sections
    )
    pl.semaphore_wait(barrier, expected)

    few = max(16, depth // 8)
    first = (depth - few + 16) // 32 * 16
    cuts = (pl.ds(0, first), pl.ds(first, depth - few - first), pl.ds(depth - few, few))
    mains, tail = (0, 1), 2

    def w_copy(which, way, origin):
        piece = w.at[origin, :, cuts[which]]
        return pltpu.make_async_remote_copy(
            src_ref=piece, dst_ref=piece,
            send_sem=w_send.at[which, way, origin], recv_sem=w_recv.at[which, origin],
            device_id={"fsdp": targets[way][1]}, device_id_type=MESH,
        )

    def w_start(which, way, origin):
        cond = targets[way][0]
        if cond is None:
            w_copy(which, way, origin).start()
        else:
            pl.when(cond)(lambda: w_copy(which, way, origin).start())

    own_k.wait()
    own_v.wait()
    for way in (2, 3):
        w_start(tail, way, f)
    for which in mains:
        for way in range(5):
            w_start(which, way, f)
    for way in (0, 1, 4):
        w_start(tail, way, f)

    mine = pl.ds(pl.multiple_of(s * part, part), part)

    def hid_copy(to):
        dst = xs if to == 0 else xin
        return pltpu.make_async_remote_copy(
            src_ref=hid.at[0], dst_ref=dst.at[mine], send_sem=hid_send.at[to],
            recv_sem=hid_recv.at[s], device_id={"section": to}, device_id_type=MESH,
        )

    def hid_local(to):
        dst = xs if to == 0 else xin
        return pltpu.make_async_copy(hid.at[0], dst.at[mine], hid_own)

    for to in range(min(2, sections)):
        pl.when(s != to)(lambda to=to: hid_copy(to).start())
        pl.when(s == to)(lambda to=to: hid_local(to).start())

    q_copy = pltpu.make_async_remote_copy(
        src_ref=q_in.at[0, 0], dst_ref=qp, send_sem=q_sem.at[0], recv_sem=q_sem.at[1],
        device_id={"section": jnp.minimum(s + 1, sections - 1)}, device_id_type=MESH,
    )
    def kv_copy(g):
        return pltpu.make_async_remote_copy(
            src_ref=kv.at[g], dst_ref=kvp.at[g], send_sem=kv_sem.at[0, g], recv_sem=kv_sem.at[1, g],
            device_id={"section": jnp.minimum(s + 1, sections - 1)}, device_id_type=MESH,
        )

    x_copy = pltpu.make_async_remote_copy(
        src_ref=xs, dst_ref=xin, send_sem=x_sem.at[0], recv_sem=x_sem.at[1],
        device_id={"section": jnp.minimum(s + 1, sections - 1)}, device_id_type=MESH,
    )
    last = s == sections - 1
    pl.when(jnp.logical_not(last))(lambda: q_copy.start())

    for load in loads:
        load.wait()

    def rope_queries(ref):
        def one(h, _):
            cols = pl.ds(pl.multiple_of(h * HD, HD), HD)
            u = ref[:, cols].astype(jnp.float32)
            ref[:, cols] = rope(u, cos_ref[...], sin_ref[...]).astype(jnp.bfloat16)
            return 0
        lax.fori_loop(0, width // HD, one, 0)

    rope_queries(qs)

    def hid_arrive(to):
        hid_local(to).wait()
        dst = xs if to == 0 else xin
        for step in range(1, sections):
            j = lax.rem(to + step, sections)
            pltpu.make_async_remote_copy(
                src_ref=hid.at[0], dst_ref=dst.at[pl.ds(j * part, part)],
                send_sem=hid_send.at[to], recv_sem=hid_recv.at[j],
                device_id={"section": to}, device_id_type=MESH,
            ).wait_recv()

    block = 16

    def norm():
        def one(r, _):
            at = pl.ds(pl.multiple_of(r * block, block), block)
            x = xs[at, :].astype(jnp.float32)
            mean_square = jnp.mean(x * x, axis=-1, keepdims=True)
            y = (x * lax.rsqrt(mean_square + EPS) * gain[...]).astype(jnp.bfloat16)
            for pair in range(n // 2):
                normed[pair, at, :] = y[:, pair * 2 * depth:(pair + 1) * 2 * depth]
            return 0
        lax.fori_loop(0, rows // block, one, 0)

    def project(pair):
        a = normed[pair]
        for half in range(2):
            b = w[pl.ds(pair * 2, 2), half].reshape(2 * depth, kvw)
            acc[half] += jnp.dot(a, b, preferred_element_type=jnp.float32)

    acc[...] = jnp.zeros_like(acc)

    def arrive(which, origin, ways):
        w_copy(which, 4, origin).wait_recv()
        for way in ways:
            w_start(which, way, origin)

    def relay(which, origin, ways):
        arrive(which, origin, ways)

    def from_other(which, origin, ways):
        arrive(which, origin, ())

    def project_pair(which, origin, ways):
        if which == tail - 1:
            project(origin // 2)

    def sides(t, act):
        for sign, way in ((-1, 1), (1, 0)):
            far = o - t if sign < 0 else o + t
            there = (far >= 0) if sign < 0 else ((far < outer) & (t > 0))
            act(far, there, way)

    def around(there, act):
        for d in range(1, inner):
            pl.when(there & (i - d >= 0))(lambda d=d: act(i - d, 3))
            pl.when(there & (i + d < inner))(lambda d=d: act(i + d, 2))

    def along_outer(t, c, receive):
        for which in mains:
            def act(far, there, way, which=which):
                pl.when(there)(lambda: receive(which, index(far, i, c), (way, 2, 3, 4)))
            sides(t, act)

        def act_tail(far, there, way):
            pl.when(there)(lambda: receive(tail, index(far, i, c), (way, 4)))
            around(there, lambda ii, _: receive(tail, index(far, ii, c), (way, 4)))
        sides(t, act_tail)

    def along_inner(t, c, receive):
        for which in mains:
            def act(far, there, _, which=which):
                around(there, lambda ii, way: receive(which, index(far, ii, c), (way, 4)))
            sides(t, act)

    def first_inner(c, receive):
        around(o >= 0, lambda ii, way: receive(tail, index(o, ii, c), (way, 0, 1, 4)))

    first_inner(core, relay)

    def step(t, _):
        along_outer(t + 1, core, relay)

        @pl.when((t == 0) & (s == 0))
        def _():
            hid_arrive(0)
            norm()

        @pl.when(t == 0)
        def _():
            for which in (*mains, tail):
                arrive(which, index(o, i, 1 - core), ())
            first_inner(1 - core, from_other)

        along_inner(t, core, relay)
        along_outer(t + 1, 1 - core, from_other)
        along_inner(t, 1 - core, from_other)

        @pl.when(s == 0)
        def _():
            pl.when(t == 0)(lambda: project(chip))
            along_outer(t + 1, core, project_pair)
            along_inner(t, core, project_pair)

        return 0

    lax.fori_loop(0, outer, step, 0)

    row = lax.broadcasted_iota(jnp.int32, (rows, rows), 0)
    col = lax.broadcasted_iota(jnp.int32, (rows, rows), 1)
    scale = math.log2(math.e) / math.sqrt(HD)

    def attend(q_ref, kv_ref, x_ref, o_write, ready):
        ones = jnp.ones((rows, HD), jnp.bfloat16)
        allowed = (col <= row)[None]

        def one(g, _):
            ready(g)
            k = kv_ref[g, 0]
            v = jnp.concatenate([kv_ref[g, 1], ones], axis=1)
            base = g * group * HD
            cols = [pl.ds(pl.multiple_of(base + h * HD, HD), HD) for h in range(group)]
            q = jnp.concatenate([q_ref[:, c] for c in cols], axis=0)
            scores = lax.dot_general(q, k, (((1,), (1,)), ((), ())), preferred_element_type=jnp.float32)
            scores = jnp.where(allowed, scores.reshape(group, rows, rows), -1e30)
            top = jnp.max(scores, axis=-1, keepdims=True)
            p = jnp.exp2((scores - top) * scale).astype(jnp.bfloat16).reshape(group * rows, rows)
            mixed = jnp.dot(p, v, preferred_element_type=jnp.float32)
            mixed = mixed[:, :HD] / mixed[:, HD:]
            for h in range(group):
                o_write(cols[h], (
                    x_ref[:, cols[h]].astype(jnp.float32) + mixed[h * rows:(h + 1) * rows]
                ).astype(jnp.bfloat16))
            return 0

        lax.fori_loop(0, kv_heads, one, 0)

    def write_xs(c, value):
        xs[:, c] = value

    def write_out(c, value):
        out[0, 0, :, c] = value

    @pl.when(s > 0)
    def _():
        q_copy.wait_recv()
        rope_queries(qp)
        pl.when(s == 1)(lambda: hid_arrive(1))
        if sections > 2:
            pl.when(s > 1)(lambda: x_copy.wait_recv())
        attend(qp, kvp, xin, write_xs, lambda g: kv_copy(g).wait_recv())
        if sections > 2:
            pl.when(jnp.logical_not(last))(lambda: x_copy.start())
        norm()
        def one(j, _):
            project(j)
            return 0
        lax.fori_loop(0, n // 2, one, 0)

    for h in range(kv_heads):
        at = slice(h * HD, (h + 1) * HD)
        kv[h, 0] = rope(acc[0, :, at], cos_ref[...], sin_ref[...]).astype(jnp.bfloat16)
        kv[h, 1] = acc[1, :, at].astype(jnp.bfloat16)
        pl.when(jnp.logical_not(last))(lambda h=h: kv_copy(h).start())
    attend(qs, kv, xs, write_out, lambda g: None)

    def drain(which, origin, ways):
        for way in ways:
            cond = targets[way][0]
            if cond is None:
                w_copy(which, way, origin).wait_send()
            else:
                pl.when(cond)(lambda way=way: w_copy(which, way, origin).wait_send())

    for which in (*mains, tail):
        drain(which, f, range(5))
    first_inner(core, drain)

    def drain_step(t, _):
        along_outer(t + 1, core, drain)
        along_inner(t, core, drain)
        return 0

    lax.fori_loop(0, outer, drain_step, 0)
    for to in range(min(2, sections)):
        pl.when(s != to)(lambda to=to: hid_copy(to).wait_send())

    @pl.when(jnp.logical_not(last))
    def _():
        q_copy.wait_send()
        for h in range(kv_heads):
            kv_copy(h).wait_send()
        if sections > 2:
            pl.when(s > 0)(lambda: x_copy.wait_send())


ORDER = (
    "OM000", "OM001", "OM110", "OT00", "OU00", "OT11", "OM111", "*Q", "OM010", "OM011", "OT01", "OU01",
    "ZM000", "ZM001", "F00", "OM101", "ZM011", "ZM010", "ZM021", "ZM020", "ZT00", "*X", "Y010", "Y011",
    "ZT01", "OM100", "Y020", "*q", "Y001", "Y031", "OT10", "Y000", "Y021", "*R0", "ZT02", "Y030", "*P",
    "ZM101", "ZM100", "*A0", "OU11", "ZM110", "ZM111", "OU10", "F10", "*R1", "*A1", "*D", "ZM120", "*C",
    "Y101", "Y100", "ZM121", "ZT10", "ZT11", "*M", "Y110", "Y120", "Y130", "*S", "Y111", "Y121", "Y131", "*N",
    "*L", "*T", "ZT12",
)


def pair_kernel(
    n, outer, inner,
    hid, q_in, kw, vw, gain_in, cos_in, sin_in,
    out,
    w, stage, xs, x1, xb, xr, q0, q1, acc, give, take, kv0, kv1, gains, ssq, cos_ref, sin_ref,
    w_recv, w_send, stage_send, own_sem, load_sem, gain_sem, hid_sem, hid_own,
    q_sem, x1_sem, kv_sem, swap0_sem, swap_sem, part_sem,
):
    side = lax.axis_index("section")
    f = lax.axis_index("fsdp")
    mate = {"section": 1 - side}
    core = lax.rem(f, 2)
    chip = f // 2
    i = lax.rem(chip, inner)
    o = chip // inner
    twin = {"fsdp": 2 * chip + 1 - core}
    rows, width = xs.shape
    part = hid.shape[1]
    kvw = kw.shape[2]
    kv_heads = kvw // HD
    heads = kv_heads // 2
    group = width // kvw
    gw = group * HD
    depth = kw.shape[1]
    chips = n // 2
    blk = width // chips
    half = width // 2
    pieces = half // blk
    per_group = gw // blk

    local = []
    for hh in range(heads):
        for to_mate in (False, True):
            head = (1 - side if to_mate else side) * heads + hh
            cols = pl.ds(pl.multiple_of(head * HD, HD), HD)
            at = pl.ds(hh * depth, depth)
            for kind, src in enumerate((kw, vw)):
                lanes = pl.ds(kind * HD, HD)
                dst = stage.at[at, lanes] if to_mate else w.at[side, chip, at, lanes]
                local.append(pltpu.make_async_copy(src.at[0, :, cols], dst, own_sem.at[len(local)]))
    for copy in local:
        copy.start()
    loads = [
        pltpu.make_async_copy(src, dst, load_sem.at[at])
        for at, (src, dst) in enumerate(
            ((gain_in, gains.at[side]), (cos_in, cos_ref), (sin_in, sin_ref)))
    ]
    for load in loads:
        load.start()

    def q_local(which):
        if which == 0:
            return pltpu.make_async_copy(q_in.at[0, 0, :, pl.ds(0, half)], q0, load_sem.at[3])
        return pltpu.make_async_copy(q_in.at[0, 0], q1, load_sem.at[3])

    for which in range(2):
        pl.when(side == which)(lambda which=which: q_local(which).start())

    def index(oo, ii):
        return (oo * inner + ii) * 2 + core

    targets = (
        (o > 0, index(o - 1, i)),
        (o < outer - 1, index(o + 1, i)),
        (i > 0, index(o, i - 1)),
        (i < inner - 1, index(o, i + 1)),
    )

    barrier = pltpu.get_barrier_semaphore()
    for cond, target in targets:
        pl.when(cond)(lambda target=target: pl.semaphore_signal(
            barrier, inc=1, device_id={"fsdp": target}, device_id_type=MESH))
    for device in (twin, mate):
        pl.semaphore_signal(barrier, inc=1, device_id=device, device_id_type=MESH)
    expected = (
        jnp.where(o > 0, 1, 0) + jnp.where(o < outer - 1, 1, 0)
        + jnp.where(i > 0, 1, 0) + jnp.where(i < inner - 1, 1, 0) + 2
    )
    pl.semaphore_wait(barrier, expected)

    deep = heads * depth
    few = max(16, (deep * 96 // 512 + 8) // 16 * 16)
    early = (heads - 1) * depth
    cuts = [
        (pl.ds(0, at), pl.ds(at, deep - few - at), pl.ds(deep - few, few))
        for at in (deep * 160 // 512 // 16 * 16, early)
    ]
    tail = 2

    def w_copy(layer, which, way, origin):
        piece = w.at[layer, origin, cuts[layer][which]]
        return pltpu.make_async_remote_copy(
            src_ref=piece, dst_ref=piece,
            send_sem=w_send.at[layer, which, way, origin], recv_sem=w_recv.at[layer, which, origin],
            device_id={"fsdp": targets[way][1]}, device_id_type=MESH,
        )

    def w_start(layer, which, way, origin):
        pl.when(targets[way][0])(lambda: w_copy(layer, which, way, origin).start())

    def stage_copy(layer, which):
        return pltpu.make_async_remote_copy(
            src_ref=stage.at[cuts[layer][which]], dst_ref=w.at[layer, chip, cuts[layer][which]],
            send_sem=stage_send.at[which], recv_sem=w_recv.at[layer, which, chip],
            device_id=mate, device_id_type=MESH,
        )

    def gain_copy(layer):
        return pltpu.make_async_remote_copy(
            src_ref=gain_in, dst_ref=gains.at[layer], send_sem=gain_sem.at[0], recv_sem=gain_sem.at[1],
            device_id=mate, device_id_type=MESH,
        )

    def hid_copy(of):
        return pltpu.make_async_remote_copy(
            src_ref=hid.at[0], dst_ref=xs.at[pl.ds(pl.multiple_of(of * part, part), part)],
            send_sem=hid_sem.at[0], recv_sem=hid_sem.at[1], device_id=mate, device_id_type=MESH,
        )

    hid_local = pltpu.make_async_copy(
        hid.at[0], xs.at[pl.ds(pl.multiple_of(side * part, part), part)], hid_own)

    def q_copy(g):
        return pltpu.make_async_remote_copy(
            src_ref=q_in.at[0, 0, :, pl.ds(half + g * gw, gw)], dst_ref=q0.at[:, pl.ds(g * gw, gw)],
            send_sem=q_sem.at[0, g], recv_sem=q_sem.at[1, g], device_id=mate, device_id_type=MESH,
        )

    def x1_copy(of, b):
        cols = pl.ds(pl.multiple_of(of * half + b * blk, blk), blk)
        return pltpu.make_async_remote_copy(
            src_ref=x1.at[:, cols], dst_ref=x1.at[:, cols],
            send_sem=x1_sem.at[0, b], recv_sem=x1_sem.at[1, b], device_id=mate, device_id_type=MESH,
        )

    def kv_copy(hh, kind):
        return pltpu.make_async_remote_copy(
            src_ref=kv1.at[hh, kind], dst_ref=kv1.at[hh, kind],
            send_sem=kv_sem.at[0, hh, kind], recv_sem=kv_sem.at[1, hh, kind], device_id=mate, device_id_type=MESH,
        )

    swap0 = pltpu.make_async_remote_copy(
        src_ref=xb.at[0, 1 - core], dst_ref=xr.at[0], send_sem=swap0_sem.at[0], recv_sem=swap0_sem.at[1],
        device_id=twin, device_id_type=MESH,
    )

    def swap_copy(c):
        cols = pl.ds(pl.multiple_of(c * depth, depth), depth)
        return pltpu.make_async_remote_copy(
            src_ref=xb.at[1, 1 - core, :, cols], dst_ref=xr.at[1, :, cols],
            send_sem=swap_sem.at[0, c], recv_sem=swap_sem.at[1, c], device_id=twin, device_id_type=MESH,
        )

    def part_copy(layer, hh):
        return pltpu.make_async_remote_copy(
            src_ref=give.at[layer, hh], dst_ref=take.at[layer, hh],
            send_sem=part_sem.at[0, layer, hh], recv_sem=part_sem.at[1, layer, hh],
            device_id=twin, device_id_type=MESH,
        )

    for copy in local:
        copy.wait()

    for layer in range(2):
        @pl.when(side == layer)
        def _(layer=layer):
            for which in range(3):
                stage_copy(layer, which).start()
    gain_copy(side).start()
    hid_copy(side).start()
    hid_local.start()

    @pl.when(side == 0)
    def _():
        for g in range(heads):
            q_copy(g).start()

    def rope_queries(ref, first, count):
        together = math.gcd(count, 4)

        def one(at, _):
            cosine, sine = cos_ref[...], sin_ref[...]
            for h in range(together):
                cols = pl.ds(pl.multiple_of((first + at * together + h) * HD, HD), HD)
                u = ref[:, cols].astype(jnp.float32)
                ref[:, cols] = rope(u, cosine, sine).astype(jnp.bfloat16)
            return 0
        lax.fori_loop(0, count // together, one, 0)

    def relay(layer, which, origin, ways):
        w_copy(layer, which, 0, origin).wait_recv()
        for way in ways:
            w_start(layer, which, way, origin)

    def drain(layer, which, origin, ways):
        for way in ways:
            pl.when(targets[way][0])(lambda way=way: w_copy(layer, which, way, origin).wait_send())

    def sides(t, act):
        if t == 0:
            act(o, None, 0)
        else:
            act(o - t, o - t >= 0, 1)
            act(o + t, o + t < outer, 0)

    def around(there, act):
        for d in range(1, inner):
            for cond, ii, way in ((i - d >= 0, i - d, 3), (i + d < inner, i + d, 2)):
                pl.when(cond if there is None else there & cond)(lambda ii=ii, way=way: act(ii, way))

    def own(kind, layer, on, which, receive):
        ways = {"OM": (0, 1, 2, 3), "OT": (2, 3), "OU": (0, 1)}[kind]

        @pl.when(side == on)
        def _():
            if receive is relay:
                if on != layer and kind != "OU":
                    w_copy(layer, which, 0, chip).wait_recv()
                for way in ways:
                    w_start(layer, which, way, chip)
            else:
                drain(layer, which, chip, ways)

    def far(t, act):
        sides(t, lambda oo, there, way: pl.when(there)(lambda: act(oo, way)))

    def move(kind, layer, t, which, receive):
        if kind[0] == "O":
            own(kind, layer, t, tail if which is None else which, receive)
        elif kind == "F":
            around(None, lambda ii, way: receive(layer, tail, o * inner + ii, (way, 0, 1)))
        elif kind == "ZM":
            far(t + 1, lambda oo, way: receive(layer, which, oo * inner + i, (way, 2, 3)))
        elif kind == "ZT":
            def both(oo, there, way):
                pl.when(there)(lambda: receive(layer, tail, oo * inner + i, (way,)))
                around(there, lambda ii, _: receive(layer, tail, oo * inner + ii, (way,)))
            sides(t + 1, both)
        elif kind == "Y":
            sides(t, lambda oo, there, _: around(
                there, lambda ii, way: receive(layer, which, oo * inner + ii, (way,))))

    row = lax.broadcasted_iota(jnp.int32, (rows, rows), 0)
    col = lax.broadcasted_iota(jnp.int32, (rows, rows), 1)
    scale = math.log2(math.e) / math.sqrt(HD)

    def scaled(src, c, layer):
        cols = pl.ds(pl.multiple_of(c * blk, blk), blk)
        x = src[:, cols].astype(jnp.float32)
        y = (x * gains[layer, :, cols]).astype(jnp.bfloat16)
        for kind in range(2):
            xb[layer, kind, :, pl.ds(pl.multiple_of(c * depth, depth), depth)] = y[:, kind * depth:(kind + 1) * depth]
        square = x * x
        total = square[:, :HD]
        for at in range(1, blk // HD):
            total += square[:, at * HD:(at + 1) * HD]
        ssq[layer] += total

    def project(layer, hh, first, count, fresh):
        cols = pl.ds(pl.multiple_of(first * depth, depth), count * depth)
        a = jnp.concatenate([xb[layer, core, :, cols], xr[layer, :, cols]], axis=0)
        b = w[layer, pl.ds(first, count), hh * depth:(hh + 1) * depth].reshape(count * depth, 2 * HD)
        y = jnp.dot(a, b, preferred_element_type=jnp.float32)
        if fresh:
            acc[layer, hh] = y[:rows]
            give[layer, hh] = y[rows:]
        else:
            acc[layer, hh] += y[:rows]
            give[layer, hh] += y[rows:]

    def finish(layer, hh, ref, at, then=None):
        part_copy(layer, hh).wait_recv()
        r = lax.rsqrt(jnp.sum(ssq[layer], axis=-1, keepdims=True) / width + EPS)
        y = (acc[layer, hh] + take[layer, hh]) * r
        ref[at, 0] = rope(y[:, :HD], cos_ref[...], sin_ref[...]).astype(jnp.bfloat16)
        if then is not None:
            then(0)
        ref[at, 1] = y[:, HD:].astype(jnp.bfloat16)
        if then is not None:
            then(1)

    def attend(q_ref, q_first, kv_ref, head, x_ref, x_first, write, ready=None):
        if ready is not None:
            ready(0)
        k = kv_ref[head, 0]
        allowed = (col <= row)[None]
        batch = group // 4
        probs = []
        for first in range(0, group, batch):
            q = jnp.concatenate(
                [q_ref[:, pl.ds(pl.multiple_of(q_first + (first + h) * HD, HD), HD)] for h in range(batch)], axis=0)
            scores = lax.dot_general(q, k, (((1,), (1,)), ((), ())), preferred_element_type=jnp.float32)
            scores = jnp.where(allowed, scores.reshape(batch, rows, rows), -1e30)
            top = jnp.max(scores, axis=-1, keepdims=True)
            probs.append(jnp.exp2((scores - top) * scale).astype(jnp.bfloat16).reshape(batch * rows, rows))
        if ready is not None:
            ready(1)
        v = jnp.concatenate([kv_ref[head, 1], jnp.ones((rows, HD), jnp.bfloat16)], axis=1)
        for first, p in zip(range(0, group, batch), probs):
            mixed = jnp.dot(p, v, preferred_element_type=jnp.float32)
            mixed = mixed[:, :HD] / mixed[:, HD:]
            for h in range(batch):
                cols = pl.ds(pl.multiple_of(x_first + (first + h) * HD, HD), HD)
                write(cols, (
                    x_ref[:, cols].astype(jnp.float32) + mixed[h * rows:(h + 1) * rows]
                ).astype(jnp.bfloat16))

    def write_x1(cols, value):
        x1[:, cols] = value

    def write_out(cols, value):
        out[0, 0, :, cols] = value

    def queries_in():
        for load in loads:
            load.wait()

        @pl.when(side == 1)
        def _():
            q_local(1).wait()
            rope_queries(q1, 0, width // HD)

        ssq[...] = jnp.zeros_like(ssq)

    def queries_mine():
        @pl.when(side == 0)
        def _():
            q_local(0).wait()
            rope_queries(q0, 0, half // HD)

    def inputs_in():
        hid_local.wait()
        hid_copy(1 - side).wait_recv()
        gain_copy(1 - side).wait_recv()

        def one(c, _):
            scaled(xs, c, 0)
            return 0
        lax.fori_loop(0, chips, one, 0)
        swap0.start()

    def first_layer():
        swap0.wait_recv()
        for hh in range(heads):
            project(0, hh, 0, chips, True)
            part_copy(0, hh).start()

    def queries_arrive(g):
        @pl.when(side == 1)
        def _():
            q_copy(g).wait_recv()
            rope_queries(q0, g * group, group)

    def first_attention(g):
        finish(0, g, kv0, g)
        attend(q0, g * gw, kv0, g, xs, side * half + g * gw, write_x1)

        def one(b, _):
            x1_copy(side, b).start()
            scaled(x1, side * pieces + b, 1)
            swap_copy(side * pieces + b).start()
            return 0
        lax.fori_loop(g * per_group, (g + 1) * per_group, one, 0)

    def mate_in():
        def one(b, _):
            c = (1 - side) * pieces + b
            x1_copy(1 - side, b).wait_recv()
            scaled(x1, c, 1)
            swap_copy(c).start()
            return 0
        lax.fori_loop(0, pieces, one, 0)

    def swapped(of):
        def one(b, _):
            swap_copy(of * pieces + b).wait_recv()
            return 0
        lax.fori_loop(0, pieces, one, 0)

    def second_layer(hh, first, count, fresh, send=True):
        project(1, hh, first, count, fresh)
        if send:
            part_copy(1, hh).start()

    def second_done(hh, then=None):
        finish(1, hh, kv1, side * heads + hh, then)

    def send_done(hh):
        @pl.when(side == 0)
        def _():
            second_done(hh, lambda kind: kv_copy(hh, kind).start())

    def first_side_in():
        @pl.when(side == 0)
        def _():
            mate_in()
            out[0, 0] = x1[...]
            swapped(1)
        swapped(side)

    def second_side_in():
        @pl.when(side == 1)
        def _():
            mate_in()
            swapped(0)

    def early_heads():
        for hh in range(heads - 1):
            pl.when(side == 0)(lambda hh=hh: second_layer(hh, 0, chips, True))
            pl.when(side == 1)(lambda hh=hh: second_layer(hh, side * pieces, pieces, True, send=False))

    def settle_first():
        for layer in range(2):
            @pl.when(side == layer)
            def _(layer=layer):
                for which in range(3):
                    stage_copy(layer, which).wait_send()
        gain_copy(side).wait_send()
        hid_copy(side).wait_send()
        swap0.wait_send()
        for hh in range(heads):
            part_copy(0, hh).wait_send()

    def drain_moves(layers):
        for step in [step for step in moves if step[1] in layers]:
            moves.remove(step)
            move(*step, drain)

    moves = []
    for word in ORDER:
        if word[0] == "*":
            if word == "*Q":
                queries_in()
            elif word == "*q":
                queries_mine()
            elif word == "*X":
                inputs_in()
            elif word == "*P":
                first_layer()
            elif word[1] == "A":
                first_attention(int(word[2]))
            elif word[1] in "ab":
                pl.when(side == "ba".index(word[1]))(lambda g=int(word[2]): first_attention(g))
            elif word == "*L":
                second_layer(heads - 1, jnp.where(o < outer // 2, 0, inner), chips - inner, True, send=False)
            elif word == "*N":
                second_side_in()
            elif word == "*C":
                settle_first()
            elif word == "*D":
                drain_moves((0,))
            elif word[1] == "R":
                queries_arrive(int(word[2]))
            elif word == "*M":
                first_side_in()
            elif word == "*S":
                early_heads()
            elif word == "*T":
                for hh in range(heads - 1):
                    send_done(hh)
        else:
            kind = word.rstrip("0123456789")
            digits = [int(d) for d in word[len(kind):]]
            step = (kind, digits[0], digits[1], digits[2] if len(digits) > 2 else None)
            moves.append(step)
            move(*step, relay)

    @pl.when(side == 1)
    def _():
        for hh in range(heads - 1):
            second_layer(hh, (1 - side) * pieces, pieces, False)
    second_layer(heads - 1, jnp.where(o < outer // 2, (outer - 1) * inner, 0), inner, False)
    send_done(heads - 1)

    @pl.when(side == 1)
    def _():
        for hh in range(heads - 1):
            second_done(hh)

        def one(g, _):
            pl.when(g == heads - 1)(lambda: second_done(heads - 1))
            attend(q1, (heads + g) * gw, kv1, heads + g, x1, (heads + g) * gw, write_out)
            return 0
        lax.fori_loop(0, heads, one, 0)

    drain_moves((0, 1))
    for c in range(chips):
        swap_copy(c).wait_send()
    for hh in range(heads):
        part_copy(1, hh).wait_send()
    for b in range(pieces):
        x1_copy(side, b).wait_send()

    @pl.when(side == 0)
    def _():
        for g in range(heads):
            q_copy(g).wait_send()
        for hh in range(heads):
            for kind in range(2):
                kv_copy(hh, kind).wait_send()

    @pl.when(side == 1)
    def _():
        def one(g, _):
            attend(q1, g * gw, kv1, g, x1, g * gw, write_out, lambda kind: kv_copy(g, kind).wait_recv())
            return 0
        lax.fori_loop(0, heads, one, 0)


def solution(mesh):
    sections, n = mesh.shape["section"], mesh.shape["fsdp"]
    chips = n // 2
    outer = 4 if chips % 4 == 0 else 1
    inner = chips // outer

    def body(hidden_in, queries, key_weight, value_weight, norm_gain):
        rows, width = queries.shape[2:]
        depth, kvw = key_weight.shape[1:]
        cosine, sine = rope_tables(rows)
        hbm = pl.BlockSpec(memory_space=pltpu.HBM)
        vmem = pl.BlockSpec(memory_space=pltpu.VMEM)
        dma = pltpu.SemaphoreType.DMA
        bf16, f32 = jnp.bfloat16, jnp.float32
        if sections == 2 and outer == 4 and depth % HD == 0:
            heads = kvw // HD // 2
            pieces = chips // 2
            run = functools.partial(pair_kernel, n, outer, inner)
            scratch = [
                pltpu.VMEM((2, chips, heads * depth, 2 * HD), bf16),
                pltpu.VMEM((heads * depth, 2 * HD), bf16),
                pltpu.VMEM((rows, width), bf16),
                pltpu.VMEM((rows, width), bf16),
                pltpu.VMEM((2, 2, rows, width // 2), bf16),
                pltpu.VMEM((2, rows, width // 2), bf16),
                pltpu.VMEM((rows, width // 2), bf16),
                pltpu.VMEM((rows, width), bf16),
                pltpu.VMEM((2, heads, rows, 2 * HD), f32),
                pltpu.VMEM((2, heads, rows, 2 * HD), f32),
                pltpu.VMEM((2, heads, rows, 2 * HD), f32),
                pltpu.VMEM((heads, 2, rows, HD), bf16),
                pltpu.VMEM((2 * heads, 2, rows, HD), bf16),
                pltpu.VMEM((2, 1, width), f32),
                pltpu.VMEM((2, rows, HD), f32),
                pltpu.VMEM((rows, HD), f32),
                pltpu.VMEM((rows, HD), f32),
                dma((2, 3, chips)), dma((2, 3, 4, chips)), dma((3,)), dma((4 * heads,)),
                dma((4,)), dma((2,)), dma((2,)), dma,
                dma((2, heads)), dma((2, pieces)), dma((2, heads, 2)), dma((2,)), dma((2, chips)), dma((2, 2, heads)),
            ]
        else:
            run = functools.partial(chain_kernel, n, sections, outer, inner)
            scratch = [
                pltpu.VMEM((n, 2, depth, kvw), bf16),
                pltpu.VMEM((rows, width), bf16),
                pltpu.VMEM((rows, width), bf16),
                pltpu.VMEM((rows, width), bf16),
                pltpu.VMEM((rows, width), bf16),
                pltpu.VMEM((n // 2, rows, 2 * depth), bf16),
                pltpu.VMEM((2, rows, kvw), f32),
                pltpu.VMEM((kvw // HD, 2, rows, HD), bf16),
                pltpu.VMEM((kvw // HD, 2, rows, HD), bf16),
                pltpu.VMEM((1, width), f32),
                pltpu.VMEM((rows, HD), f32),
                pltpu.VMEM((rows, HD), f32),
                dma((3, n)), dma((3, 5, n)), dma((2,)), dma((sections,)), dma((2,)), dma,
                dma((2,)), dma((2, kvw // HD)), dma((2,)), dma((4,)),
            ]
        return pl.pallas_call(
            run,
            out_shape=jax.ShapeDtypeStruct(queries.shape, bf16),
            in_specs=[hbm] * 7,
            out_specs=vmem,
            scratch_shapes=scratch,
            compiler_params=pltpu.CompilerParams(
                collective_id=0, has_side_effects=True, vmem_limit_bytes=28 * 2**20
            ),
        )(*(
            pltpu.with_memory_space_constraint(x, pltpu.HBM)
            for x in (hidden_in, queries, key_weight, value_weight, norm_gain, jnp.asarray(cosine), jnp.asarray(sine))
        ))

    placed = (
        P("fsdp", "section", None),
        P("section", "fsdp", None, None),
        P("section", "fsdp", None),
        P("section", "fsdp", None),
        P("section", None),
    )
    return jax.shard_map(
        body, mesh=mesh, in_specs=placed, out_specs=P("section", "fsdp", None, None), check_vma=False
    )
```

```python
import functools
import math

import jax
import jax.numpy as jnp
import numpy as np
from jax import lax
from jax.experimental import pallas as pl
from jax.experimental.pallas import tpu as pltpu
from jax.sharding import PartitionSpec as P

HD = 128
EPS = 1e-05
MESH = pl.DeviceIdType.MESH


def rope_tables(rows):
    half = HD // 2
    frequency = np.exp(np.arange(half, dtype=np.float32) * np.float32(-2.0 * math.log(10000.0) / HD))
    angles = np.arange(rows, dtype=np.float32)[:, None] * frequency[None, :].astype(np.float32)
    cosine, sine = np.cos(angles), np.sin(angles)
    return (
        np.concatenate([cosine, cosine], 1).astype(np.float32),
        np.concatenate([-sine, sine], 1).astype(np.float32),
    )


def rope(u, cosine, sine):
    return u * cosine + pltpu.roll(u, HD // 2, 1) * sine


def chain_kernel(
    n, sections, outer, inner,
    hid, q_in, kw, vw, gain_in, cos_in, sin_in,
    out,
    w, xin, xs, qs, qp, normed, acc, kv, kvp, gain, cos_ref, sin_ref,
    w_recv, w_send, own_sem, hid_recv, hid_send, hid_own, q_sem, kv_sem, x_sem, load_sem,
):
    s = lax.axis_index("section")
    f = lax.axis_index("fsdp")
    core = lax.rem(f, 2)
    chip = f // 2
    i = lax.rem(chip, inner)
    o = chip // inner
    rows, width = xs.shape
    part = hid.shape[1]
    kvw = kw.shape[2]
    kv_heads = kvw // HD
    group = width // kvw
    depth = kw.shape[1]

    def index(oo, ii, cc):
        return (oo * inner + ii) * 2 + cc

    own_k = pltpu.make_async_copy(kw.at[0], w.at[f, 0], own_sem.at[0])
    own_v = pltpu.make_async_copy(vw.at[0], w.at[f, 1], own_sem.at[1])
    own_k.start()
    own_v.start()
    loads = [
        pltpu.make_async_copy(src, dst, load_sem.at[at])
        for at, (src, dst) in enumerate(
            ((q_in.at[0, 0], qs), (gain_in, gain), (cos_in, cos_ref), (sin_in, sin_ref)))
    ]
    for load in loads:
        load.start()

    targets = (
        (o > 0, index(o - 1, i, core)),
        (o < outer - 1, index(o + 1, i, core)),
        (i > 0, index(o, i - 1, core)),
        (i < inner - 1, index(o, i + 1, core)),
        (None, index(o, i, 1 - core)),
    )

    barrier = pltpu.get_barrier_semaphore()
    for cond, target in targets:
        def greet(target=target):
            pl.semaphore_signal(barrier, inc=1, device_id={"fsdp": target}, device_id_type=MESH)
        if cond is None:
            greet()
        else:
            pl.when(cond)(greet)
    for step in range(1, sections):
        pl.semaphore_signal(
            barrier, inc=1, device_id={"section": lax.rem(s + step, sections)}, device_id_type=MESH
        )
    expected = (
        jnp.where(o > 0, 1, 0) + jnp.where(o < outer - 1, 1, 0)
        + jnp.where(i > 0, 1, 0) + jnp.where(i < inner - 1, 1, 0) + sections
    )
    pl.semaphore_wait(barrier, expected)

    few = max(16, depth // 8)
    first = (depth - few + 16) // 32 * 16
    cuts = (pl.ds(0, first), pl.ds(first, depth - few - first), pl.ds(depth - few, few))
    mains, tail = (0, 1), 2

    def w_copy(which, way, origin):
        piece = w.at[origin, :, cuts[which]]
        return pltpu.make_async_remote_copy(
            src_ref=piece, dst_ref=piece,
            send_sem=w_send.at[which, way, origin], recv_sem=w_recv.at[which, origin],
            device_id={"fsdp": targets[way][1]}, device_id_type=MESH,
        )

    def w_start(which, way, origin):
        cond = targets[way][0]
        if cond is None:
            w_copy(which, way, origin).start()
        else:
            pl.when(cond)(lambda: w_copy(which, way, origin).start())

    own_k.wait()
    own_v.wait()
    for way in (2, 3):
        w_start(tail, way, f)
    for which in mains:
        for way in range(5):
            w_start(which, way, f)
    for way in (0, 1, 4):
        w_start(tail, way, f)

    mine = pl.ds(pl.multiple_of(s * part, part), part)

    def hid_copy(to):
        dst = xs if to == 0 else xin
        return pltpu.make_async_remote_copy(
            src_ref=hid.at[0], dst_ref=dst.at[mine], send_sem=hid_send.at[to],
            recv_sem=hid_recv.at[s], device_id={"section": to}, device_id_type=MESH,
        )

    def hid_local(to):
        dst = xs if to == 0 else xin
        return pltpu.make_async_copy(hid.at[0], dst.at[mine], hid_own)

    for to in range(min(2, sections)):
        pl.when(s != to)(lambda to=to: hid_copy(to).start())
        pl.when(s == to)(lambda to=to: hid_local(to).start())

    q_copy = pltpu.make_async_remote_copy(
        src_ref=q_in.at[0, 0], dst_ref=qp, send_sem=q_sem.at[0], recv_sem=q_sem.at[1],
        device_id={"section": jnp.minimum(s + 1, sections - 1)}, device_id_type=MESH,
    )
    def kv_copy(g):
        return pltpu.make_async_remote_copy(
            src_ref=kv.at[g], dst_ref=kvp.at[g], send_sem=kv_sem.at[0, g], recv_sem=kv_sem.at[1, g],
            device_id={"section": jnp.minimum(s + 1, sections - 1)}, device_id_type=MESH,
        )

    x_copy = pltpu.make_async_remote_copy(
        src_ref=xs, dst_ref=xin, send_sem=x_sem.at[0], recv_sem=x_sem.at[1],
        device_id={"section": jnp.minimum(s + 1, sections - 1)}, device_id_type=MESH,
    )
    last = s == sections - 1
    pl.when(jnp.logical_not(last))(lambda: q_copy.start())

    for load in loads:
        load.wait()

    def rope_queries(ref):
        def one(h, _):
            cols = pl.ds(pl.multiple_of(h * HD, HD), HD)
            u = ref[:, cols].astype(jnp.float32)
            ref[:, cols] = rope(u, cos_ref[...], sin_ref[...]).astype(jnp.bfloat16)
            return 0
        lax.fori_loop(0, width // HD, one, 0)

    rope_queries(qs)

    def hid_arrive(to):
        hid_local(to).wait()
        dst = xs if to == 0 else xin
        for step in range(1, sections):
            j = lax.rem(to + step, sections)
            pltpu.make_async_remote_copy(
                src_ref=hid.at[0], dst_ref=dst.at[pl.ds(j * part, part)],
                send_sem=hid_send.at[to], recv_sem=hid_recv.at[j],
                device_id={"section": to}, device_id_type=MESH,
            ).wait_recv()

    block = 16

    def norm():
        def one(r, _):
            at = pl.ds(pl.multiple_of(r * block, block), block)
            x = xs[at, :].astype(jnp.float32)
            mean_square = jnp.mean(x * x, axis=-1, keepdims=True)
            y = (x * lax.rsqrt(mean_square + EPS) * gain[...]).astype(jnp.bfloat16)
            for pair in range(n // 2):
                normed[pair, at, :] = y[:, pair * 2 * depth:(pair + 1) * 2 * depth]
            return 0
        lax.fori_loop(0, rows // block, one, 0)

    def project(pair):
        a = normed[pair]
        for half in range(2):
            b = w[pl.ds(pair * 2, 2), half].reshape(2 * depth, kvw)
            acc[half] += jnp.dot(a, b, preferred_element_type=jnp.float32)

    acc[...] = jnp.zeros_like(acc)

    def arrive(which, origin, ways):
        w_copy(which, 4, origin).wait_recv()
        for way in ways:
            w_start(which, way, origin)

    def relay(which, origin, ways):
        arrive(which, origin, ways)

    def from_other(which, origin, ways):
        arrive(which, origin, ())

    def project_pair(which, origin, ways):
        if which == tail - 1:
            project(origin // 2)

    def sides(t, act):
        for sign, way in ((-1, 1), (1, 0)):
            far = o - t if sign < 0 else o + t
            there = (far >= 0) if sign < 0 else ((far < outer) & (t > 0))
            act(far, there, way)

    def around(there, act):
        for d in range(1, inner):
            pl.when(there & (i - d >= 0))(lambda d=d: act(i - d, 3))
            pl.when(there & (i + d < inner))(lambda d=d: act(i + d, 2))

    def along_outer(t, c, receive):
        for which in mains:
            def act(far, there, way, which=which):
                pl.when(there)(lambda: receive(which, index(far, i, c), (way, 2, 3, 4)))
            sides(t, act)

        def act_tail(far, there, way):
            pl.when(there)(lambda: receive(tail, index(far, i, c), (way, 4)))
            around(there, lambda ii, _: receive(tail, index(far, ii, c), (way, 4)))
        sides(t, act_tail)

    def along_inner(t, c, receive):
        for which in mains:
            def act(far, there, _, which=which):
                around(there, lambda ii, way: receive(which, index(far, ii, c), (way, 4)))
            sides(t, act)

    def first_inner(c, receive):
        around(o >= 0, lambda ii, way: receive(tail, index(o, ii, c), (way, 0, 1, 4)))

    first_inner(core, relay)

    def step(t, _):
        along_outer(t + 1, core, relay)

        @pl.when((t == 0) & (s == 0))
        def _():
            hid_arrive(0)
            norm()

        @pl.when(t == 0)
        def _():
            for which in (*mains, tail):
                arrive(which, index(o, i, 1 - core), ())
            first_inner(1 - core, from_other)

        along_inner(t, core, relay)
        along_outer(t + 1, 1 - core, from_other)
        along_inner(t, 1 - core, from_other)

        @pl.when(s == 0)
        def _():
            pl.when(t == 0)(lambda: project(chip))
            along_outer(t + 1, core, project_pair)
            along_inner(t, core, project_pair)

        return 0

    lax.fori_loop(0, outer, step, 0)

    row = lax.broadcasted_iota(jnp.int32, (rows, rows), 0)
    col = lax.broadcasted_iota(jnp.int32, (rows, rows), 1)
    scale = math.log2(math.e) / math.sqrt(HD)

    def attend(q_ref, kv_ref, x_ref, o_write, ready):
        ones = jnp.ones((rows, HD), jnp.bfloat16)
        allowed = (col <= row)[None]

        def one(g, _):
            ready(g)
            k = kv_ref[g, 0]
            v = jnp.concatenate([kv_ref[g, 1], ones], axis=1)
            base = g * group * HD
            cols = [pl.ds(pl.multiple_of(base + h * HD, HD), HD) for h in range(group)]
            q = jnp.concatenate([q_ref[:, c] for c in cols], axis=0)
            scores = lax.dot_general(q, k, (((1,), (1,)), ((), ())), preferred_element_type=jnp.float32)
            scores = jnp.where(allowed, scores.reshape(group, rows, rows), -1e30)
            top = jnp.max(scores, axis=-1, keepdims=True)
            p = jnp.exp2((scores - top) * scale).astype(jnp.bfloat16).reshape(group * rows, rows)
            mixed = jnp.dot(p, v, preferred_element_type=jnp.float32)
            mixed = mixed[:, :HD] / mixed[:, HD:]
            for h in range(group):
                o_write(cols[h], (
                    x_ref[:, cols[h]].astype(jnp.float32) + mixed[h * rows:(h + 1) * rows]
                ).astype(jnp.bfloat16))
            return 0

        lax.fori_loop(0, kv_heads, one, 0)

    def write_xs(c, value):
        xs[:, c] = value

    def write_out(c, value):
        out[0, 0, :, c] = value

    @pl.when(s > 0)
    def _():
        q_copy.wait_recv()
        rope_queries(qp)
        pl.when(s == 1)(lambda: hid_arrive(1))
        if sections > 2:
            pl.when(s > 1)(lambda: x_copy.wait_recv())
        attend(qp, kvp, xin, write_xs, lambda g: kv_copy(g).wait_recv())
        if sections > 2:
            pl.when(jnp.logical_not(last))(lambda: x_copy.start())
        norm()
        def one(j, _):
            project(j)
            return 0
        lax.fori_loop(0, n // 2, one, 0)

    for h in range(kv_heads):
        at = slice(h * HD, (h + 1) * HD)
        kv[h, 0] = rope(acc[0, :, at], cos_ref[...], sin_ref[...]).astype(jnp.bfloat16)
        kv[h, 1] = acc[1, :, at].astype(jnp.bfloat16)
        pl.when(jnp.logical_not(last))(lambda h=h: kv_copy(h).start())
    attend(qs, kv, xs, write_out, lambda g: None)

    def drain(which, origin, ways):
        for way in ways:
            cond = targets[way][0]
            if cond is None:
                w_copy(which, way, origin).wait_send()
            else:
                pl.when(cond)(lambda way=way: w_copy(which, way, origin).wait_send())

    for which in (*mains, tail):
        drain(which, f, range(5))
    first_inner(core, drain)

    def drain_step(t, _):
        along_outer(t + 1, core, drain)
        along_inner(t, core, drain)
        return 0

    lax.fori_loop(0, outer, drain_step, 0)
    for to in range(min(2, sections)):
        pl.when(s != to)(lambda to=to: hid_copy(to).wait_send())

    @pl.when(jnp.logical_not(last))
    def _():
        q_copy.wait_send()
        for h in range(kv_heads):
            kv_copy(h).wait_send()
        if sections > 2:
            pl.when(s > 0)(lambda: x_copy.wait_send())


ORDER = (
    "OM000", "OM001", "OM110", "OT00", "OU00", "OT11", "OM111", "*Q", "OM010", "OM011", "OT01", "OU01",
    "ZM000", "ZM001", "F00", "OM101", "ZM011", "ZM010", "ZM021", "ZM020", "ZT00", "*X", "Y010", "Y011",
    "ZT01", "OM100", "Y020", "*q", "Y001", "Y031", "OT10", "Y000", "Y021", "*R0", "ZT02", "Y030", "*P",
    "ZM101", "ZM100", "*A0", "OU11", "ZM110", "ZM111", "OU10", "F10", "*R1", "*A1", "*D", "ZM120", "*C",
    "Y101", "Y100", "ZM121", "ZT10", "ZT11", "*M", "Y110", "Y120", "Y130", "*S", "Y111", "Y121", "Y131", "*N",
    "*L", "*T", "ZT12",
)


def pair_kernel(
    n, outer, inner,
    hid, q_in, kw, vw, gain_in, cos_in, sin_in,
    out,
    w, stage, xs, x1, xb, xr, q0, q1, acc, give, take, kv0, kv1, gains, ssq, cos_ref, sin_ref,
    w_recv, w_send, stage_send, own_sem, load_sem, gain_sem, hid_sem, hid_own,
    q_sem, x1_sem, kv_sem, swap0_sem, swap_sem, part_sem,
):
    side = lax.axis_index("section")
    f = lax.axis_index("fsdp")
    mate = {"section": 1 - side}
    core = lax.rem(f, 2)
    chip = f // 2
    i = lax.rem(chip, inner)
    o = chip // inner
    twin = {"fsdp": 2 * chip + 1 - core}
    rows, width = xs.shape
    part = hid.shape[1]
    kvw = kw.shape[2]
    kv_heads = kvw // HD
    heads = kv_heads // 2
    group = width // kvw
    gw = group * HD
    depth = kw.shape[1]
    chips = n // 2
    blk = width // chips
    half = width // 2
    pieces = half // blk
    per_group = gw // blk

    local = []
    for hh in range(heads):
        for to_mate in (False, True):
            head = (1 - side if to_mate else side) * heads + hh
            cols = pl.ds(pl.multiple_of(head * HD, HD), HD)
            at = pl.ds(hh * depth, depth)
            for kind, src in enumerate((kw, vw)):
                lanes = pl.ds(kind * HD, HD)
                dst = stage.at[at, lanes] if to_mate else w.at[side, chip, at, lanes]
                local.append(pltpu.make_async_copy(src.at[0, :, cols], dst, own_sem.at[len(local)]))
    for copy in local:
        copy.start()
    loads = [
        pltpu.make_async_copy(src, dst, load_sem.at[at])
        for at, (src, dst) in enumerate(
            ((gain_in, gains.at[side]), (cos_in, cos_ref), (sin_in, sin_ref)))
    ]
    for load in loads:
        load.start()

    def q_local(which):
        if which == 0:
            return pltpu.make_async_copy(q_in.at[0, 0, :, pl.ds(0, half)], q0, load_sem.at[3])
        return pltpu.make_async_copy(q_in.at[0, 0], q1, load_sem.at[3])

    for which in range(2):
        pl.when(side == which)(lambda which=which: q_local(which).start())

    def index(oo, ii):
        return (oo * inner + ii) * 2 + core

    targets = (
        (o > 0, index(o - 1, i)),
        (o < outer - 1, index(o + 1, i)),
        (i > 0, index(o, i - 1)),
        (i < inner - 1, index(o, i + 1)),
    )

    barrier = pltpu.get_barrier_semaphore()
    for cond, target in targets:
        pl.when(cond)(lambda target=target: pl.semaphore_signal(
            barrier, inc=1, device_id={"fsdp": target}, device_id_type=MESH))
    for device in (twin, mate):
        pl.semaphore_signal(barrier, inc=1, device_id=device, device_id_type=MESH)
    expected = (
        jnp.where(o > 0, 1, 0) + jnp.where(o < outer - 1, 1, 0)
        + jnp.where(i > 0, 1, 0) + jnp.where(i < inner - 1, 1, 0) + 2
    )
    pl.semaphore_wait(barrier, expected)

    deep = heads * depth
    few = max(16, (deep * 96 // 512 + 8) // 16 * 16)
    early = (heads - 1) * depth
    cuts = [
        (pl.ds(0, at), pl.ds(at, deep - few - at), pl.ds(deep - few, few))
        for at in (deep * 160 // 512 // 16 * 16, early)
    ]
    tail = 2

    def w_copy(layer, which, way, origin):
        piece = w.at[layer, origin, cuts[layer][which]]
        return pltpu.make_async_remote_copy(
            src_ref=piece, dst_ref=piece,
            send_sem=w_send.at[layer, which, way, origin], recv_sem=w_recv.at[layer, which, origin],
            device_id={"fsdp": targets[way][1]}, device_id_type=MESH,
        )

    def w_start(layer, which, way, origin):
        pl.when(targets[way][0])(lambda: w_copy(layer, which, way, origin).start())

    def stage_copy(layer, which):
        return pltpu.make_async_remote_copy(
            src_ref=stage.at[cuts[layer][which]], dst_ref=w.at[layer, chip, cuts[layer][which]],
            send_sem=stage_send.at[which], recv_sem=w_recv.at[layer, which, chip],
            device_id=mate, device_id_type=MESH,
        )

    def gain_copy(layer):
        return pltpu.make_async_remote_copy(
            src_ref=gain_in, dst_ref=gains.at[layer], send_sem=gain_sem.at[0], recv_sem=gain_sem.at[1],
            device_id=mate, device_id_type=MESH,
        )

    def hid_copy(of):
        return pltpu.make_async_remote_copy(
            src_ref=hid.at[0], dst_ref=xs.at[pl.ds(pl.multiple_of(of * part, part), part)],
            send_sem=hid_sem.at[0], recv_sem=hid_sem.at[1], device_id=mate, device_id_type=MESH,
        )

    hid_local = pltpu.make_async_copy(
        hid.at[0], xs.at[pl.ds(pl.multiple_of(side * part, part), part)], hid_own)

    def q_copy(g):
        return pltpu.make_async_remote_copy(
            src_ref=q_in.at[0, 0, :, pl.ds(half + g * gw, gw)], dst_ref=q0.at[:, pl.ds(g * gw, gw)],
            send_sem=q_sem.at[0, g], recv_sem=q_sem.at[1, g], device_id=mate, device_id_type=MESH,
        )

    def x1_copy(of, b):
        cols = pl.ds(pl.multiple_of(of * half + b * blk, blk), blk)
        return pltpu.make_async_remote_copy(
            src_ref=x1.at[:, cols], dst_ref=x1.at[:, cols],
            send_sem=x1_sem.at[0, b], recv_sem=x1_sem.at[1, b], device_id=mate, device_id_type=MESH,
        )

    def kv_copy(hh, kind):
        return pltpu.make_async_remote_copy(
            src_ref=kv1.at[hh, kind], dst_ref=kv1.at[hh, kind],
            send_sem=kv_sem.at[0, hh, kind], recv_sem=kv_sem.at[1, hh, kind], device_id=mate, device_id_type=MESH,
        )

    swap0 = pltpu.make_async_remote_copy(
        src_ref=xb.at[0, 1 - core], dst_ref=xr.at[0], send_sem=swap0_sem.at[0], recv_sem=swap0_sem.at[1],
        device_id=twin, device_id_type=MESH,
    )

    def swap_copy(c):
        cols = pl.ds(pl.multiple_of(c * depth, depth), depth)
        return pltpu.make_async_remote_copy(
            src_ref=xb.at[1, 1 - core, :, cols], dst_ref=xr.at[1, :, cols],
            send_sem=swap_sem.at[0, c], recv_sem=swap_sem.at[1, c], device_id=twin, device_id_type=MESH,
        )

    def part_copy(layer, hh):
        return pltpu.make_async_remote_copy(
            src_ref=give.at[layer, hh], dst_ref=take.at[layer, hh],
            send_sem=part_sem.at[0, layer, hh], recv_sem=part_sem.at[1, layer, hh],
            device_id=twin, device_id_type=MESH,
        )

    for copy in local:
        copy.wait()

    for layer in range(2):
        @pl.when(side == layer)
        def _(layer=layer):
            for which in range(3):
                stage_copy(layer, which).start()
    hid_copy(side).start()
    gain_copy(side).start()
    hid_local.start()

    @pl.when(side == 0)
    def _():
        for g in range(heads):
            q_copy(g).start()

    def rope_queries(ref, first, count):
        together = math.gcd(count, 4)

        def one(at, _):
            cosine, sine = cos_ref[...], sin_ref[...]
            for h in range(together):
                cols = pl.ds(pl.multiple_of((first + at * together + h) * HD, HD), HD)
                u = ref[:, cols].astype(jnp.float32)
                ref[:, cols] = rope(u, cosine, sine).astype(jnp.bfloat16)
            return 0
        lax.fori_loop(0, count // together, one, 0)

    def relay(layer, which, origin, ways):
        w_copy(layer, which, 0, origin).wait_recv()
        for way in ways:
            w_start(layer, which, way, origin)

    def drain(layer, which, origin, ways):
        for way in ways:
            pl.when(targets[way][0])(lambda way=way: w_copy(layer, which, way, origin).wait_send())

    def sides(t, act):
        if t == 0:
            act(o, None, 0)
        else:
            act(o - t, o - t >= 0, 1)
            act(o + t, o + t < outer, 0)

    def around(there, act):
        for d in range(1, inner):
            for cond, ii, way in ((i - d >= 0, i - d, 3), (i + d < inner, i + d, 2)):
                pl.when(cond if there is None else there & cond)(lambda ii=ii, way=way: act(ii, way))

    def own(kind, layer, on, which, receive):
        ways = {"OM": (0, 1, 2, 3), "OT": (2, 3), "OU": (0, 1)}[kind]

        @pl.when(side == on)
        def _():
            if receive is relay:
                if on != layer and kind != "OU":
                    w_copy(layer, which, 0, chip).wait_recv()
                for way in ways:
                    w_start(layer, which, way, chip)
            else:
                drain(layer, which, chip, ways)

    def far(t, act):
        sides(t, lambda oo, there, way: pl.when(there)(lambda: act(oo, way)))

    def move(kind, layer, t, which, receive):
        if kind[0] == "O":
            own(kind, layer, t, tail if which is None else which, receive)
        elif kind == "F":
            around(None, lambda ii, way: receive(layer, tail, o * inner + ii, (way, 0, 1)))
        elif kind == "ZM":
            far(t + 1, lambda oo, way: receive(layer, which, oo * inner + i, (way, 2, 3)))
        elif kind == "ZT":
            def both(oo, there, way):
                pl.when(there)(lambda: receive(layer, tail, oo * inner + i, (way,)))
                around(there, lambda ii, _: receive(layer, tail, oo * inner + ii, (way,)))
            sides(t + 1, both)
        elif kind == "Y":
            sides(t, lambda oo, there, _: around(
                there, lambda ii, way: receive(layer, which, oo * inner + ii, (way,))))

    row = lax.broadcasted_iota(jnp.int32, (rows, rows), 0)
    col = lax.broadcasted_iota(jnp.int32, (rows, rows), 1)
    scale = math.log2(math.e) / math.sqrt(HD)

    def scaled(src, c, layer):
        cols = pl.ds(pl.multiple_of(c * blk, blk), blk)
        x = src[:, cols].astype(jnp.float32)
        y = (x * gains[layer, :, cols]).astype(jnp.bfloat16)
        for kind in range(2):
            xb[layer, kind, :, pl.ds(pl.multiple_of(c * depth, depth), depth)] = y[:, kind * depth:(kind + 1) * depth]
        square = x * x
        total = square[:, :HD]
        for at in range(1, blk // HD):
            total += square[:, at * HD:(at + 1) * HD]
        ssq[layer] += total

    def project(layer, hh, first, count, fresh):
        cols = pl.ds(pl.multiple_of(first * depth, depth), count * depth)
        a = jnp.concatenate([xb[layer, core, :, cols], xr[layer, :, cols]], axis=0)
        b = w[layer, pl.ds(first, count), hh * depth:(hh + 1) * depth].reshape(count * depth, 2 * HD)
        y = jnp.dot(a, b, preferred_element_type=jnp.float32)
        if fresh:
            acc[layer, hh] = y[:rows]
            give[layer, hh] = y[rows:]
        else:
            acc[layer, hh] += y[:rows]
            give[layer, hh] += y[rows:]

    def finish(layer, hh, ref, at, then=None):
        part_copy(layer, hh).wait_recv()
        r = lax.rsqrt(jnp.sum(ssq[layer], axis=-1, keepdims=True) / width + EPS)
        y = (acc[layer, hh] + take[layer, hh]) * r
        ref[at, 0] = rope(y[:, :HD], cos_ref[...], sin_ref[...]).astype(jnp.bfloat16)
        if then is not None:
            then(0)
        ref[at, 1] = y[:, HD:].astype(jnp.bfloat16)
        if then is not None:
            then(1)

    def attend(q_ref, q_first, kv_ref, head, x_ref, x_first, write, ready=None):
        if ready is not None:
            ready(0)
        k = kv_ref[head, 0]
        allowed = (col <= row)[None]
        batch = group // 4
        probs = []
        for first in range(0, group, batch):
            q = jnp.concatenate(
                [q_ref[:, pl.ds(pl.multiple_of(q_first + (first + h) * HD, HD), HD)] for h in range(batch)], axis=0)
            scores = lax.dot_general(q, k, (((1,), (1,)), ((), ())), preferred_element_type=jnp.float32)
            scores = jnp.where(allowed, scores.reshape(batch, rows, rows), -1e30)
            top = jnp.max(scores, axis=-1, keepdims=True)
            probs.append(jnp.exp2((scores - top) * scale).astype(jnp.bfloat16).reshape(batch * rows, rows))
        if ready is not None:
            ready(1)
        v = jnp.concatenate([kv_ref[head, 1], jnp.ones((rows, HD), jnp.bfloat16)], axis=1)
        for first, p in zip(range(0, group, batch), probs):
            mixed = jnp.dot(p, v, preferred_element_type=jnp.float32)
            mixed = mixed[:, :HD] / mixed[:, HD:]
            for h in range(batch):
                cols = pl.ds(pl.multiple_of(x_first + (first + h) * HD, HD), HD)
                write(cols, (
                    x_ref[:, cols].astype(jnp.float32) + mixed[h * rows:(h + 1) * rows]
                ).astype(jnp.bfloat16))

    def write_x1(cols, value):
        x1[:, cols] = value

    def write_out(cols, value):
        out[0, 0, :, cols] = value

    def queries_in():
        for load in loads:
            load.wait()

        @pl.when(side == 1)
        def _():
            q_local(1).wait()
            rope_queries(q1, 0, width // HD)

        ssq[...] = jnp.zeros_like(ssq)

    def queries_mine():
        @pl.when(side == 0)
        def _():
            q_local(0).wait()
            rope_queries(q0, 0, half // HD)

    def inputs_in():
        hid_local.wait()
        hid_copy(1 - side).wait_recv()
        gain_copy(1 - side).wait_recv()

        def one(c, _):
            scaled(xs, c, 0)
            return 0
        lax.fori_loop(0, chips, one, 0)
        swap0.start()

    def first_layer():
        swap0.wait_recv()
        for hh in range(heads):
            project(0, hh, 0, chips, True)
            part_copy(0, hh).start()

    def queries_arrive(g):
        @pl.when(side == 1)
        def _():
            q_copy(g).wait_recv()
            rope_queries(q0, g * group, group)

    def first_attention(g):
        finish(0, g, kv0, g)
        attend(q0, g * gw, kv0, g, xs, side * half + g * gw, write_x1)

        def one(b, _):
            x1_copy(side, b).start()
            scaled(x1, side * pieces + b, 1)
            swap_copy(side * pieces + b).start()
            return 0
        lax.fori_loop(g * per_group, (g + 1) * per_group, one, 0)

    def mate_in():
        def one(b, _):
            c = (1 - side) * pieces + b
            x1_copy(1 - side, b).wait_recv()
            scaled(x1, c, 1)
            swap_copy(c).start()
            return 0
        lax.fori_loop(0, pieces, one, 0)

    def swapped(of):
        def one(b, _):
            swap_copy(of * pieces + b).wait_recv()
            return 0
        lax.fori_loop(0, pieces, one, 0)

    def second_layer(hh, first, count, fresh, send=True):
        project(1, hh, first, count, fresh)
        if send:
            part_copy(1, hh).start()

    def second_done(hh, then=None):
        finish(1, hh, kv1, side * heads + hh, then)

    def send_done(hh):
        @pl.when(side == 0)
        def _():
            second_done(hh, lambda kind: kv_copy(hh, kind).start())

    def first_side_in():
        @pl.when(side == 0)
        def _():
            mate_in()
            out[0, 0] = x1[...]
            swapped(1)
        swapped(side)

    def second_side_in():
        @pl.when(side == 1)
        def _():
            mate_in()
            swapped(0)

    def early_heads():
        for hh in range(heads - 1):
            pl.when(side == 0)(lambda hh=hh: second_layer(hh, 0, chips, True))
            pl.when(side == 1)(lambda hh=hh: second_layer(hh, side * pieces, pieces, True, send=False))

    def settle_first():
        for layer in range(2):
            @pl.when(side == layer)
            def _(layer=layer):
                for which in range(3):
                    stage_copy(layer, which).wait_send()
        gain_copy(side).wait_send()
        hid_copy(side).wait_send()
        swap0.wait_send()
        for hh in range(heads):
            part_copy(0, hh).wait_send()

    def drain_moves(layers):
        for step in [step for step in moves if step[1] in layers]:
            moves.remove(step)
            move(*step, drain)

    moves = []
    for word in ORDER:
        if word[0] == "*":
            if word == "*Q":
                queries_in()
            elif word == "*q":
                queries_mine()
            elif word == "*X":
                inputs_in()
            elif word == "*P":
                first_layer()
            elif word[1] == "A":
                first_attention(int(word[2]))
            elif word[1] in "ab":
                pl.when(side == "ba".index(word[1]))(lambda g=int(word[2]): first_attention(g))
            elif word == "*L":
                second_layer(heads - 1, jnp.where(o < outer // 2, 0, inner), chips - inner, True, send=False)
            elif word == "*N":
                second_side_in()
            elif word == "*C":
                settle_first()
            elif word == "*D":
                drain_moves((0,))
            elif word[1] == "R":
                queries_arrive(int(word[2]))
            elif word == "*M":
                first_side_in()
            elif word == "*S":
                early_heads()
            elif word == "*T":
                for hh in range(heads - 1):
                    send_done(hh)
        else:
            kind = word.rstrip("0123456789")
            digits = [int(d) for d in word[len(kind):]]
            step = (kind, digits[0], digits[1], digits[2] if len(digits) > 2 else None)
            moves.append(step)
            move(*step, relay)

    @pl.when(side == 1)
    def _():
        for hh in range(heads - 1):
            second_layer(hh, (1 - side) * pieces, pieces, False)
    second_layer(heads - 1, jnp.where(o < outer // 2, (outer - 1) * inner, 0), inner, False)
    send_done(heads - 1)

    @pl.when(side == 1)
    def _():
        for hh in range(heads - 1):
            second_done(hh)

        def one(g, _):
            pl.when(g == heads - 1)(lambda: second_done(heads - 1))
            attend(q1, (heads + g) * gw, kv1, heads + g, x1, (heads + g) * gw, write_out)
            return 0
        lax.fori_loop(0, heads, one, 0)

    drain_moves((0, 1))
    for c in range(chips):
        swap_copy(c).wait_send()
    for hh in range(heads):
        part_copy(1, hh).wait_send()
    for b in range(pieces):
        x1_copy(side, b).wait_send()

    @pl.when(side == 0)
    def _():
        for g in range(heads):
            q_copy(g).wait_send()
        for hh in range(heads):
            for kind in range(2):
                kv_copy(hh, kind).wait_send()

    @pl.when(side == 1)
    def _():
        def one(g, _):
            attend(q1, g * gw, kv1, g, x1, g * gw, write_out, lambda kind: kv_copy(g, kind).wait_recv())
            return 0
        lax.fori_loop(0, heads, one, 0)


def solution(mesh):
    sections, n = mesh.shape["section"], mesh.shape["fsdp"]
    chips = n // 2
    outer = 4 if chips % 4 == 0 else 1
    inner = chips // outer

    def body(hidden_in, queries, key_weight, value_weight, norm_gain):
        rows, width = queries.shape[2:]
        depth, kvw = key_weight.shape[1:]
        cosine, sine = rope_tables(rows)
        hbm = pl.BlockSpec(memory_space=pltpu.HBM)
        vmem = pl.BlockSpec(memory_space=pltpu.VMEM)
        dma = pltpu.SemaphoreType.DMA
        bf16, f32 = jnp.bfloat16, jnp.float32
        if sections == 2 and outer == 4 and depth % HD == 0:
            heads = kvw // HD // 2
            pieces = chips // 2
            run = functools.partial(pair_kernel, n, outer, inner)
            scratch = [
                pltpu.VMEM((2, chips, heads * depth, 2 * HD), bf16),
                pltpu.VMEM((heads * depth, 2 * HD), bf16),
                pltpu.VMEM((rows, width), bf16),
                pltpu.VMEM((rows, width), bf16),
                pltpu.VMEM((2, 2, rows, width // 2), bf16),
                pltpu.VMEM((2, rows, width // 2), bf16),
                pltpu.VMEM((rows, width // 2), bf16),
                pltpu.VMEM((rows, width), bf16),
                pltpu.VMEM((2, heads, rows, 2 * HD), f32),
                pltpu.VMEM((2, heads, rows, 2 * HD), f32),
                pltpu.VMEM((2, heads, rows, 2 * HD), f32),
                pltpu.VMEM((heads, 2, rows, HD), bf16),
                pltpu.VMEM((2 * heads, 2, rows, HD), bf16),
                pltpu.VMEM((2, 1, width), f32),
                pltpu.VMEM((2, rows, HD), f32),
                pltpu.VMEM((rows, HD), f32),
                pltpu.VMEM((rows, HD), f32),
                dma((2, 3, chips)), dma((2, 3, 4, chips)), dma((3,)), dma((4 * heads,)),
                dma((4,)), dma((2,)), dma((2,)), dma,
                dma((2, heads)), dma((2, pieces)), dma((2, heads, 2)), dma((2,)), dma((2, chips)), dma((2, 2, heads)),
            ]
        else:
            run = functools.partial(chain_kernel, n, sections, outer, inner)
            scratch = [
                pltpu.VMEM((n, 2, depth, kvw), bf16),
                pltpu.VMEM((rows, width), bf16),
                pltpu.VMEM((rows, width), bf16),
                pltpu.VMEM((rows, width), bf16),
                pltpu.VMEM((rows, width), bf16),
                pltpu.VMEM((n // 2, rows, 2 * depth), bf16),
                pltpu.VMEM((2, rows, kvw), f32),
                pltpu.VMEM((kvw // HD, 2, rows, HD), bf16),
                pltpu.VMEM((kvw // HD, 2, rows, HD), bf16),
                pltpu.VMEM((1, width), f32),
                pltpu.VMEM((rows, HD), f32),
                pltpu.VMEM((rows, HD), f32),
                dma((3, n)), dma((3, 5, n)), dma((2,)), dma((sections,)), dma((2,)), dma,
                dma((2,)), dma((2, kvw // HD)), dma((2,)), dma((4,)),
            ]
        return pl.pallas_call(
            run,
            out_shape=jax.ShapeDtypeStruct(queries.shape, bf16),
            in_specs=[hbm] * 7,
            out_specs=vmem,
            scratch_shapes=scratch,
            compiler_params=pltpu.CompilerParams(
                collective_id=0, has_side_effects=True, vmem_limit_bytes=28 * 2**20
            ),
        )(*(
            pltpu.with_memory_space_constraint(x, pltpu.HBM)
            for x in (hidden_in, queries, key_weight, value_weight, norm_gain, jnp.asarray(cosine), jnp.asarray(sine))
        ))

    placed = (
        P("fsdp", "section", None),
        P("section", "fsdp", None, None),
        P("section", "fsdp", None),
        P("section", "fsdp", None),
        P("section", None),
    )
    return jax.shard_map(
        body, mesh=mesh, in_specs=placed, out_specs=P("section", "fsdp", None, None), check_vma=False
    )
```

```python
import functools
import math

import jax
import jax.numpy as jnp
import numpy as np
from jax import lax
from jax.experimental import pallas as pl
from jax.experimental.pallas import tpu as pltpu
from jax.sharding import PartitionSpec as P

HD = 128
EPS = 1e-05
MESH = pl.DeviceIdType.MESH


def rope_tables(rows):
    half = HD // 2
    frequency = np.exp(np.arange(half, dtype=np.float32) * np.float32(-2.0 * math.log(10000.0) / HD))
    angles = np.arange(rows, dtype=np.float32)[:, None] * frequency[None, :].astype(np.float32)
    cosine, sine = np.cos(angles), np.sin(angles)
    return (
        np.concatenate([cosine, cosine], 1).astype(np.float32),
        np.concatenate([-sine, sine], 1).astype(np.float32),
    )


def rope(u, cosine, sine):
    return u * cosine + pltpu.roll(u, HD // 2, 1) * sine


def chain_kernel(
    n, sections, outer, inner,
    hid, q_in, kw, vw, gain_in, cos_in, sin_in,
    out,
    w, xin, xs, qs, qp, normed, acc, kv, kvp, gain, cos_ref, sin_ref,
    w_recv, w_send, own_sem, hid_recv, hid_send, hid_own, q_sem, kv_sem, x_sem, load_sem,
):
    s = lax.axis_index("section")
    f = lax.axis_index("fsdp")
    core = lax.rem(f, 2)
    chip = f // 2
    i = lax.rem(chip, inner)
    o = chip // inner
    rows, width = xs.shape
    part = hid.shape[1]
    kvw = kw.shape[2]
    kv_heads = kvw // HD
    group = width // kvw
    depth = kw.shape[1]

    def index(oo, ii, cc):
        return (oo * inner + ii) * 2 + cc

    own_k = pltpu.make_async_copy(kw.at[0], w.at[f, 0], own_sem.at[0])
    own_v = pltpu.make_async_copy(vw.at[0], w.at[f, 1], own_sem.at[1])
    own_k.start()
    own_v.start()
    loads = [
        pltpu.make_async_copy(src, dst, load_sem.at[at])
        for at, (src, dst) in enumerate(
            ((q_in.at[0, 0], qs), (gain_in, gain), (cos_in, cos_ref), (sin_in, sin_ref)))
    ]
    for load in loads:
        load.start()

    targets = (
        (o > 0, index(o - 1, i, core)),
        (o < outer - 1, index(o + 1, i, core)),
        (i > 0, index(o, i - 1, core)),
        (i < inner - 1, index(o, i + 1, core)),
        (None, index(o, i, 1 - core)),
    )

    barrier = pltpu.get_barrier_semaphore()
    for cond, target in targets:
        def greet(target=target):
            pl.semaphore_signal(barrier, inc=1, device_id={"fsdp": target}, device_id_type=MESH)
        if cond is None:
            greet()
        else:
            pl.when(cond)(greet)
    for step in range(1, sections):
        pl.semaphore_signal(
            barrier, inc=1, device_id={"section": lax.rem(s + step, sections)}, device_id_type=MESH
        )
    expected = (
        jnp.where(o > 0, 1, 0) + jnp.where(o < outer - 1, 1, 0)
        + jnp.where(i > 0, 1, 0) + jnp.where(i < inner - 1, 1, 0) + sections
    )
    pl.semaphore_wait(barrier, expected)

    few = max(16, depth // 8)
    first = (depth - few + 16) // 32 * 16
    cuts = (pl.ds(0, first), pl.ds(first, depth - few - first), pl.ds(depth - few, few))
    mains, tail = (0, 1), 2

    def w_copy(which, way, origin):
        piece = w.at[origin, :, cuts[which]]
        return pltpu.make_async_remote_copy(
            src_ref=piece, dst_ref=piece,
            send_sem=w_send.at[which, way, origin], recv_sem=w_recv.at[which, origin],
            device_id={"fsdp": targets[way][1]}, device_id_type=MESH,
        )

    def w_start(which, way, origin):
        cond = targets[way][0]
        if cond is None:
            w_copy(which, way, origin).start()
        else:
            pl.when(cond)(lambda: w_copy(which, way, origin).start())

    own_k.wait()
    own_v.wait()
    for way in (2, 3):
        w_start(tail, way, f)
    for which in mains:
        for way in range(5):
            w_start(which, way, f)
    for way in (0, 1, 4):
        w_start(tail, way, f)

    mine = pl.ds(pl.multiple_of(s * part, part), part)

    def hid_copy(to):
        dst = xs if to == 0 else xin
        return pltpu.make_async_remote_copy(
            src_ref=hid.at[0], dst_ref=dst.at[mine], send_sem=hid_send.at[to],
            recv_sem=hid_recv.at[s], device_id={"section": to}, device_id_type=MESH,
        )

    def hid_local(to):
        dst = xs if to == 0 else xin
        return pltpu.make_async_copy(hid.at[0], dst.at[mine], hid_own)

    for to in range(min(2, sections)):
        pl.when(s != to)(lambda to=to: hid_copy(to).start())
        pl.when(s == to)(lambda to=to: hid_local(to).start())

    q_copy = pltpu.make_async_remote_copy(
        src_ref=q_in.at[0, 0], dst_ref=qp, send_sem=q_sem.at[0], recv_sem=q_sem.at[1],
        device_id={"section": jnp.minimum(s + 1, sections - 1)}, device_id_type=MESH,
    )
    def kv_copy(g):
        return pltpu.make_async_remote_copy(
            src_ref=kv.at[g], dst_ref=kvp.at[g], send_sem=kv_sem.at[0, g], recv_sem=kv_sem.at[1, g],
            device_id={"section": jnp.minimum(s + 1, sections - 1)}, device_id_type=MESH,
        )

    x_copy = pltpu.make_async_remote_copy(
        src_ref=xs, dst_ref=xin, send_sem=x_sem.at[0], recv_sem=x_sem.at[1],
        device_id={"section": jnp.minimum(s + 1, sections - 1)}, device_id_type=MESH,
    )
    last = s == sections - 1
    pl.when(jnp.logical_not(last))(lambda: q_copy.start())

    for load in loads:
        load.wait()

    def rope_queries(ref):
        def one(h, _):
            cols = pl.ds(pl.multiple_of(h * HD, HD), HD)
            u = ref[:, cols].astype(jnp.float32)
            ref[:, cols] = rope(u, cos_ref[...], sin_ref[...]).astype(jnp.bfloat16)
            return 0
        lax.fori_loop(0, width // HD, one, 0)

    rope_queries(qs)

    def hid_arrive(to):
        hid_local(to).wait()
        dst = xs if to == 0 else xin
        for step in range(1, sections):
            j = lax.rem(to + step, sections)
            pltpu.make_async_remote_copy(
                src_ref=hid.at[0], dst_ref=dst.at[pl.ds(j * part, part)],
                send_sem=hid_send.at[to], recv_sem=hid_recv.at[j],
                device_id={"section": to}, device_id_type=MESH,
            ).wait_recv()

    block = 16

    def norm():
        def one(r, _):
            at = pl.ds(pl.multiple_of(r * block, block), block)
            x = xs[at, :].astype(jnp.float32)
            mean_square = jnp.mean(x * x, axis=-1, keepdims=True)
            y = (x * lax.rsqrt(mean_square + EPS) * gain[...]).astype(jnp.bfloat16)
            for pair in range(n // 2):
                normed[pair, at, :] = y[:, pair * 2 * depth:(pair + 1) * 2 * depth]
            return 0
        lax.fori_loop(0, rows // block, one, 0)

    def project(pair):
        a = normed[pair]
        for half in range(2):
            b = w[pl.ds(pair * 2, 2), half].reshape(2 * depth, kvw)
            acc[half] += jnp.dot(a, b, preferred_element_type=jnp.float32)

    acc[...] = jnp.zeros_like(acc)

    def arrive(which, origin, ways):
        w_copy(which, 4, origin).wait_recv()
        for way in ways:
            w_start(which, way, origin)

    def relay(which, origin, ways):
        arrive(which, origin, ways)

    def from_other(which, origin, ways):
        arrive(which, origin, ())

    def project_pair(which, origin, ways):
        if which == tail - 1:
            project(origin // 2)

    def sides(t, act):
        for sign, way in ((-1, 1), (1, 0)):
            far = o - t if sign < 0 else o + t
            there = (far >= 0) if sign < 0 else ((far < outer) & (t > 0))
            act(far, there, way)

    def around(there, act):
        for d in range(1, inner):
            pl.when(there & (i - d >= 0))(lambda d=d: act(i - d, 3))
            pl.when(there & (i + d < inner))(lambda d=d: act(i + d, 2))

    def along_outer(t, c, receive):
        for which in mains:
            def act(far, there, way, which=which):
                pl.when(there)(lambda: receive(which, index(far, i, c), (way, 2, 3, 4)))
            sides(t, act)

        def act_tail(far, there, way):
            pl.when(there)(lambda: receive(tail, index(far, i, c), (way, 4)))
            around(there, lambda ii, _: receive(tail, index(far, ii, c), (way, 4)))
        sides(t, act_tail)

    def along_inner(t, c, receive):
        for which in mains:
            def act(far, there, _, which=which):
                around(there, lambda ii, way: receive(which, index(far, ii, c), (way, 4)))
            sides(t, act)

    def first_inner(c, receive):
        around(o >= 0, lambda ii, way: receive(tail, index(o, ii, c), (way, 0, 1, 4)))

    first_inner(core, relay)

    def step(t, _):
        along_outer(t + 1, core, relay)

        @pl.when((t == 0) & (s == 0))
        def _():
            hid_arrive(0)
            norm()

        @pl.when(t == 0)
        def _():
            for which in (*mains, tail):
                arrive(which, index(o, i, 1 - core), ())
            first_inner(1 - core, from_other)

        along_inner(t, core, relay)
        along_outer(t + 1, 1 - core, from_other)
        along_inner(t, 1 - core, from_other)

        @pl.when(s == 0)
        def _():
            pl.when(t == 0)(lambda: project(chip))
            along_outer(t + 1, core, project_pair)
            along_inner(t, core, project_pair)

        return 0

    lax.fori_loop(0, outer, step, 0)

    row = lax.broadcasted_iota(jnp.int32, (rows, rows), 0)
    col = lax.broadcasted_iota(jnp.int32, (rows, rows), 1)
    scale = math.log2(math.e) / math.sqrt(HD)

    def attend(q_ref, kv_ref, x_ref, o_write, ready):
        ones = jnp.ones((rows, HD), jnp.bfloat16)
        allowed = (col <= row)[None]

        def one(g, _):
            ready(g)
            k = kv_ref[g, 0]
            v = jnp.concatenate([kv_ref[g, 1], ones], axis=1)
            base = g * group * HD
            cols = [pl.ds(pl.multiple_of(base + h * HD, HD), HD) for h in range(group)]
            q = jnp.concatenate([q_ref[:, c] for c in cols], axis=0)
            scores = lax.dot_general(q, k, (((1,), (1,)), ((), ())), preferred_element_type=jnp.float32)
            scores = jnp.where(allowed, scores.reshape(group, rows, rows), -1e30)
            top = jnp.max(scores, axis=-1, keepdims=True)
            p = jnp.exp2((scores - top) * scale).astype(jnp.bfloat16).reshape(group * rows, rows)
            mixed = jnp.dot(p, v, preferred_element_type=jnp.float32)
            mixed = mixed[:, :HD] / mixed[:, HD:]
            for h in range(group):
                o_write(cols[h], (
                    x_ref[:, cols[h]].astype(jnp.float32) + mixed[h * rows:(h + 1) * rows]
                ).astype(jnp.bfloat16))
            return 0

        lax.fori_loop(0, kv_heads, one, 0)

    def write_xs(c, value):
        xs[:, c] = value

    def write_out(c, value):
        out[0, 0, :, c] = value

    @pl.when(s > 0)
    def _():
        q_copy.wait_recv()
        rope_queries(qp)
        pl.when(s == 1)(lambda: hid_arrive(1))
        if sections > 2:
            pl.when(s > 1)(lambda: x_copy.wait_recv())
        attend(qp, kvp, xin, write_xs, lambda g: kv_copy(g).wait_recv())
        if sections > 2:
            pl.when(jnp.logical_not(last))(lambda: x_copy.start())
        norm()
        def one(j, _):
            project(j)
            return 0
        lax.fori_loop(0, n // 2, one, 0)

    for h in range(kv_heads):
        at = slice(h * HD, (h + 1) * HD)
        kv[h, 0] = rope(acc[0, :, at], cos_ref[...], sin_ref[...]).astype(jnp.bfloat16)
        kv[h, 1] = acc[1, :, at].astype(jnp.bfloat16)
        pl.when(jnp.logical_not(last))(lambda h=h: kv_copy(h).start())
    attend(qs, kv, xs, write_out, lambda g: None)

    def drain(which, origin, ways):
        for way in ways:
            cond = targets[way][0]
            if cond is None:
                w_copy(which, way, origin).wait_send()
            else:
                pl.when(cond)(lambda way=way: w_copy(which, way, origin).wait_send())

    for which in (*mains, tail):
        drain(which, f, range(5))
    first_inner(core, drain)

    def drain_step(t, _):
        along_outer(t + 1, core, drain)
        along_inner(t, core, drain)
        return 0

    lax.fori_loop(0, outer, drain_step, 0)
    for to in range(min(2, sections)):
        pl.when(s != to)(lambda to=to: hid_copy(to).wait_send())

    @pl.when(jnp.logical_not(last))
    def _():
        q_copy.wait_send()
        for h in range(kv_heads):
            kv_copy(h).wait_send()
        if sections > 2:
            pl.when(s > 0)(lambda: x_copy.wait_send())


ORDER = (
    "OM000", "OM001", "OM110", "OT00", "OU00", "OT11", "OM111", "*Q", "OM010", "OM011", "OT01", "OU01",
    "ZM000", "ZM001", "F00", "OM101", "ZM011", "ZM010", "ZM021", "ZM020", "ZT00", "*X", "Y010", "Y011",
    "ZT01", "OM100", "Y020", "*q", "Y001", "Y031", "OT10", "Y000", "Y021", "*R0", "ZT02", "Y030", "*P",
    "ZM101", "ZM100", "*A0", "OU11", "ZM110", "ZM111", "OU10", "F10", "*R1", "*A1", "*D", "ZM120", "*C",
    "Y101", "Y100", "ZM121", "ZT10", "ZT11", "*M", "Y110", "Y120", "Y130", "*S", "Y111", "Y121", "Y131", "*N",
    "*L", "*T", "ZT12",
)


def pair_kernel(
    n, outer, inner,
    hid, q_in, kw, vw, gain_in, cos_in, sin_in,
    out,
    w, stage, xs, x1, xb, xr, q0, q1, acc, give, take, kv0, kv1, gains, ssq, cos_ref, sin_ref,
    w_recv, w_send, stage_send, own_sem, load_sem, gain_sem, hid_sem, hid_own,
    q_sem, x1_sem, kv_sem, swap0_sem, swap_sem, part_sem,
):
    side = lax.axis_index("section")
    f = lax.axis_index("fsdp")
    mate = {"section": 1 - side}
    core = lax.rem(f, 2)
    chip = f // 2
    i = lax.rem(chip, inner)
    o = chip // inner
    twin = {"fsdp": 2 * chip + 1 - core}
    rows, width = xs.shape
    part = hid.shape[1]
    kvw = kw.shape[2]
    kv_heads = kvw // HD
    heads = kv_heads // 2
    group = width // kvw
    gw = group * HD
    depth = kw.shape[1]
    chips = n // 2
    blk = width // chips
    half = width // 2
    pieces = half // blk
    per_group = gw // blk

    local = []
    for hh in range(heads):
        for to_mate in (False, True):
            head = (1 - side if to_mate else side) * heads + hh
            cols = pl.ds(pl.multiple_of(head * HD, HD), HD)
            at = pl.ds(hh * depth, depth)
            for kind, src in enumerate((kw, vw)):
                lanes = pl.ds(kind * HD, HD)
                dst = stage.at[at, lanes] if to_mate else w.at[side, chip, at, lanes]
                local.append(pltpu.make_async_copy(src.at[0, :, cols], dst, own_sem.at[len(local)]))
    for copy in local:
        copy.start()
    loads = [
        pltpu.make_async_copy(src, dst, load_sem.at[at])
        for at, (src, dst) in enumerate(
            ((gain_in, gains.at[side]), (cos_in, cos_ref), (sin_in, sin_ref)))
    ]
    for load in loads:
        load.start()

    def q_local(which):
        if which == 0:
            return pltpu.make_async_copy(q_in.at[0, 0, :, pl.ds(0, half)], q0, load_sem.at[3])
        return pltpu.make_async_copy(q_in.at[0, 0], q1, load_sem.at[3])

    for which in range(2):
        pl.when(side == which)(lambda which=which: q_local(which).start())

    def index(oo, ii):
        return (oo * inner + ii) * 2 + core

    targets = (
        (o > 0, index(o - 1, i)),
        (o < outer - 1, index(o + 1, i)),
        (i > 0, index(o, i - 1)),
        (i < inner - 1, index(o, i + 1)),
    )

    barrier = pltpu.get_barrier_semaphore()
    for cond, target in targets:
        pl.when(cond)(lambda target=target: pl.semaphore_signal(
            barrier, inc=1, device_id={"fsdp": target}, device_id_type=MESH))
    for device in (twin, mate):
        pl.semaphore_signal(barrier, inc=1, device_id=device, device_id_type=MESH)
    expected = (
        jnp.where(o > 0, 1, 0) + jnp.where(o < outer - 1, 1, 0)
        + jnp.where(i > 0, 1, 0) + jnp.where(i < inner - 1, 1, 0) + 2
    )
    pl.semaphore_wait(barrier, expected)

    deep = heads * depth
    few = max(16, (deep * 96 // 512 + 8) // 16 * 16)
    early = (heads - 1) * depth
    cuts = [
        (pl.ds(0, at), pl.ds(at, deep - few - at), pl.ds(deep - few, few))
        for at in (deep * 112 // 512 // 16 * 16, early)
    ]
    tail = 2

    def w_copy(layer, which, way, origin):
        piece = w.at[layer, origin, cuts[layer][which]]
        return pltpu.make_async_remote_copy(
            src_ref=piece, dst_ref=piece,
            send_sem=w_send.at[layer, which, way, origin], recv_sem=w_recv.at[layer, which, origin],
            device_id={"fsdp": targets[way][1]}, device_id_type=MESH,
        )

    def w_start(layer, which, way, origin):
        pl.when(targets[way][0])(lambda: w_copy(layer, which, way, origin).start())

    def stage_copy(layer, which):
        return pltpu.make_async_remote_copy(
            src_ref=stage.at[cuts[layer][which]], dst_ref=w.at[layer, chip, cuts[layer][which]],
            send_sem=stage_send.at[which], recv_sem=w_recv.at[layer, which, chip],
            device_id=mate, device_id_type=MESH,
        )

    def gain_copy(layer):
        return pltpu.make_async_remote_copy(
            src_ref=gain_in, dst_ref=gains.at[layer], send_sem=gain_sem.at[0], recv_sem=gain_sem.at[1],
            device_id=mate, device_id_type=MESH,
        )

    def hid_copy(of):
        return pltpu.make_async_remote_copy(
            src_ref=hid.at[0], dst_ref=xs.at[pl.ds(pl.multiple_of(of * part, part), part)],
            send_sem=hid_sem.at[0], recv_sem=hid_sem.at[1], device_id=mate, device_id_type=MESH,
        )

    hid_local = pltpu.make_async_copy(
        hid.at[0], xs.at[pl.ds(pl.multiple_of(side * part, part), part)], hid_own)

    def q_copy(g):
        return pltpu.make_async_remote_copy(
            src_ref=q_in.at[0, 0, :, pl.ds(half + g * gw, gw)], dst_ref=q0.at[:, pl.ds(g * gw, gw)],
            send_sem=q_sem.at[0, g], recv_sem=q_sem.at[1, g], device_id=mate, device_id_type=MESH,
        )

    def x1_copy(of, b):
        cols = pl.ds(pl.multiple_of(of * half + b * blk, blk), blk)
        return pltpu.make_async_remote_copy(
            src_ref=x1.at[:, cols], dst_ref=x1.at[:, cols],
            send_sem=x1_sem.at[0, b], recv_sem=x1_sem.at[1, b], device_id=mate, device_id_type=MESH,
        )

    def kv_copy(hh, kind):
        return pltpu.make_async_remote_copy(
            src_ref=kv1.at[hh, kind], dst_ref=kv1.at[hh, kind],
            send_sem=kv_sem.at[0, hh, kind], recv_sem=kv_sem.at[1, hh, kind], device_id=mate, device_id_type=MESH,
        )

    swap0 = pltpu.make_async_remote_copy(
        src_ref=xb.at[0, 1 - core], dst_ref=xr.at[0], send_sem=swap0_sem.at[0], recv_sem=swap0_sem.at[1],
        device_id=twin, device_id_type=MESH,
    )

    def swap_copy(c):
        cols = pl.ds(pl.multiple_of(c * depth, depth), depth)
        return pltpu.make_async_remote_copy(
            src_ref=xb.at[1, 1 - core, :, cols], dst_ref=xr.at[1, :, cols],
            send_sem=swap_sem.at[0, c], recv_sem=swap_sem.at[1, c], device_id=twin, device_id_type=MESH,
        )

    def part_copy(layer, hh):
        return pltpu.make_async_remote_copy(
            src_ref=give.at[layer, hh], dst_ref=take.at[layer, hh],
            send_sem=part_sem.at[0, layer, hh], recv_sem=part_sem.at[1, layer, hh],
            device_id=twin, device_id_type=MESH,
        )

    for copy in local:
        copy.wait()

    for layer in range(2):
        @pl.when(side == layer)
        def _(layer=layer):
            for which in range(3):
                stage_copy(layer, which).start()
    hid_copy(side).start()
    gain_copy(side).start()
    hid_local.start()

    @pl.when(side == 0)
    def _():
        for g in range(heads):
            q_copy(g).start()

    def rope_queries(ref, first, count):
        together = math.gcd(count, 4)

        def one(at, _):
            cosine, sine = cos_ref[...], sin_ref[...]
            for h in range(together):
                cols = pl.ds(pl.multiple_of((first + at * together + h) * HD, HD), HD)
                u = ref[:, cols].astype(jnp.float32)
                ref[:, cols] = rope(u, cosine, sine).astype(jnp.bfloat16)
            return 0
        lax.fori_loop(0, count // together, one, 0)

    def relay(layer, which, origin, ways):
        w_copy(layer, which, 0, origin).wait_recv()
        for way in ways:
            w_start(layer, which, way, origin)

    def drain(layer, which, origin, ways):
        for way in ways:
            pl.when(targets[way][0])(lambda way=way: w_copy(layer, which, way, origin).wait_send())

    def sides(t, act):
        if t == 0:
            act(o, None, 0)
        else:
            act(o - t, o - t >= 0, 1)
            act(o + t, o + t < outer, 0)

    def around(there, act):
        for d in range(1, inner):
            for cond, ii, way in ((i - d >= 0, i - d, 3), (i + d < inner, i + d, 2)):
                pl.when(cond if there is None else there & cond)(lambda ii=ii, way=way: act(ii, way))

    def own(kind, layer, on, which, receive):
        ways = {"OM": (0, 1, 2, 3), "OT": (2, 3), "OU": (0, 1)}[kind]

        @pl.when(side == on)
        def _():
            if receive is relay:
                if on != layer and kind != "OU":
                    w_copy(layer, which, 0, chip).wait_recv()
                for way in ways:
                    w_start(layer, which, way, chip)
            else:
                drain(layer, which, chip, ways)

    def far(t, act):
        sides(t, lambda oo, there, way: pl.when(there)(lambda: act(oo, way)))

    def move(kind, layer, t, which, receive):
        if kind[0] == "O":
            own(kind, layer, t, tail if which is None else which, receive)
        elif kind == "F":
            around(None, lambda ii, way: receive(layer, tail, o * inner + ii, (way, 0, 1)))
        elif kind == "ZM":
            far(t + 1, lambda oo, way: receive(layer, which, oo * inner + i, (way, 2, 3)))
        elif kind == "ZT":
            def both(oo, there, way):
                pl.when(there)(lambda: receive(layer, tail, oo * inner + i, (way,)))
                around(there, lambda ii, _: receive(layer, tail, oo * inner + ii, (way,)))
            sides(t + 1, both)
        elif kind == "Y":
            sides(t, lambda oo, there, _: around(
                there, lambda ii, way: receive(layer, which, oo * inner + ii, (way,))))

    row = lax.broadcasted_iota(jnp.int32, (rows, rows), 0)
    col = lax.broadcasted_iota(jnp.int32, (rows, rows), 1)
    scale = math.log2(math.e) / math.sqrt(HD)

    def scaled(src, c, layer):
        cols = pl.ds(pl.multiple_of(c * blk, blk), blk)
        x = src[:, cols].astype(jnp.float32)
        y = (x * gains[layer, :, cols]).astype(jnp.bfloat16)
        for kind in range(2):
            xb[layer, kind, :, pl.ds(pl.multiple_of(c * depth, depth), depth)] = y[:, kind * depth:(kind + 1) * depth]
        square = x * x
        total = square[:, :HD]
        for at in range(1, blk // HD):
            total += square[:, at * HD:(at + 1) * HD]
        ssq[layer] += total

    def project(layer, hh, first, count, fresh):
        cols = pl.ds(pl.multiple_of(first * depth, depth), count * depth)
        a = jnp.concatenate([xb[layer, core, :, cols], xr[layer, :, cols]], axis=0)
        b = w[layer, pl.ds(first, count), hh * depth:(hh + 1) * depth].reshape(count * depth, 2 * HD)
        y = jnp.dot(a, b, preferred_element_type=jnp.float32)
        if fresh:
            acc[layer, hh] = y[:rows]
            give[layer, hh] = y[rows:]
        else:
            acc[layer, hh] += y[:rows]
            give[layer, hh] += y[rows:]

    def finish(layer, hh, ref, at, then=None):
        part_copy(layer, hh).wait_recv()
        r = lax.rsqrt(jnp.sum(ssq[layer], axis=-1, keepdims=True) / width + EPS)
        y = (acc[layer, hh] + take[layer, hh]) * r
        ref[at, 0] = rope(y[:, :HD], cos_ref[...], sin_ref[...]).astype(jnp.bfloat16)
        if then is not None:
            then(0)
        ref[at, 1] = y[:, HD:].astype(jnp.bfloat16)
        if then is not None:
            then(1)

    def attend(q_ref, q_first, kv_ref, head, x_ref, x_first, write, ready=None):
        if ready is not None:
            ready(0)
        k = kv_ref[head, 0]
        allowed = (col <= row)[None]
        batch = group // 4
        probs = []
        for first in range(0, group, batch):
            q = jnp.concatenate(
                [q_ref[:, pl.ds(pl.multiple_of(q_first + (first + h) * HD, HD), HD)] for h in range(batch)], axis=0)
            scores = lax.dot_general(q, k, (((1,), (1,)), ((), ())), preferred_element_type=jnp.float32)
            scores = jnp.where(allowed, scores.reshape(batch, rows, rows), -1e30)
            top = jnp.max(scores, axis=-1, keepdims=True)
            probs.append(jnp.exp2((scores - top) * scale).astype(jnp.bfloat16).reshape(batch * rows, rows))
        if ready is not None:
            ready(1)
        v = jnp.concatenate([kv_ref[head, 1], jnp.ones((rows, HD), jnp.bfloat16)], axis=1)
        for first, p in zip(range(0, group, batch), probs):
            mixed = jnp.dot(p, v, preferred_element_type=jnp.float32)
            mixed = mixed[:, :HD] / mixed[:, HD:]
            for h in range(batch):
                cols = pl.ds(pl.multiple_of(x_first + (first + h) * HD, HD), HD)
                write(cols, (
                    x_ref[:, cols].astype(jnp.float32) + mixed[h * rows:(h + 1) * rows]
                ).astype(jnp.bfloat16))

    def write_x1(cols, value):
        x1[:, cols] = value

    def write_out(cols, value):
        out[0, 0, :, cols] = value

    def queries_in():
        for load in loads:
            load.wait()

        @pl.when(side == 1)
        def _():
            q_local(1).wait()
            rope_queries(q1, 0, width // HD)

        ssq[...] = jnp.zeros_like(ssq)

    def queries_mine():
        @pl.when(side == 0)
        def _():
            q_local(0).wait()
            rope_queries(q0, 0, half // HD)

    def inputs_in():
        hid_local.wait()
        hid_copy(1 - side).wait_recv()
        gain_copy(1 - side).wait_recv()

        def one(c, _):
            scaled(xs, c, 0)
            return 0
        lax.fori_loop(0, chips, one, 0)
        swap0.start()

    def first_layer():
        swap0.wait_recv()
        for hh in range(heads):
            project(0, hh, 0, chips, True)
            part_copy(0, hh).start()

    def queries_arrive(g):
        @pl.when(side == 1)
        def _():
            q_copy(g).wait_recv()
            rope_queries(q0, g * group, group)

    def first_attention(g):
        finish(0, g, kv0, g)
        attend(q0, g * gw, kv0, g, xs, side * half + g * gw, write_x1)

        def one(b, _):
            x1_copy(side, b).start()
            scaled(x1, side * pieces + b, 1)
            swap_copy(side * pieces + b).start()
            return 0
        lax.fori_loop(g * per_group, (g + 1) * per_group, one, 0)

    def mate_in():
        def one(b, _):
            c = (1 - side) * pieces + b
            x1_copy(1 - side, b).wait_recv()
            scaled(x1, c, 1)
            swap_copy(c).start()
            return 0
        lax.fori_loop(0, pieces, one, 0)

    def swapped(of):
        def one(b, _):
            swap_copy(of * pieces + b).wait_recv()
            return 0
        lax.fori_loop(0, pieces, one, 0)

    def second_layer(hh, first, count, fresh, send=True):
        project(1, hh, first, count, fresh)
        if send:
            part_copy(1, hh).start()

    def second_done(hh, then=None):
        finish(1, hh, kv1, side * heads + hh, then)

    def send_done(hh):
        @pl.when(side == 0)
        def _():
            second_done(hh, lambda kind: kv_copy(hh, kind).start())

    def first_side_in():
        @pl.when(side == 0)
        def _():
            mate_in()
            out[0, 0] = x1[...]
            swapped(1)
        swapped(side)

    def second_side_in():
        @pl.when(side == 1)
        def _():
            mate_in()
            swapped(0)

    def early_heads():
        for hh in range(heads - 1):
            pl.when(side == 0)(lambda hh=hh: second_layer(hh, 0, chips, True))
            pl.when(side == 1)(lambda hh=hh: second_layer(hh, side * pieces, pieces, True, send=False))

    def settle_first():
        for layer in range(2):
            @pl.when(side == layer)
            def _(layer=layer):
                for which in range(3):
                    stage_copy(layer, which).wait_send()
        gain_copy(side).wait_send()
        hid_copy(side).wait_send()
        swap0.wait_send()
        for hh in range(heads):
            part_copy(0, hh).wait_send()

    def drain_moves(layers):
        for step in [step for step in moves if step[1] in layers]:
            moves.remove(step)
            move(*step, drain)

    moves = []
    for word in ORDER:
        if word[0] == "*":
            if word == "*Q":
                queries_in()
            elif word == "*q":
                queries_mine()
            elif word == "*X":
                inputs_in()
            elif word == "*P":
                first_layer()
            elif word[1] == "A":
                first_attention(int(word[2]))
            elif word[1] in "ab":
                pl.when(side == "ba".index(word[1]))(lambda g=int(word[2]): first_attention(g))
            elif word == "*L":
                second_layer(heads - 1, jnp.where(o < outer // 2, 0, inner), chips - inner, True, send=False)
            elif word == "*N":
                second_side_in()
            elif word == "*C":
                settle_first()
            elif word == "*D":
                drain_moves((0,))
            elif word[1] == "R":
                queries_arrive(int(word[2]))
            elif word == "*M":
                first_side_in()
            elif word == "*S":
                early_heads()
            elif word == "*T":
                for hh in range(heads - 1):
                    send_done(hh)
        else:
            kind = word.rstrip("0123456789")
            digits = [int(d) for d in word[len(kind):]]
            step = (kind, digits[0], digits[1], digits[2] if len(digits) > 2 else None)
            moves.append(step)
            move(*step, relay)

    @pl.when(side == 1)
    def _():
        for hh in range(heads - 1):
            second_layer(hh, (1 - side) * pieces, pieces, False)
    second_layer(heads - 1, jnp.where(o < outer // 2, (outer - 1) * inner, 0), inner, False)
    send_done(heads - 1)

    @pl.when(side == 1)
    def _():
        for hh in range(heads - 1):
            second_done(hh)

        def one(g, _):
            pl.when(g == heads - 1)(lambda: second_done(heads - 1))
            attend(q1, (heads + g) * gw, kv1, heads + g, x1, (heads + g) * gw, write_out)
            return 0
        lax.fori_loop(0, heads, one, 0)

    drain_moves((0, 1))
    for c in range(chips):
        swap_copy(c).wait_send()
    for hh in range(heads):
        part_copy(1, hh).wait_send()
    for b in range(pieces):
        x1_copy(side, b).wait_send()

    @pl.when(side == 0)
    def _():
        for g in range(heads):
            q_copy(g).wait_send()
        for hh in range(heads):
            for kind in range(2):
                kv_copy(hh, kind).wait_send()

    @pl.when(side == 1)
    def _():
        def one(g, _):
            attend(q1, g * gw, kv1, g, x1, g * gw, write_out, lambda kind: kv_copy(g, kind).wait_recv())
            return 0
        lax.fori_loop(0, heads, one, 0)


def solution(mesh):
    sections, n = mesh.shape["section"], mesh.shape["fsdp"]
    chips = n // 2
    outer = 4 if chips % 4 == 0 else 1
    inner = chips // outer

    def body(hidden_in, queries, key_weight, value_weight, norm_gain):
        rows, width = queries.shape[2:]
        depth, kvw = key_weight.shape[1:]
        cosine, sine = rope_tables(rows)
        hbm = pl.BlockSpec(memory_space=pltpu.HBM)
        vmem = pl.BlockSpec(memory_space=pltpu.VMEM)
        dma = pltpu.SemaphoreType.DMA
        bf16, f32 = jnp.bfloat16, jnp.float32
        if sections == 2 and outer == 4 and depth % HD == 0:
            heads = kvw // HD // 2
            pieces = chips // 2
            run = functools.partial(pair_kernel, n, outer, inner)
            scratch = [
                pltpu.VMEM((2, chips, heads * depth, 2 * HD), bf16),
                pltpu.VMEM((heads * depth, 2 * HD), bf16),
                pltpu.VMEM((rows, width), bf16),
                pltpu.VMEM((rows, width), bf16),
                pltpu.VMEM((2, 2, rows, width // 2), bf16),
                pltpu.VMEM((2, rows, width // 2), bf16),
                pltpu.VMEM((rows, width // 2), bf16),
                pltpu.VMEM((rows, width), bf16),
                pltpu.VMEM((2, heads, rows, 2 * HD), f32),
                pltpu.VMEM((2, heads, rows, 2 * HD), f32),
                pltpu.VMEM((2, heads, rows, 2 * HD), f32),
                pltpu.VMEM((heads, 2, rows, HD), bf16),
                pltpu.VMEM((2 * heads, 2, rows, HD), bf16),
                pltpu.VMEM((2, 1, width), f32),
                pltpu.VMEM((2, rows, HD), f32),
                pltpu.VMEM((rows, HD), f32),
                pltpu.VMEM((rows, HD), f32),
                dma((2, 3, chips)), dma((2, 3, 4, chips)), dma((3,)), dma((4 * heads,)),
                dma((4,)), dma((2,)), dma((2,)), dma,
                dma((2, heads)), dma((2, pieces)), dma((2, heads, 2)), dma((2,)), dma((2, chips)), dma((2, 2, heads)),
            ]
        else:
            run = functools.partial(chain_kernel, n, sections, outer, inner)
            scratch = [
                pltpu.VMEM((n, 2, depth, kvw), bf16),
                pltpu.VMEM((rows, width), bf16),
                pltpu.VMEM((rows, width), bf16),
                pltpu.VMEM((rows, width), bf16),
                pltpu.VMEM((rows, width), bf16),
                pltpu.VMEM((n // 2, rows, 2 * depth), bf16),
                pltpu.VMEM((2, rows, kvw), f32),
                pltpu.VMEM((kvw // HD, 2, rows, HD), bf16),
                pltpu.VMEM((kvw // HD, 2, rows, HD), bf16),
                pltpu.VMEM((1, width), f32),
                pltpu.VMEM((rows, HD), f32),
                pltpu.VMEM((rows, HD), f32),
                dma((3, n)), dma((3, 5, n)), dma((2,)), dma((sections,)), dma((2,)), dma,
                dma((2,)), dma((2, kvw // HD)), dma((2,)), dma((4,)),
            ]
        return pl.pallas_call(
            run,
            out_shape=jax.ShapeDtypeStruct(queries.shape, bf16),
            in_specs=[hbm] * 7,
            out_specs=vmem,
            scratch_shapes=scratch,
            compiler_params=pltpu.CompilerParams(
                collective_id=0, has_side_effects=True, vmem_limit_bytes=28 * 2**20
            ),
        )(*(
            pltpu.with_memory_space_constraint(x, pltpu.HBM)
            for x in (hidden_in, queries, key_weight, value_weight, norm_gain, jnp.asarray(cosine), jnp.asarray(sine))
        ))

    placed = (
        P("fsdp", "section", None),
        P("section", "fsdp", None, None),
        P("section", "fsdp", None),
        P("section", "fsdp", None),
        P("section", None),
    )
    return jax.shard_map(
        body, mesh=mesh, in_specs=placed, out_specs=P("section", "fsdp", None, None), check_vma=False
    )
```
